32 devices in a mesh: gx: 4 (over z), gy: 2 (over y), gz: 4 (over x, core).
Axes of the slice: x: 2, y: 2, z: 4, core: 2. Of those that a mesh axis runs over, the one named last changes fastest.
Arguments:
- pop_ratio: float32 [19, 8, 32, 512], P(None, 'gx', 'gy', 'gz'), may hold values from 0.7 to 1.3
- solid_flags: int32 [8, 32, 512], P('gx', 'gy', 'gz'), may hold values 0 or 1
- class_ids: int32 [8, 32, 512], P('gx', 'gy', 'gz'), may hold values from 0 to 7
- drag_table: float32 [8], replicated, may hold values from 0.05 to 1
- row_map: int32 [8, 32, 512], P('gx', 'gy', 'gz'), may hold values from 0 to 4095, as said below
- old_basis: float32 [32, 16384], P(None, ('gx', 'gy', 'gz')), may hold values from -6 to 6
- old_sigma: float32 [32], replicated, may hold values from 1 to 10
Outputs:
- final_populations: float32 [19, 8, 32, 512], P(None, 'gx', 'gy', 'gz')
- new_basis: float32 [44, 16384], P(None, ('gx', 'gy', 'gz'))
- triangle: float32 [44, 44], replicated
The draws below stay inside these ranges and needn't reach their ends.
Inputs may be any that keep to these rules, and one draw needn't show every extreme that they name: `row_map`: within each slab along the first dimension every snapshot row is named by exactly 8 voxels, and the voxels of one device name rows of each block of 512 rows exactly 512 times.
All inputs are finite; a program needn't handle non-finite values. No bound on the sum of `solid_flags` on one device may be relied on, other than what follows from the above.
Results may differ from the reference program's by a relative error of at most 0.0003.
Values sent between devices are 32-bit elements; how exact they have to be, the bound alone decides.
No kernel may reach another device: no remote copies, remote signals or barrier semaphores. Data moves between devices by JAX's collectives and lax.ppermute only.
A program may use at most 64 MiB of HBM per device.

```python
import math
import jax
import jax.numpy as jnp
import numpy as np

CX = 2
CY = 16
CZ = 128
STEPS = 4
MODES = 32
CLASSES = 8
VOX_ROW = 8
CELLS = 4096
ROWS_DEV = 512
SLAB_DEV = 8
SEND = 512
ROWS_SLAB = 4096
ROWS = 16384
NX = 8
NY = 32
NZ = 512


def draw_row_map(key, part):
    slabs = NX // CX
    across = NY // CY
    deep = NZ // CZ
    count = slabs * SLAB_DEV
    source_keys = jax.random.split(jax.random.fold_in(key, 11), count)
    owner_keys = jax.random.split(jax.random.fold_in(key, 12), count)
    source_perm = jax.vmap(lambda k: jax.random.permutation(k, CELLS))(source_keys).reshape(slabs, SLAB_DEV, CELLS)
    owner_perm = jax.vmap(lambda k: jax.random.permutation(k, CELLS))(owner_keys).reshape(slabs, SLAB_DEV * CELLS)
    owner = source_perm // SEND
    ranks = source_perm % SEND
    source = jnp.arange(SLAB_DEV, dtype=jnp.int32)[None, :, None]
    flat_slot = owner * CELLS + source * SEND + ranks
    picked = jnp.take_along_axis(owner_perm, flat_slot.reshape(slabs, -1), axis=1).reshape(slabs, SLAB_DEV, CELLS)
    rows = owner * ROWS_DEV + picked // VOX_ROW
    grid = rows.reshape(slabs, across, deep, CX, CY, CZ).transpose(0, 3, 1, 4, 2, 5).reshape(NX, NY, NZ)
    return grid.astype(jnp.int32)


def plant(values, key, low, high):
    index_at = [jax.random.randint(jax.random.fold_in(key, axis), (), 0, length) for axis, length in enumerate(values.shape)]
    widest = values.shape.index(max(values.shape))
    next_to = index_at[:widest] + [(index_at[widest] + 1) % values.shape[widest]] + index_at[widest + 1:]
    return values.at[tuple(index_at)].set(low).at[tuple(next_to)].set(high)


def shard_levels(stream_key, extent, cuts, least, top_value):
    level = 1.0
    for axis_at, shards_of in cuts:
        steps = jax.random.uniform(jax.random.fold_in(jax.random.fold_in(stream_key, 6), axis_at), (shards_of,), jnp.float32, least / len(cuts), top_value / len(cuts))
        level = level * jnp.repeat(jnp.exp(steps), extent[axis_at] // shards_of).reshape((-1,) + (1,) * (len(extent) - 1 - axis_at))
    return level


def normal_values(stream_key, dims, spread, reach, cuts=(), kind=jnp.bfloat16):
    values = jax.random.normal(stream_key, dims, jnp.float32) * spread
    if len(cuts) > 0:
        values = shard_levels(stream_key, dims, cuts, -0.22, 0.18) * values
    return jnp.clip(values, min=-reach, max=reach).astype(kind)


def setup_inputs(seed: int = 0) -> dict:
    key_list = jax.random.split(jax.random.key(seed), 8)
    return {
        "pop_ratio": jnp.clip(0.7 + 0.59999996 * jax.random.uniform(key_list[0], (19, NX, NY, NZ), jnp.float32) ** shard_levels(key_list[0], (19, NX, NY, NZ), ((1, 4), (2, 2), (3, 4)), -0.2, 0.2), 0.7, 1.3),
        "solid_flags": plant((jax.random.randint(key_list[1], (NX, NY, NZ), 0, 5) < 1).astype(jnp.int32), jax.random.fold_in(key_list[1], 1), 0, 1),
        "class_ids": plant(jax.random.randint(key_list[2], (NX, NY, NZ), 0, CLASSES), jax.random.fold_in(key_list[2], 1), 0, CLASSES - 1).astype(jnp.int32),
        "drag_table": jnp.clip(jnp.exp(jax.random.uniform(key_list[3], (CLASSES,), jnp.float32, math.log(0.05), math.log(1.0))), 0.05, 1.0),
        "row_map": draw_row_map(jax.random.fold_in(key_list[7], 71), 0),
        "old_basis": normal_values(key_list[5], (MODES, ROWS), 1.0, 6.0, ((1, 32),), jnp.float32),
        "old_sigma": jnp.clip(jnp.exp(jax.random.uniform(key_list[6], (MODES,), jnp.float32, math.log(1.0), math.log(10.0))), 1.0, 10.0),
    }


LATTICE = np.array([[0, 0, 0], [1, 0, 0], [-1, 0, 0], [0, 1, 0], [0, -1, 0], [0, 0, 1], [0, 0, -1], [1, 1, 0], [-1, -1, 0], [1, -1, 0], [-1, 1, 0], [1, 0, 1], [-1, 0, -1], [1, 0, -1], [-1, 0, 1], [0, 1, 1], [0, -1, -1], [0, 1, -1], [0, -1, 1]])
OPPOSITE = [0, 2, 1, 4, 3, 6, 5, 8, 7, 10, 9, 12, 11, 14, 13, 16, 15, 18, 17]
WEIGHTS = [1.0 / 3.0] + [1.0 / 18.0] * 6 + [1.0 / 36.0] * 12
relax_time = 0.9
vel_scale = 16.0

def collide(populations, solid_flags, drag_rate):
    density = populations[0]
    for q in range(1, 19):
        density = density + populations[q]
    scale = 1.0 / (density * (1.0 + 0.5 * drag_rate))
    speeds = []
    for a in range(3):
        total = jnp.zeros_like(density)
        for q in range(19):
            if LATTICE[q, a] != 0:
                total = total + float(LATTICE[q, a]) * populations[q]
        speeds.append(total * scale)
    square = speeds[0] * speeds[0] + speeds[1] * speeds[1] + speeds[2] * speeds[2]
    relaxed = []
    for q in range(19):
        along = jnp.zeros_like(density)
        for a in range(3):
            if LATTICE[q, a] != 0:
                along = along + float(LATTICE[q, a]) * speeds[a]
        equilib = WEIGHTS[q] * density * (1.0 + 3.0 * along + 4.5 * along * along - 1.5 * square)
        relaxed.append(populations[q] - (populations[q] - equilib) / relax_time)
    relaxed = jnp.stack(relaxed)
    bounced = jnp.stack([populations[OPPOSITE[q]] for q in range(19)])
    result = jnp.where(solid_flags[None] == 1, bounced, relaxed)
    fluid_part = (1 - solid_flags).astype(jnp.float32)
    velocity = jnp.stack(speeds) * fluid_part[None]
    return (result, velocity)

def reference(pop_ratio, solid_flags, class_ids, drag_table, row_map, old_basis, old_sigma):
    weights = jnp.asarray(WEIGHTS, jnp.float32)
    populations = pop_ratio * weights[:, None, None, None]
    drag_rate = drag_table[class_ids]
    snaps = []
    for step in range(STEPS):
        relaxed, velocity = collide(populations, solid_flags, drag_rate)
        snaps.append(velocity.reshape(3, -1))
        populations = jnp.stack([jnp.roll(relaxed[q], (int(LATTICE[q, 0]), int(LATTICE[q, 1]), int(LATTICE[q, 2])), axis=(0, 1, 2)) for q in range(19)])
    values = jnp.concatenate(snaps, 0) * (vel_scale / VOX_ROW)
    slab_start = jnp.arange(NX, dtype=jnp.int32) // CX * ROWS_SLAB
    global_rows = (row_map + slab_start[:, None, None]).reshape(-1).astype(jnp.int32)
    snapshot = jax.vmap(lambda v: jax.ops.segment_sum(v, global_rows, num_segments=ROWS))(values)
    augmented = jnp.concatenate([old_sigma[:, None] * old_basis, snapshot], 0)
    orthogonal, upper = jnp.linalg.qr(augmented.T / math.sqrt(ROWS))
    signs = jnp.sign(jnp.diagonal(upper))
    triangle = upper * signs[:, None]
    new_basis = (orthogonal * signs[None, :]).T * math.sqrt(ROWS)
    return (populations, new_basis, triangle)
```

```python
import functools

import jax
import jax.numpy as jnp
import numpy as np
from jax import lax
from jax.experimental import pallas as pl
from jax.experimental.pallas import tpu as pltpu
from jax.sharding import PartitionSpec as P

STEPS = 4
VOX_ROW = 8
LATTICE = np.array(
    [
        [0, 0, 0],
        [1, 0, 0],
        [-1, 0, 0],
        [0, 1, 0],
        [0, -1, 0],
        [0, 0, 1],
        [0, 0, -1],
        [1, 1, 0],
        [-1, -1, 0],
        [1, -1, 0],
        [-1, 1, 0],
        [1, 0, 1],
        [-1, 0, -1],
        [1, 0, -1],
        [-1, 0, 1],
        [0, 1, 1],
        [0, -1, -1],
        [0, 1, -1],
        [0, -1, 1],
    ]
)
OPPOSITE = [0, 2, 1, 4, 3, 6, 5, 8, 7, 10, 9, 12, 11, 14, 13, 16, 15, 18, 17]
WEIGHTS = [1.0 / 3.0] + [1.0 / 18.0] * 6 + [1.0 / 36.0] * 12
PAIRS = [(q, OPPOSITE[q]) for q in range(1, 19) if q < OPPOSITE[q]]
PLUS_X = [q for q in range(19) if LATTICE[q, 0] == 1]
MINUS_X = [q for q in range(19) if LATTICE[q, 0] == -1]
relax_time = 0.9
vel_scale = 16.0

HALO = 4
FIELDS = 20
LOW = 256


def lanes(shape=(8, 128)):
    return lax.broadcasted_iota(jnp.int32, shape, len(shape) - 1)


def subs(shape=(8, 128)):
    return lax.broadcasted_iota(jnp.int32, shape, len(shape) - 2)


def roll(value, shift, axis):
    size = value.shape[axis]
    shift = shift % size
    return value if shift == 0 else pltpu.roll(value, shift, axis)


def init_kernel(table, ratio, solid, cls, g_ref, zr_ref, zl_ref, yu_ref, yd_ref):
    lane, sub = lanes(), subs()
    zr = [jnp.zeros((8, 128), jnp.float32) for _ in range(3)]
    zl = [jnp.zeros((8, 128), jnp.float32) for _ in range(3)]
    for f in range(FIELDS):
        tiles = {}
        for x in range(2):
            for yt in range(2):
                rows = pl.ds(8 * yt, 8)
                if f < 19:
                    tile = ratio[f, x, rows, :] * WEIGHTS[f]
                else:
                    ids = cls[x, rows, :]
                    drag = jnp.zeros((8, 128), jnp.float32)
                    for c in range(table.shape[0]):
                        drag = jnp.where(ids == c, table[c], drag)
                    tile = jnp.where(solid[x, rows, :] == 1, -1.0, 1.0 + 0.5 * drag)
                    g_ref[x, rows, :] = tile
                tiles[x, yt] = tile
                at, k = divmod(f * 4 + x * 2 + yt, 32)
                here = (lane >= 4 * k) & (lane < 4 * k + 4)
                zr[at] = jnp.where(here, roll(tile, 4 * k - 124, 1), zr[at])
                zl[at] = jnp.where(here, roll(tile, 4 * k, 1), zl[at])
        yu_ref[f] = jnp.where(sub < 4, roll(tiles[0, 1], 4, 0), tiles[1, 1])
        yd_ref[f] = jnp.where(sub < 4, tiles[0, 0], roll(tiles[1, 0], 4, 0))
    for at in range(3):
        zr_ref[at] = zr[at]
        zl_ref[at] = zl[at]


def corner_kernel(ratio, g_ref, left, right, z_ref, cu_ref, cd_ref):
    lane, sub = lanes(), subs()
    cu = [jnp.zeros((8, 128), jnp.float32) for _ in range(2)]
    cd = [jnp.zeros((8, 128), jnp.float32) for _ in range(2)]
    for f in range(FIELDS):
        tiles = {}
        for x in range(2):
            for yt in range(2):
                rows = pl.ds(8 * yt, 8)
                own = ratio[f, x, rows, :] * WEIGHTS[f] if f < 19 else g_ref[x, rows, :]
                at, k = divmod(f * 4 + x * 2 + yt, 32)
                tile = jnp.where(lane < 4, roll(right[at], -4 * k, 1), own)
                tile = jnp.where(lane >= 124, roll(left[at], 124 - 4 * k, 1), tile)
                z_ref[f, x, rows, :] = tile
                tiles[x, yt] = tile
        up = jnp.where(sub < 4, roll(tiles[0, 1], 4, 0), tiles[1, 1])
        down = jnp.where(sub < 4, tiles[0, 0], roll(tiles[1, 0], 4, 0))
        at, k = divmod(f, 16)
        here = (lane >= 8 * k) & (lane < 8 * k + 8)
        cu[at] = jnp.where(here, roll(up, 4 + 8 * k, 1), cu[at])
        cd[at] = jnp.where(here, roll(down, 4 + 8 * k, 1), cd[at])
    for at in range(2):
        cu_ref[at] = cu[at]
        cd_ref[at] = cd[at]


def collide(pops, g):
    density = pops[0]
    for q in range(1, 19):
        density = density + pops[q]
    scale = 1.0 / (density * jnp.abs(g))
    speeds = []
    for a in range(3):
        total = None
        for q in range(19):
            c = LATTICE[q, a]
            if c == 1:
                total = pops[q] if total is None else total + pops[q]
            elif c == -1:
                total = total - pops[q]
        speeds.append(total * scale)
    square = speeds[0] * speeds[0] + speeds[1] * speeds[1] + speeds[2] * speeds[2]
    solid = g < 0.0
    keep = 1.0 - 1.0 / relax_time
    base = 1.0 - 1.5 * square
    part = {w: density * (w / relax_time) for w in sorted(set(WEIGHTS))}
    relaxed = [None] * 19
    rest = pops[0] * keep + part[WEIGHTS[0]] * base
    relaxed[0] = jnp.where(solid, pops[0], rest)
    for q, o in PAIRS:
        along = None
        for a in range(3):
            c = LATTICE[q, a]
            if c == 1:
                along = speeds[a] if along is None else along + speeds[a]
            elif c == -1:
                along = -speeds[a] if along is None else along - speeds[a]
        even = part[WEIGHTS[q]] * (base + 4.5 * along * along)
        odd = part[WEIGHTS[q]] * (3.0 * along)
        relaxed[q] = jnp.where(solid, pops[o], pops[q] * keep + (even + odd))
        relaxed[o] = jnp.where(solid, pops[q], pops[o] * keep + (even - odd))
    factor = jnp.where(solid, 0.0, vel_scale / VOX_ROW)
    return relaxed, [s * factor for s in speeds]


def collide_all(source, g_of, out, vel_ref):
    for x in range(2):
        for yt in range(3):
            for lt in range(2):
                rows, cols = pl.ds(8 * yt, 8), pl.ds(128 * lt, 128)
                pops = [source[q, x, rows, cols] for q in range(19)]
                relaxed, vel = collide(pops, g_of[x, rows, cols])
                for q in range(19):
                    out[q, x, rows, cols] = relaxed[q]
                if yt < 2 and lt == 0:
                    for a in range(3):
                        vel_ref[a, x, rows, :] = vel[a]


def pack_x(out, xr_ref, xl_ref):
    lane = lanes()
    for ref, directions, x in ((xr_ref, PLUS_X, 1), (xl_ref, MINUS_X, 0)):
        extra = jnp.zeros((8, 128), jnp.float32)
        for i, q in enumerate(directions):
            for yt in range(3):
                j = 3 * i + yt
                ref[j] = out[q, x, pl.ds(8 * yt, 8), pl.ds(0, 128)]
                tile = out[q, x, pl.ds(8 * yt, 8), pl.ds(128, 128)]
                here = (lane >= 8 * j) & (lane < 8 * j + 8)
                extra = jnp.where(here, roll(tile, 4 + 8 * j, 1), extra)
        ref[15] = extra


def first_kernel(ratio, g_in, z_in, yu, yd, cu, cd, out, g_ref, vel_ref, xr_ref, xl_ref, wide):
    lane, sub = lanes(), subs()
    edge = (lane < 4) | (lane >= 124)
    for f in range(FIELDS):
        ref = wide.at[f] if f < 19 else g_ref
        at, k = divmod(f, 16)
        low = (yd[f], roll(cd[at], -(8 * k + 4), 1))
        high = (yu[f], roll(cu[at], -(8 * k + 4), 1))
        for x in range(2):
            for yt in range(2):
                rows = pl.ds(8 * yt, 8)
                own = ratio[f, x, rows, :] * WEIGHTS[f] if f < 19 else g_in[x, rows, :]
                ref[x, rows, pl.ds(0, 128)] = own
                ref[x, rows, pl.ds(128, 128)] = z_in[f, x, rows, :]
            tiles = []
            for lt in range(2):
                if x == 0:
                    tiles.append(jnp.where(sub < 4, low[lt], roll(high[lt], 4, 0)))
                else:
                    tiles.append(jnp.where(sub < 4, roll(low[lt], 4, 0), high[lt]))
            ref[x, pl.ds(16, 8), pl.ds(0, 128)] = tiles[0]
            ref[x, pl.ds(16, 8), pl.ds(128, 128)] = jnp.where(edge, tiles[1], tiles[0])
    collide_all(wide, g_ref, out, vel_ref)
    pack_x(out, xr_ref, xl_ref)


def unpack_x(xr, xl, side):
    for s, ref in enumerate((xr, xl)):
        for i in range(5):
            for yt in range(3):
                j = 3 * i + yt
                side[s, i, pl.ds(8 * yt, 8), pl.ds(0, 128)] = ref[j]
                side[s, i, pl.ds(8 * yt, 8), pl.ds(128, 128)] = roll(ref[15], -(8 * j + 4), 1)


def streamed(prev, side, q, x):
    c = [int(v) for v in LATTICE[q]]
    if c[0] == 1 and x == 0:
        value = side[0, PLUS_X.index(q)]
    elif c[0] == -1 and x == 1:
        value = side[1, MINUS_X.index(q)]
    else:
        value = prev[q, x - c[0]]
    return roll(roll(value, c[1], 0), c[2], 1)


def step_kernel(prev, g_ref, xr, xl, out, vel_ref, xr_ref, xl_ref, wide, side):
    unpack_x(xr, xl, side)
    for q in range(19):
        for x in range(2):
            wide[q, x] = streamed(prev, side, q, x)
    collide_all(wide, g_ref, out, vel_ref)
    pack_x(out, xr_ref, xl_ref)


def last_kernel(prev, xr, xl, out, side):
    unpack_x(xr, xl, side)
    for q in range(19):
        for x in range(2):
            out[q, x] = streamed(prev, side, q, x)[:16, :128]


def restrict_kernel(v0, v1, v2, v3, row_map, out, left, right):
    highs = out.shape[0] // 16
    low_at = lax.broadcasted_iota(jnp.int32, (LOW, 128), 0)
    vels = (v0, v1, v2, v3)
    for x in range(2):
        for y in range(16):
            cols = pl.ds(128 * (16 * x + y), 128)
            rows = row_map[x, pl.ds(y, 1), :]
            high = rows // LOW
            low = rows - high * LOW
            right[:, cols] = jnp.where(low_at == low, 1.0, 0.0).astype(jnp.bfloat16)
            vals = [v[a, x, pl.ds(y, 1), :] for v in vels for a in range(3)]
            vals = jnp.concatenate(vals + [jnp.zeros((4, 128), jnp.float32)], 0)
            big = vals.astype(jnp.bfloat16).astype(jnp.float32)
            rest = vals - big
            for h in range(highs):
                here = high == h
                left[pl.ds(16 * h, 16), cols] = jnp.where(here, big, 0.0).astype(jnp.bfloat16)
                left[pl.ds(16 * (highs + h), 16), cols] = jnp.where(here, rest, 0.0).astype(jnp.bfloat16)
    both = lax.dot_general(
        left[...], right[...], (((1,), (1,)), ((), ())), preferred_element_type=jnp.float32
    )
    half = 16 * highs
    out[...] = both[:half] + both[half:]


def gram_kernel(total_rows, parts, basis, sigma, aug_ref, out, gram):
    owners = parts.shape[0] // 32
    total = parts[pl.ds(0, 32), :]
    for o in range(1, owners):
        total = total + parts[pl.ds(32 * o, 32), :]
    aug_ref[pl.ds(0, 32), :] = basis[...] * sigma[...]
    aug_ref[pl.ds(32, 16), pl.ds(0, LOW)] = total[:16]
    aug_ref[pl.ds(32, 16), pl.ds(LOW, LOW)] = total[16:]
    aug = aug_ref[...]
    product = lax.dot_general(
        aug,
        aug,
        (((1,), (1,)), ((), ())),
        precision=lax.Precision.HIGHEST,
        preferred_element_type=jnp.float32,
    ) * (1.0 / total_rows)
    gram[...] = jnp.zeros((48, 128), jnp.float32)
    gram[:, pl.ds(0, 48)] = product
    lane = lanes()
    first = gram[pl.ds(0, 8), :]
    for k in range(1, 4):
        here = (lane >= 32 * k) & (lane < 32 * k + 32)
        first = jnp.where(here, roll(gram[pl.ds(8 * k, 8), :], 32 * k, 1), first)
    second = jnp.where(lane < 64, gram[pl.ds(32, 8), :], roll(gram[pl.ds(40, 8), :], 64, 1))
    for d in range(out.shape[0]):
        out[d, pl.ds(0, 8), :] = first
        out[d, pl.ds(8, 8), :] = second


def factor_kernel(parts, aug_ref, basis_ref, tri_ref, work):
    lane = lanes()
    total = parts[0]
    for d in range(1, parts.shape[0]):
        total = total + parts[d]
    first, second = total[:8], total[8:]
    low = jnp.concatenate([jnp.where(lane < 64, second, 0.0), jnp.where(lane < 64, roll(second, -64, 1), 0.0)], 0)
    turned = low.T
    for k in range(4):
        own = jnp.where(lane < 32, roll(first, -32 * k, 1), 0.0)
        work[pl.ds(8 * k, 8), :] = own
        work[pl.ds(8 * k, 8), pl.ds(32, 16)] = turned[8 * k : 8 * k + 8]
    work[pl.ds(32, 16), :] = low
    tiles = []
    for t in range(6):
        row = lax.broadcasted_iota(jnp.int32, (8, 128), 0) + 8 * t
        tiles.append(work[pl.ds(8 * t, 8), :] + jnp.where(lane == row + 64, 1.0, 0.0))
    done = list(tiles)
    sub = subs()
    for k in range(44):
        t, r = divmod(k, 8)
        pivot_row = jnp.broadcast_to(tiles[t][r : r + 1, :], (8, 128))
        pivot = jnp.broadcast_to(pivot_row[:, k : k + 1], (8, 128))
        inv = 1.0 / jnp.sqrt(pivot)
        scaled = pivot_row * inv
        for u in range(t, 6):
            column = jnp.broadcast_to(tiles[u][:, k : k + 1], (8, 128))
            update = tiles[u] - (column * inv) * scaled
            if u == t:
                done[t] = jnp.where(sub == r, scaled, done[t])
                tiles[t] = jnp.where(sub > r, update, tiles[t])
            else:
                tiles[u] = update
    for t in range(6):
        row = sub + 8 * t
        work[pl.ds(8 * t, 8), :] = jnp.where(lane >= 64, done[t], jnp.where(lane >= row, done[t], 0.0))
        if t == 5:
            work[pl.ds(40, 8), :] = jnp.where(sub < 4, work[pl.ds(40, 8), :], 0.0)
    both = work[...]
    tri_ref[...] = both[:44, :44]
    inverse = both[:, 64:112]
    basis_ref[...] = lax.dot_general(
        inverse,
        aug_ref[...],
        (((1,), (0,)), ((), ())),
        precision=lax.Precision.HIGHEST,
        preferred_element_type=jnp.float32,
    )[:44]


def f32(*shape):
    return jax.ShapeDtypeStruct(shape, jnp.float32)


def call(kernel, outs, scratch=(), smem=(), count=None):
    specs = [
        pl.BlockSpec(memory_space=pltpu.SMEM) if i in smem else pl.BlockSpec(memory_space=pltpu.VMEM)
        for i in range(count)
    ]
    many = isinstance(outs, (tuple, list))
    out_specs = [pl.BlockSpec(memory_space=pltpu.VMEM)] * len(outs) if many else pl.BlockSpec(memory_space=pltpu.VMEM)
    name = kernel.func.__name__ if isinstance(kernel, functools.partial) else kernel.__name__
    return pl.pallas_call(
        kernel, out_shape=outs, in_specs=specs, out_specs=out_specs, scratch_shapes=list(scratch), name=name
    )


def shift(value, axis, step):
    count = lax.axis_size(axis)
    return lax.ppermute(value, axis, [(i, (i + step) % count) for i in range(count)])


def on_device(pop_ratio, solid_flags, class_ids, drag_table, row_map, old_basis, old_sigma):
    slab = ("gy", "gz")
    everyone = ("gx", "gy", "gz")
    owners = lax.axis_size(slab)
    devices = lax.axis_size(everyone)
    rows_local = old_basis.shape[1]
    highs = owners * rows_local // LOW

    g, zr, zl, yu, yd = call(
        init_kernel,
        (f32(2, 16, 128), f32(3, 8, 128), f32(3, 8, 128), f32(FIELDS, 8, 128), f32(FIELDS, 8, 128)),
        smem=(0,),
        count=4,
    )(drag_table, pop_ratio, solid_flags, class_ids)
    left, right = shift(zr, "gz", 1), shift(zl, "gz", -1)
    yu, yd = shift(yu, "gy", 1), shift(yd, "gy", -1)
    z_tiles, cu, cd = call(
        corner_kernel, (f32(FIELDS, 2, 16, 128), f32(2, 8, 128), f32(2, 8, 128)), count=4
    )(pop_ratio, g, left, right)
    cu, cd = shift(cu, "gy", 1), shift(cd, "gy", -1)

    step_outs = (f32(19, 2, 24, 256), f32(3, 2, 16, 128), f32(16, 8, 128), f32(16, 8, 128))
    wide = pltpu.VMEM((19, 2, 24, 256), jnp.float32)
    side = pltpu.VMEM((2, 5, 24, 256), jnp.float32)
    relaxed, g_wide, vel, xr, xl = call(
        first_kernel, (step_outs[0], f32(2, 24, 256)) + step_outs[1:], (wide,), count=7
    )(pop_ratio, g, z_tiles, yu, yd, cu, cd)
    vels = [vel]
    for _ in range(STEPS - 1):
        xr, xl = shift(xr, "gx", 1), shift(xl, "gx", -1)
        relaxed, vel, xr, xl = call(step_kernel, step_outs, (wide, side), count=4)(relaxed, g_wide, xr, xl)
        vels.append(vel)
    xr, xl = shift(xr, "gx", 1), shift(xl, "gx", -1)

    cells = 4096
    term = call(
        restrict_kernel,
        f32(16 * highs, LOW),
        (pltpu.VMEM((32 * highs, cells), jnp.bfloat16), pltpu.VMEM((LOW, cells), jnp.bfloat16)),
        count=5,
    )(*vels, row_map)
    parts = lax.all_to_all(term, slab, 0, 0, tiled=True)
    aug, gram = call(
        functools.partial(gram_kernel, float(rows_local * devices)),
        (f32(48, rows_local), f32(devices, 16, 128)),
        (pltpu.VMEM((48, 128), jnp.float32),),
        count=3,
    )(parts, old_basis, old_sigma[:, None])
    grams = lax.all_to_all(gram, everyone, 0, 0, tiled=True)
    new_basis, upper = call(
        factor_kernel, (f32(44, rows_local), f32(44, 44)), (pltpu.VMEM((48, 128), jnp.float32),), count=2
    )(grams, aug)
    populations = call(last_kernel, f32(19, 2, 16, 128), (side,), count=3)(relaxed, xr, xl)
    return (populations, new_basis, upper)


def solution(mesh):
    in_specs = (
        P(None, "gx", "gy", "gz"),
        P("gx", "gy", "gz"),
        P("gx", "gy", "gz"),
        P(),
        P("gx", "gy", "gz"),
        P(None, ("gx", "gy", "gz")),
        P(),
    )
    out_specs = (P(None, "gx", "gy", "gz"), P(None, ("gx", "gy", "gz")), P())
    return jax.shard_map(
        on_device, mesh=mesh, in_specs=in_specs, out_specs=out_specs, check_vma=False
    )
```

```python
import functools

import jax
import jax.numpy as jnp
import numpy as np
from jax import lax
from jax.experimental import pallas as pl
from jax.experimental.pallas import tpu as pltpu
from jax.sharding import PartitionSpec as P


STEPS = 4
VOX_ROW = 8
LATTICE = np.array(
    [
        [0, 0, 0],
        [1, 0, 0],
        [-1, 0, 0],
        [0, 1, 0],
        [0, -1, 0],
        [0, 0, 1],
        [0, 0, -1],
        [1, 1, 0],
        [-1, -1, 0],
        [1, -1, 0],
        [-1, 1, 0],
        [1, 0, 1],
        [-1, 0, -1],
        [1, 0, -1],
        [-1, 0, 1],
        [0, 1, 1],
        [0, -1, -1],
        [0, 1, -1],
        [0, -1, 1],
    ]
)
OPPOSITE = [0, 2, 1, 4, 3, 6, 5, 8, 7, 10, 9, 12, 11, 14, 13, 16, 15, 18, 17]
WEIGHTS = [1.0 / 3.0] + [1.0 / 18.0] * 6 + [1.0 / 36.0] * 12
PAIRS = [(q, OPPOSITE[q]) for q in range(1, 19) if q < OPPOSITE[q]]
PLUS_X = [q for q in range(19) if LATTICE[q, 0] == 1]
MINUS_X = [q for q in range(19) if LATTICE[q, 0] == -1]
relax_time = 0.9
vel_scale = 16.0

FIELDS = 20
LOW = 256


def lanes(shape=(8, 128)):
    return lax.broadcasted_iota(jnp.int32, shape, len(shape) - 1)


def subs(shape=(8, 128)):
    return lax.broadcasted_iota(jnp.int32, shape, len(shape) - 2)


def roll(value, shift, axis):
    size = value.shape[axis]
    shift = shift % size
    return value if shift == 0 else pltpu.roll(value, shift, axis)


def init_kernel(table, ratio, solid, cls, g_ref, zr_ref, zl_ref, y_ref, cr_ref, cl_ref):
    lane, sub = lanes(), subs()
    blank = jnp.zeros((8, 128), jnp.float32)
    zr, zl = [blank] * 3, [blank] * 3
    cr, cl = [blank] * 2, [blank] * 2
    for f in range(FIELDS):
        tiles = {}
        for x in range(2):
            for yt in range(2):
                rows = pl.ds(8 * yt, 8)
                if f < 19:
                    tile = ratio[f, x, rows, :] * WEIGHTS[f]
                else:
                    ids = cls[x, rows, :]
                    drag = jnp.zeros((8, 128), jnp.float32)
                    for c in range(table.shape[0]):
                        drag = jnp.where(ids == c, table[c], drag)
                    tile = jnp.where(solid[x, rows, :] == 1, -1.0, 1.0 + 0.5 * drag)
                    g_ref[x, rows, :] = tile
                tiles[x, yt] = tile
                at, k = divmod(f * 4 + x * 2 + yt, 32)
                here = (lane >= 4 * k) & (lane < 4 * k + 4)
                zr[at] = jnp.where(here, roll(tile, 4 * k - 124, 1), zr[at])
                zl[at] = jnp.where(here, roll(tile, 4 * k, 1), zl[at])
        up = jnp.where(sub < 4, roll(tiles[0, 1], 4, 0), tiles[1, 1])
        down = jnp.where(sub < 4, tiles[0, 0], roll(tiles[1, 0], 4, 0))
        y_ref[f] = up
        y_ref[FIELDS + f] = down
        here = (lane >= 4 * f) & (lane < 4 * f + 4)
        for i, tile in enumerate((up, down)):
            cr[i] = jnp.where(here, roll(tile, 4 * f - 124, 1), cr[i])
            cl[i] = jnp.where(here, roll(tile, 4 * f, 1), cl[i])
    for at in range(3):
        zr_ref[at] = zr[at]
        zl_ref[at] = zl[at]
    for at in range(2):
        cr_ref[at] = cr[at]
        cl_ref[at] = cl[at]


def collide(pops, g):
    density = pops[0]
    for q in range(1, 19):
        density = density + pops[q]
    scale = 1.0 / (density * jnp.abs(g))
    speeds = []
    for a in range(3):
        total = None
        for q in range(19):
            c = LATTICE[q, a]
            if c == 1:
                total = pops[q] if total is None else total + pops[q]
            elif c == -1:
                total = total - pops[q]
        speeds.append(total * scale)
    square = speeds[0] * speeds[0] + speeds[1] * speeds[1] + speeds[2] * speeds[2]
    solid = g < 0.0
    keep = 1.0 - 1.0 / relax_time
    base = 1.0 - 1.5 * square
    part = {w: density * (w / relax_time) for w in sorted(set(WEIGHTS))}
    relaxed = [None] * 19
    rest = pops[0] * keep + part[WEIGHTS[0]] * base
    relaxed[0] = jnp.where(solid, pops[0], rest)
    for q, o in PAIRS:
        along = None
        for a in range(3):
            c = LATTICE[q, a]
            if c == 1:
                along = speeds[a] if along is None else along + speeds[a]
            elif c == -1:
                along = -speeds[a] if along is None else along - speeds[a]
        even = part[WEIGHTS[q]] * (base + 4.5 * along * along)
        odd = part[WEIGHTS[q]] * (3.0 * along)
        relaxed[q] = jnp.where(solid, pops[o], pops[q] * keep + (even + odd))
        relaxed[o] = jnp.where(solid, pops[q], pops[o] * keep + (even - odd))
    factor = jnp.where(solid, 0.0, vel_scale / VOX_ROW)
    return relaxed, [s * factor for s in speeds]


def collide_all(source, g_of, out, vel_ref, tiles=range(3)):
    for x in range(2):
        for yt in tiles:
            for lt in range(2):
                rows, cols = pl.ds(8 * yt, 8), pl.ds(128 * lt, 128)
                pops = [source[q, x, rows, cols] for q in range(19)]
                relaxed, vel = collide(pops, g_of[x, rows, cols])
                for q in range(19):
                    out[q, x, rows, cols] = relaxed[q]
                if yt < 2 and lt == 0:
                    for a in range(3):
                        vel_ref[a, x, rows, :] = vel[a]


def pack_x(out, xr_ref, xl_ref):
    lane = lanes()
    for ref, directions, x in ((xr_ref, PLUS_X, 1), (xl_ref, MINUS_X, 0)):
        extra = jnp.zeros((8, 128), jnp.float32)
        for i, q in enumerate(directions):
            for yt in range(3):
                j = 3 * i + yt
                ref[j] = out[q, x, pl.ds(8 * yt, 8), pl.ds(0, 128)]
                tile = out[q, x, pl.ds(8 * yt, 8), pl.ds(128, 128)]
                here = (lane >= 8 * j) & (lane < 8 * j + 8)
                extra = jnp.where(here, roll(tile, 4 + 8 * j, 1), extra)
        ref[15] = extra


def inner_kernel(ratio, g_in, left, right, out, g_ref, vel_ref, wide):
    lane = lanes()
    for f in range(FIELDS):
        ref = wide.at[f] if f < 19 else g_ref
        for x in range(2):
            for yt in range(2):
                rows = pl.ds(8 * yt, 8)
                own = ratio[f, x, rows, :] * WEIGHTS[f] if f < 19 else g_in[x, rows, :]
                at, k = divmod(f * 4 + x * 2 + yt, 32)
                tile = jnp.where(lane < 4, roll(right[at], -4 * k, 1), own)
                tile = jnp.where(lane >= 124, roll(left[at], 124 - 4 * k, 1), tile)
                ref[x, rows, pl.ds(0, 128)] = own
                ref[x, rows, pl.ds(128, 128)] = tile
    collide_all(wide, g_ref, out, vel_ref, range(2))


def outer_kernel(out_in, g_in, y, cr, cl, out, g_ref, xr_ref, xl_ref, wide):
    lane, sub = lanes(), subs()
    for f in range(FIELDS):
        ref = wide.at[f] if f < 19 else g_ref
        pairs = []
        for i in range(2):
            own = y[FIELDS * i + f]
            tile = jnp.where(lane < 4, roll(cl[i], -4 * f, 1), own)
            pairs.append((own, jnp.where(lane >= 124, roll(cr[i], 124 - 4 * f, 1), tile)))
        high, low = pairs
        for lt in range(2):
            cols = pl.ds(128 * lt, 128)
            ref[0, pl.ds(16, 8), cols] = jnp.where(sub < 4, low[lt], roll(high[lt], 4, 0))
            ref[1, pl.ds(16, 8), cols] = jnp.where(sub < 4, roll(low[lt], 4, 0), high[lt])
    collide_all(wide, g_ref, out, None, (2,))
    pack_x(out, xr_ref, xl_ref)


def unpack_x(xr, xl, side):
    for s, ref in enumerate((xr, xl)):
        for i in range(5):
            for yt in range(3):
                j = 3 * i + yt
                side[s, i, pl.ds(8 * yt, 8), pl.ds(0, 128)] = ref[j]
                side[s, i, pl.ds(8 * yt, 8), pl.ds(128, 128)] = roll(ref[15], -(8 * j + 4), 1)


def streamed(prev, side, q, x):
    c = [int(v) for v in LATTICE[q]]
    if c[0] == 1 and x == 0:
        value = side[0, PLUS_X.index(q)]
    elif c[0] == -1 and x == 1:
        value = side[1, MINUS_X.index(q)]
    else:
        value = prev[q, x - c[0]]
    return roll(roll(value, c[1], 0), c[2], 1)


def step_kernel(prev, g_ref, xr, xl, out, vel_ref, xr_ref, xl_ref, wide, side):
    unpack_x(xr, xl, side)
    for q in range(19):
        for x in range(2):
            wide[q, x] = streamed(prev, side, q, x)
    collide_all(wide, g_ref, out, vel_ref)
    pack_x(out, xr_ref, xl_ref)


def last_kernel(prev, xr, xl, out, side):
    unpack_x(xr, xl, side)
    for q in range(19):
        for x in range(2):
            out[q, x] = streamed(prev, side, q, x)[:16, :128]


def split(value):
    big = value.astype(jnp.bfloat16).astype(jnp.float32)
    return big, value - big


def onehot_kernel(row_map, right):
    low_at = lax.broadcasted_iota(jnp.int32, (LOW, 128), 0)
    for x in range(2):
        for y in range(16):
            rows = row_map[x, pl.ds(y, 1), :]
            low = rows - (rows // LOW) * LOW
            cols = pl.ds(128 * (16 * x + y), 128)
            right[:, cols] = jnp.where(low_at == low, 1.0, 0.0).astype(jnp.bfloat16)


def times_onehot(left, right):
    return lax.dot_general(
        left[...], right[...], (((1,), (1,)), ((), ())), preferred_element_type=jnp.float32
    )


def early_kernel(v0, v1, v2, row_map, right, out, left):
    highs = out.shape[0]
    vels = (v0, v1, v2)

    def row(i, carry):
        x, y = i // 16, i % 16
        cols = pl.ds(pl.multiple_of(128 * i, 128), 128)
        high = row_map[x, pl.ds(y, 1), :] // LOW
        vals = [v[a, x, pl.ds(y, 1), :] for v in vels for a in range(3)]
        vals = jnp.concatenate(vals + [jnp.zeros((7, 128), jnp.float32)], 0)
        big, rest = split(vals)
        for h in range(highs):
            here = high == h
            left[pl.ds(16 * h, 16), cols] = jnp.where(here, big, 0.0).astype(jnp.bfloat16)
            left[pl.ds(16 * (highs + h), 16), cols] = jnp.where(here, rest, 0.0).astype(jnp.bfloat16)
        return carry

    lax.fori_loop(0, 32, row, 0)
    both = times_onehot(left, right)
    half = 16 * highs
    for h in range(highs):
        out[h] = both[16 * h : 16 * h + 16] + both[half + 16 * h : half + 16 * h + 16]


def late_kernel(v3, row_map, right, early, out, left):
    highs = out.shape[0]
    high_at = lax.broadcasted_iota(jnp.int32, (highs, 128), 0)
    for x in range(2):
        for y in range(16):
            cols = pl.ds(128 * (16 * x + y), 128)
            here = high_at == row_map[x, pl.ds(y, 1), :] // LOW
            for a in range(3):
                for i, part in enumerate(split(v3[a, x, pl.ds(y, 1), :])):
                    left[pl.ds(highs * (3 * i + a), highs), cols] = jnp.where(here, part, 0.0).astype(jnp.bfloat16)
    both = times_onehot(left, right)
    half = 3 * highs
    both = both[:half] + both[half:]
    out[...] = early[...]
    for a in range(3):
        for h in range(highs):
            out[h, pl.ds(9 + a, 1), :] = both[highs * a + h : highs * a + h + 1]


def gram_kernel(total_rows, parts, basis, sigma, aug_ref, out, gram):
    owners = parts.shape[0] // 32
    total = parts[pl.ds(0, 32), :]
    for o in range(1, owners):
        total = total + parts[pl.ds(32 * o, 32), :]
    aug_ref[pl.ds(0, 32), :] = basis[...] * sigma[...]
    aug_ref[pl.ds(32, 16), pl.ds(0, LOW)] = total[:16]
    aug_ref[pl.ds(32, 16), pl.ds(LOW, LOW)] = total[16:]
    aug = aug_ref[...]
    product = lax.dot_general(
        aug,
        aug,
        (((1,), (1,)), ((), ())),
        precision=lax.Precision.HIGHEST,
        preferred_element_type=jnp.float32,
    ) * (1.0 / total_rows)
    gram[...] = jnp.zeros((48, 128), jnp.float32)
    gram[:, pl.ds(0, 48)] = product
    lane = lanes()
    first = gram[pl.ds(0, 8), :]
    for k in range(1, 4):
        here = (lane >= 32 * k) & (lane < 32 * k + 32)
        first = jnp.where(here, roll(gram[pl.ds(8 * k, 8), :], 32 * k, 1), first)
    second = jnp.where(lane < 64, gram[pl.ds(32, 8), :], roll(gram[pl.ds(40, 8), :], 64, 1))
    for d in range(out.shape[0]):
        out[d, pl.ds(0, 8), :] = first
        out[d, pl.ds(8, 8), :] = second


def factor_kernel(parts, aug_ref, basis_ref, tri_ref, work):
    lane = lanes()
    total = parts[0]
    for d in range(1, parts.shape[0]):
        total = total + parts[d]
    first, second = total[:8], total[8:]
    low = jnp.concatenate([jnp.where(lane < 64, second, 0.0), jnp.where(lane < 64, roll(second, -64, 1), 0.0)], 0)
    turned = low.T
    for k in range(4):
        own = jnp.where(lane < 32, roll(first, -32 * k, 1), 0.0)
        work[pl.ds(8 * k, 8), :] = own
        work[pl.ds(8 * k, 8), pl.ds(32, 16)] = turned[8 * k : 8 * k + 8]
    work[pl.ds(32, 16), :] = low
    tiles = []
    for t in range(6):
        row = lax.broadcasted_iota(jnp.int32, (8, 128), 0) + 8 * t
        tiles.append(work[pl.ds(8 * t, 8), :] + jnp.where(lane == row + 64, 1.0, 0.0))
    done = list(tiles)
    sub = subs()
    for k in range(44):
        t, r = divmod(k, 8)
        pivot_row = jnp.broadcast_to(tiles[t][r : r + 1, :], (8, 128))
        pivot = jnp.broadcast_to(pivot_row[:, k : k + 1], (8, 128))
        inv = 1.0 / jnp.sqrt(pivot)
        scaled = pivot_row * inv
        for u in range(t, 6):
            column = jnp.broadcast_to(tiles[u][:, k : k + 1], (8, 128))
            update = tiles[u] - (column * inv) * scaled
            if u == t:
                done[t] = jnp.where(sub == r, scaled, done[t])
                tiles[t] = jnp.where(sub > r, update, tiles[t])
            else:
                tiles[u] = update
    for t in range(6):
        row = sub + 8 * t
        work[pl.ds(8 * t, 8), :] = jnp.where(lane >= 64, done[t], jnp.where(lane >= row, done[t], 0.0))
        if t == 5:
            work[pl.ds(40, 8), :] = jnp.where(sub < 4, work[pl.ds(40, 8), :], 0.0)
    both = work[...]
    tri_ref[...] = both[:44, :44]
    inverse = both[:, 64:112]
    basis_ref[...] = lax.dot_general(
        inverse,
        aug_ref[...],
        (((1,), (0,)), ((), ())),
        precision=lax.Precision.HIGHEST,
        preferred_element_type=jnp.float32,
    )[:44]


def f32(*shape):
    return jax.ShapeDtypeStruct(shape, jnp.float32)


def vmem(*shape):
    return pltpu.VMEM(shape, jnp.float32)


def held(value):
    return pltpu.with_memory_space_constraint(value, pltpu.VMEM)


def call(kernel, outs, scratch=(), smem=(), count=None, aliases=None, limit=16):
    specs = [
        pl.BlockSpec(memory_space=pltpu.SMEM) if i in smem else pl.BlockSpec(memory_space=pltpu.VMEM)
        for i in range(count)
    ]
    many = isinstance(outs, (tuple, list))
    out_specs = [pl.BlockSpec(memory_space=pltpu.VMEM)] * len(outs) if many else pl.BlockSpec(memory_space=pltpu.VMEM)
    return pl.pallas_call(
        kernel, out_shape=outs, in_specs=specs, out_specs=out_specs, scratch_shapes=list(scratch),
        input_output_aliases=aliases or {},
        compiler_params=pltpu.CompilerParams(vmem_limit_bytes=limit * 2**20),
    )


def shift(value, axis, step):
    count = lax.axis_size(axis)
    return lax.ppermute(value, axis, [(i, (i + step) % count) for i in range(count)])


def shift_both(value, step_y, step_z):
    ny, nz = lax.axis_size("gy"), lax.axis_size("gz")
    pairs = [
        (y * nz + z, (y + step_y) % ny * nz + (z + step_z) % nz) for y in range(ny) for z in range(nz)
    ]
    return lax.ppermute(value, ("gy", "gz"), pairs)


def across(value, step_z):
    if lax.axis_size("gy") == 2:
        return shift_both(value, 1, step_z)
    half = value.shape[0] // 2
    return jnp.concatenate([shift_both(value[:half], 1, step_z), shift_both(value[half:], -1, step_z)], 0)


def on_device(pop_ratio, solid_flags, class_ids, drag_table, row_map, old_basis, old_sigma):
    slab = ("gy", "gz")
    everyone = ("gx", "gy", "gz")
    owners = lax.axis_size(slab)
    devices = lax.axis_size(everyone)
    rows_local = old_basis.shape[1]
    highs = owners * rows_local // LOW
    cells = 4096
    tile = (8, 128)

    g, zr, zl, y, cr, cl = call(
        init_kernel,
        (vmem(2, 16, 128), vmem(3, *tile), vmem(3, *tile), vmem(2 * FIELDS, *tile), vmem(2, *tile), vmem(2, *tile)),
        smem=(0,),
        count=4,
    )(drag_table, pop_ratio, solid_flags, class_ids)
    y = across(y, 0)
    left, right = shift(zr, "gz", 1), shift(zl, "gz", -1)
    cr, cl = across(cr, 1), across(cl, -1)

    wide = pltpu.VMEM((19, 2, 24, 256), jnp.float32)
    side = pltpu.VMEM((2, 5, 24, 256), jnp.float32)
    big, wall, vel, face = vmem(19, 2, 24, 256), vmem(2, 24, 256), vmem(3, 2, 16, 128), vmem(16, *tile)
    relaxed, g_wide, v0 = call(inner_kernel, (big, wall, vel), (wide,), count=4)(
        pop_ratio, *map(held, (g, left, right))
    )
    relaxed, g_wide, xr, xl = call(
        outer_kernel, (big, wall, face, face), (wide,), count=5, aliases={0: 0, 1: 1}
    )(*map(held, (relaxed, g_wide, y, cr, cl)))
    vels = [v0]
    step = jax.jit(call(step_kernel, (big, vel, face, face), (wide, side), count=4))
    onehot = call(onehot_kernel, pltpu.VMEM((LOW, cells), jnp.bfloat16), count=1)(row_map)
    for _ in range(1, STEPS):
        xr, xl = shift(xr, "gx", 1), shift(xl, "gx", -1)
        relaxed, vel_s, xr, xl = step(*map(held, (relaxed, g_wide, xr, xl)))
        vels.append(vel_s)
    xr, xl = shift(xr, "gx", 1), shift(xl, "gx", -1)

    early = call(
        early_kernel, vmem(highs, 16, LOW), (pltpu.VMEM((32 * highs, cells), jnp.bfloat16),), count=5,
        limit=8 + highs // 2,
    )(*map(held, vels[:3]), row_map, held(onehot))
    term = call(
        late_kernel, f32(highs, 16, LOW), (pltpu.VMEM((6 * highs, cells), jnp.bfloat16),), count=4,
        limit=8 + highs // 2,
    )(held(vels[3]), row_map, held(onehot), held(early))
    parts = lax.all_to_all(term.reshape(16 * highs, LOW), slab, 0, 0, tiled=True)
    aug, gram = call(
        functools.partial(gram_kernel, float(rows_local * devices)),
        (vmem(48, rows_local), f32(devices, 16, 128)),
        (pltpu.VMEM((48, 128), jnp.float32),),
        count=3,
    )(held(parts), old_basis, old_sigma[:, None])
    grams = lax.all_to_all(gram, everyone, 0, 0, tiled=True)
    new_basis, upper = call(
        factor_kernel, (f32(44, rows_local), f32(44, 44)), (pltpu.VMEM((48, 128), jnp.float32),), count=2
    )(held(grams), held(aug))
    populations = call(last_kernel, f32(19, 2, 16, 128), (side,), count=3)(*map(held, (relaxed, xr, xl)))
    return (populations, new_basis, upper)


def solution(mesh):
    in_specs = (
        P(None, "gx", "gy", "gz"),
        P("gx", "gy", "gz"),
        P("gx", "gy", "gz"),
        P(),
        P("gx", "gy", "gz"),
        P(None, ("gx", "gy", "gz")),
        P(),
    )
    out_specs = (P(None, "gx", "gy", "gz"), P(None, ("gx", "gy", "gz")), P())

    return jax.shard_map(on_device, mesh=mesh, in_specs=in_specs, out_specs=out_specs, check_vma=False)
```

```python
import functools

import jax
import jax.numpy as jnp
import numpy as np
from jax import lax
from jax.experimental import pallas as pl
from jax.experimental.pallas import tpu as pltpu
from jax.sharding import PartitionSpec as P


STEPS = 4
VOX_ROW = 8
LATTICE = np.array(
    [
        [0, 0, 0],
        [1, 0, 0],
        [-1, 0, 0],
        [0, 1, 0],
        [0, -1, 0],
        [0, 0, 1],
        [0, 0, -1],
        [1, 1, 0],
        [-1, -1, 0],
        [1, -1, 0],
        [-1, 1, 0],
        [1, 0, 1],
        [-1, 0, -1],
        [1, 0, -1],
        [-1, 0, 1],
        [0, 1, 1],
        [0, -1, -1],
        [0, 1, -1],
        [0, -1, 1],
    ]
)
OPPOSITE = [0, 2, 1, 4, 3, 6, 5, 8, 7, 10, 9, 12, 11, 14, 13, 16, 15, 18, 17]
WEIGHTS = [1.0 / 3.0] + [1.0 / 18.0] * 6 + [1.0 / 36.0] * 12
PAIRS = [(q, OPPOSITE[q]) for q in range(1, 19) if q < OPPOSITE[q]]
PLUS_X = [q for q in range(19) if LATTICE[q, 0] == 1]
MINUS_X = [q for q in range(19) if LATTICE[q, 0] == -1]
relax_time = 0.9
vel_scale = 16.0

FIELDS = 20
LOW = 256


def lanes(shape=(8, 128)):
    return lax.broadcasted_iota(jnp.int32, shape, len(shape) - 1)


def subs(shape=(8, 128)):
    return lax.broadcasted_iota(jnp.int32, shape, len(shape) - 2)


def roll(value, shift, axis):
    size = value.shape[axis]
    shift = shift % size
    return value if shift == 0 else pltpu.roll(value, shift, axis)


def init_kernel(
    table_hbm, ratio_hbm, solid_hbm, cls_hbm,
    pops_ref, g_ref, zr_ref, zl_ref, y_ref, cr_ref, cl_ref,
    table, ratio, solid, cls, sems,
):
    pairs = ((ratio_hbm, ratio), (table_hbm, table), (solid_hbm, solid), (cls_hbm, cls))
    copies = [pltpu.make_async_copy(src, dst, sems.at[i]) for i, (src, dst) in enumerate(pairs)]
    for copy in copies:
        copy.start()
    for copy in copies:
        copy.wait()
    lane, sub = lanes(), subs()
    blank = jnp.zeros((8, 128), jnp.float32)
    zr, zl = [blank] * 3, [blank] * 3
    cr, cl = [blank] * 2, [blank] * 2
    for f in range(FIELDS):
        tiles = {}
        for x in range(2):
            for yt in range(2):
                rows = pl.ds(8 * yt, 8)
                if f < 19:
                    tile = ratio[f, x, rows, :] * WEIGHTS[f]
                    pops_ref[f, x, rows, :] = tile
                else:
                    ids = cls[x, rows, :]
                    drag = jnp.zeros((8, 128), jnp.float32)
                    for c in range(table.shape[0]):
                        drag = jnp.where(ids == c, table[c], drag)
                    tile = jnp.where(solid[x, rows, :] == 1, -1.0, 1.0 + 0.5 * drag)
                    g_ref[x, rows, :] = tile
                tiles[x, yt] = tile
                at, k = divmod(f * 4 + x * 2 + yt, 32)
                here = (lane >= 4 * k) & (lane < 4 * k + 4)
                zr[at] = jnp.where(here, roll(tile, 4 * k - 124, 1), zr[at])
                zl[at] = jnp.where(here, roll(tile, 4 * k, 1), zl[at])
        up = jnp.where(sub < 4, roll(tiles[0, 1], 4, 0), tiles[1, 1])
        down = jnp.where(sub < 4, tiles[0, 0], roll(tiles[1, 0], 4, 0))
        y_ref[f] = up
        y_ref[FIELDS + f] = down
        here = (lane >= 4 * f) & (lane < 4 * f + 4)
        for i, tile in enumerate((up, down)):
            cr[i] = jnp.where(here, roll(tile, 4 * f - 124, 1), cr[i])
            cl[i] = jnp.where(here, roll(tile, 4 * f, 1), cl[i])
    for at in range(3):
        zr_ref[at] = zr[at]
        zl_ref[at] = zl[at]
    for at in range(2):
        cr_ref[at] = cr[at]
        cl_ref[at] = cl[at]


def collide(pops, g):
    density = pops[0]
    for q in range(1, 19):
        density = density + pops[q]
    scale = 1.0 / (density * jnp.abs(g))
    speeds = []
    for a in range(3):
        total = None
        for q in range(19):
            c = LATTICE[q, a]
            if c == 1:
                total = pops[q] if total is None else total + pops[q]
            elif c == -1:
                total = total - pops[q]
        speeds.append(total * scale)
    square = speeds[0] * speeds[0] + speeds[1] * speeds[1] + speeds[2] * speeds[2]
    solid = g < 0.0
    keep = 1.0 - 1.0 / relax_time
    base = 1.0 - 1.5 * square
    part = {w: density * (w / relax_time) for w in sorted(set(WEIGHTS))}
    relaxed = [None] * 19
    rest = pops[0] * keep + part[WEIGHTS[0]] * base
    relaxed[0] = jnp.where(solid, pops[0], rest)
    for q, o in PAIRS:
        along = None
        for a in range(3):
            c = LATTICE[q, a]
            if c == 1:
                along = speeds[a] if along is None else along + speeds[a]
            elif c == -1:
                along = -speeds[a] if along is None else along - speeds[a]
        even = part[WEIGHTS[q]] * (base + 4.5 * along * along)
        odd = part[WEIGHTS[q]] * (3.0 * along)
        relaxed[q] = jnp.where(solid, pops[o], pops[q] * keep + (even + odd))
        relaxed[o] = jnp.where(solid, pops[q], pops[o] * keep + (even - odd))
    factor = jnp.where(solid, 0.0, vel_scale / VOX_ROW)
    return relaxed, [s * factor for s in speeds]


def collide_all(source, g_of, out, vel_ref, tiles=range(3)):
    for x in range(2):
        for yt in tiles:
            for lt in range(2):
                rows, cols = pl.ds(8 * yt, 8), pl.ds(128 * lt, 128)
                pops = [source[q, x, rows, cols] for q in range(19)]
                relaxed, vel = collide(pops, g_of[x, rows, cols])
                for q in range(19):
                    out[q, x, rows, cols] = relaxed[q]
                if yt < 2 and lt == 0:
                    for a in range(3):
                        vel_ref[a, x, rows, :] = vel[a]


def pack_x(out, xr_ref, xl_ref):
    lane = lanes()
    for ref, directions, x in ((xr_ref, PLUS_X, 1), (xl_ref, MINUS_X, 0)):
        extra = jnp.zeros((8, 128), jnp.float32)
        for i, q in enumerate(directions):
            for yt in range(3):
                j = 3 * i + yt
                ref[j] = out[q, x, pl.ds(8 * yt, 8), pl.ds(0, 128)]
                tile = out[q, x, pl.ds(8 * yt, 8), pl.ds(128, 128)]
                here = (lane >= 8 * j) & (lane < 8 * j + 8)
                extra = jnp.where(here, roll(tile, 4 + 8 * j, 1), extra)
        ref[15] = extra


def inner_kernel(pops, g_in, left, right, out, g_ref, vel_ref, wide):
    lane = lanes()
    for f in range(FIELDS):
        ref = wide.at[f] if f < 19 else g_ref
        for x in range(2):
            for yt in range(2):
                rows = pl.ds(8 * yt, 8)
                own = pops[f, x, rows, :] if f < 19 else g_in[x, rows, :]
                at, k = divmod(f * 4 + x * 2 + yt, 32)
                tile = jnp.where(lane < 4, roll(right[at], -4 * k, 1), own)
                tile = jnp.where(lane >= 124, roll(left[at], 124 - 4 * k, 1), tile)
                ref[x, rows, pl.ds(0, 128)] = own
                ref[x, rows, pl.ds(128, 128)] = tile
    collide_all(wide, g_ref, out, vel_ref, range(2))


def outer_kernel(out_in, g_in, y, cr, cl, out, g_ref, xr_ref, xl_ref, wide):
    lane, sub = lanes(), subs()
    for f in range(FIELDS):
        ref = wide.at[f] if f < 19 else g_ref
        pairs = []
        for i in range(2):
            own = y[FIELDS * i + f]
            tile = jnp.where(lane < 4, roll(cl[i], -4 * f, 1), own)
            pairs.append((own, jnp.where(lane >= 124, roll(cr[i], 124 - 4 * f, 1), tile)))
        high, low = pairs
        for lt in range(2):
            cols = pl.ds(128 * lt, 128)
            ref[0, pl.ds(16, 8), cols] = jnp.where(sub < 4, low[lt], roll(high[lt], 4, 0))
            ref[1, pl.ds(16, 8), cols] = jnp.where(sub < 4, roll(low[lt], 4, 0), high[lt])
    collide_all(wide, g_ref, out, None, (2,))
    pack_x(out, xr_ref, xl_ref)


def unpack_x(xr, xl, side):
    for s, ref in enumerate((xr, xl)):
        for i in range(5):
            for yt in range(3):
                j = 3 * i + yt
                side[s, i, pl.ds(8 * yt, 8), pl.ds(0, 128)] = ref[j]
                side[s, i, pl.ds(8 * yt, 8), pl.ds(128, 128)] = roll(ref[15], -(8 * j + 4), 1)


def streamed(prev, side, q, x):
    c = [int(v) for v in LATTICE[q]]
    if c[0] == 1 and x == 0:
        value = side[0, PLUS_X.index(q)]
    elif c[0] == -1 and x == 1:
        value = side[1, MINUS_X.index(q)]
    else:
        value = prev[q, x - c[0]]
    return roll(roll(value, c[1], 0), c[2], 1)


def step_kernel(prev, g_ref, xr, xl, rider_r, rider_l, out, vel_ref, xr_ref, xl_ref, wide, side):
    unpack_x(xr, xl, side)
    for q in range(19):
        for x in range(2):
            wide[q, x] = streamed(prev, side, q, x)
    collide_all(wide, g_ref, out, vel_ref)
    pack_x(out, xr_ref, xl_ref)
    xr_ref[16] = rider_r[...]
    xl_ref[16] = rider_l[...]


def last_kernel(prev, xr, xl, out, side):
    unpack_x(xr, xl, side)
    for q in range(19):
        for x in range(2):
            out[q, x] = streamed(prev, side, q, x)[:16, :128]


def split(value):
    big = value.astype(jnp.bfloat16).astype(jnp.float32)
    return big, value - big


def onehot_kernel(row_map, right):
    low_at = lax.broadcasted_iota(jnp.int32, (LOW, 128), 0)
    for x in range(2):
        for y in range(16):
            rows = row_map[x, pl.ds(y, 1), :]
            low = rows - (rows // LOW) * LOW
            cols = pl.ds(128 * (16 * x + y), 128)
            right[:, cols] = jnp.where(low_at == low, 1.0, 0.0).astype(jnp.bfloat16)


def times_onehot(left, right):
    return lax.dot_general(
        left[...], right[...], (((1,), (1,)), ((), ())), preferred_element_type=jnp.float32
    )


def early_kernel(v0, v1, v2, row_map, right, out, left):
    highs = out.shape[0]
    vels = (v0, v1, v2)

    def row(i, carry):
        x, y = i // 16, i % 16
        cols = pl.ds(pl.multiple_of(128 * i, 128), 128)
        high = row_map[x, pl.ds(y, 1), :] // LOW
        vals = [v[a, x, pl.ds(y, 1), :] for v in vels for a in range(3)]
        vals = jnp.concatenate(vals + [jnp.zeros((7, 128), jnp.float32)], 0)
        big, rest = split(vals)
        for h in range(highs):
            here = high == h
            left[pl.ds(16 * h, 16), cols] = jnp.where(here, big, 0.0).astype(jnp.bfloat16)
            left[pl.ds(16 * (highs + h), 16), cols] = jnp.where(here, rest, 0.0).astype(jnp.bfloat16)
        return carry

    lax.fori_loop(0, 32, row, 0)
    both = times_onehot(left, right)
    half = 16 * highs
    for h in range(highs):
        out[h] = both[16 * h : 16 * h + 16] + both[half + 16 * h : half + 16 * h + 16]


def old_kernel(total_rows, basis, sigma, scaled_ref, tile_ref, work):
    scaled = basis[...] * sigma[...]
    scaled_ref[...] = scaled
    work[...] = jnp.zeros((32, 128), jnp.float32)
    work[:, pl.ds(0, 32)] = dot(scaled, scaled, 1) * (1.0 / total_rows)
    lane = lanes()
    tile = work[pl.ds(0, 8), :]
    for k in range(1, 4):
        here = (lane >= 32 * k) & (lane < 32 * k + 32)
        tile = jnp.where(here, roll(work[pl.ds(8 * k, 8), :], 32 * k, 1), tile)
    tile_ref[...] = tile


def dot(a, b, dim):
    return lax.dot_general(
        a,
        b,
        (((1,), (dim,)), ((), ())),
        precision=lax.Precision.HIGHEST,
        preferred_element_type=jnp.float32,
    )


def late_kernel(v3, row_map, right, early, own, near_r, near_l, far, out, left):
    highs = out.shape[0]
    high_at = lax.broadcasted_iota(jnp.int32, (highs, 128), 0)
    for x in range(2):
        for y in range(16):
            cols = pl.ds(128 * (16 * x + y), 128)
            here = high_at == row_map[x, pl.ds(y, 1), :] // LOW
            for a in range(3):
                for i, part in enumerate(split(v3[a, x, pl.ds(y, 1), :])):
                    left[pl.ds(highs * (3 * i + a), highs), cols] = jnp.where(here, part, 0.0).astype(jnp.bfloat16)
    both = times_onehot(left, right)
    half = 3 * highs
    both = both[:half] + both[half:]
    out[...] = early[...]
    old = (own[...] + far[...]) + (near_r[...] + near_l[...])
    for h in range(highs):
        for a in range(3):
            out[h, pl.ds(9 + a, 1), :] = both[highs * a + h : highs * a + h + 1]
        if h % 2 == 0:
            out[h, pl.ds(12, 4), pl.ds(0, 128)] = old[:4]
            out[h, pl.ds(12, 4), pl.ds(128, 128)] = old[4:]


def gram_kernel(total_rows, parts, scaled, snap_ref, tile_ref, out, aug):
    owners = parts.shape[0] // 32
    total = parts[pl.ds(0, 32), :]
    for o in range(1, owners):
        total = total + parts[pl.ds(32 * o, 32), :]
    tile_ref[pl.ds(0, 4), :] = total[12:16, :128]
    tile_ref[pl.ds(4, 4), :] = total[12:16, 128:]
    used = lax.broadcasted_iota(jnp.int32, (16, LOW), 0) < 12
    aug[pl.ds(0, 32), :] = scaled[...]
    aug[pl.ds(32, 16), pl.ds(0, LOW)] = jnp.where(used, total[:16], 0.0)
    aug[pl.ds(32, 16), pl.ds(LOW, LOW)] = jnp.where(used, total[16:], 0.0)
    aug[pl.ds(48, 80), :] = jnp.zeros((80, 2 * LOW), jnp.float32)
    snap = aug[pl.ds(32, 16), :]
    snap_ref[...] = snap
    product = dot(snap, aug[...], 1) * (1.0 / total_rows)
    packed = jnp.where(lanes() < 64, product[:8], roll(product[8:], 64, 1))
    for d in range(out.shape[0]):
        out[d] = packed


def eliminate(tiles, count):
    sub = subs()
    done = list(tiles)
    for k in range(count):
        t, r = divmod(k, 8)
        pivot_row = jnp.broadcast_to(tiles[t][r : r + 1, :], (8, 128))
        pivot = jnp.broadcast_to(pivot_row[:, k : k + 1], (8, 128))
        inv = 1.0 / jnp.sqrt(pivot)
        scaled = pivot_row * inv
        for u in range(t, len(tiles)):
            column = jnp.broadcast_to(tiles[u][:, k : k + 1], (8, 128))
            update = tiles[u] - (column * inv) * scaled
            if u == t:
                done[t] = jnp.where(sub == r, scaled, done[t])
                tiles[t] = jnp.where(sub > r, update, tiles[t])
            else:
                tiles[u] = update
    return [jnp.where((lanes() >= 64) | (lanes() >= sub + 8 * t), tile, 0.0) for t, tile in enumerate(done)]


def old_factor_kernel(tile, scaled, work, head_ref):
    lane, sub = lanes(), subs()
    tiles = []
    for k in range(4):
        own = jnp.where(lane < 32, roll(tile[...], -32 * k, 1), 0.0)
        tiles.append(own + jnp.where(lane == sub + 8 * k + 64, 1.0, 0.0))
    for k, value in enumerate(eliminate(tiles, 32)):
        work[pl.ds(8 * k, 8), :] = value
    head_ref[...] = dot(work[:, pl.ds(64, 32)], scaled[...], 0)


def factor_kernel(parts, factor, head, snap, basis_ref, tri_ref, work):
    lane, sub = lanes(), subs()
    total = parts[0]
    for d in range(1, parts.shape[0]):
        total = total + parts[d]
    work[pl.ds(0, 8), :] = jnp.where(lane < 64, total, 0.0)
    work[pl.ds(8, 8), :] = jnp.where(lane < 64, roll(total, -64, 1), 0.0)
    cross = work[:, pl.ds(0, 32)]
    inner = work[:, pl.ds(32, 16)]
    inverse = factor[:, pl.ds(64, 32)]
    below = dot(cross, inverse, 1)
    rest = snap[...] - dot(below, head[...], 0)
    inner = inner - dot(below, below, 1)
    work[...] = jnp.zeros((16, 128), jnp.float32)
    work[:, pl.ds(0, 16)] = inner
    tiles = [work[pl.ds(8 * t, 8), :] + jnp.where(lane == sub + 8 * t + 64, 1.0, 0.0) for t in range(2)]
    for t, value in enumerate(eliminate(tiles, 12)):
        work[pl.ds(8 * t, 8), :] = value
    tri_ref[pl.ds(0, 32), pl.ds(0, 32)] = factor[:, pl.ds(0, 32)]
    tri_ref[pl.ds(0, 32), pl.ds(32, 12)] = dot(inverse, cross, 1)[:, :12]
    tri_ref[pl.ds(32, 12), pl.ds(0, 32)] = jnp.zeros((12, 32), jnp.float32)
    tri_ref[pl.ds(32, 12), pl.ds(32, 12)] = work[pl.ds(0, 12), pl.ds(0, 12)]
    basis_ref[pl.ds(0, 32), :] = head[...]
    basis_ref[pl.ds(32, 12), :] = dot(work[:, pl.ds(64, 16)], rest, 0)[:12]


def f32(*shape):
    return jax.ShapeDtypeStruct(shape, jnp.float32)


def vmem(*shape):
    return pltpu.VMEM(shape, jnp.float32)


def held(value):
    return pltpu.with_memory_space_constraint(value, pltpu.VMEM)


def call(kernel, outs, scratch=(), count=None, aliases=None, limit=16, space=pltpu.VMEM):
    specs = [pl.BlockSpec(memory_space=space) for _ in range(count)]
    many = isinstance(outs, (tuple, list))
    out_specs = [pl.BlockSpec(memory_space=pltpu.VMEM)] * len(outs) if many else pl.BlockSpec(memory_space=pltpu.VMEM)
    return pl.pallas_call(
        kernel, out_shape=outs, in_specs=specs, out_specs=out_specs, scratch_shapes=list(scratch),
        input_output_aliases=aliases or {},
        compiler_params=pltpu.CompilerParams(vmem_limit_bytes=limit * 2**20),
    )


def shift(value, axis, step):
    count = lax.axis_size(axis)
    return lax.ppermute(value, axis, [(i, (i + step) % count) for i in range(count)])


def shift_both(value, step_y, step_z):
    ny, nz = lax.axis_size("gy"), lax.axis_size("gz")
    pairs = [
        (y * nz + z, (y + step_y) % ny * nz + (z + step_z) % nz) for y in range(ny) for z in range(nz)
    ]
    return lax.ppermute(value, ("gy", "gz"), pairs)


def across(value, step_z):
    if lax.axis_size("gy") == 2:
        return shift_both(value, 1, step_z)
    half = value.shape[0] // 2
    return jnp.concatenate([shift_both(value[:half], 1, step_z), shift_both(value[half:], -1, step_z)], 0)


def on_device(pop_ratio, solid_flags, class_ids, drag_table, row_map, old_basis, old_sigma):
    slab = ("gy", "gz")
    everyone = ("gx", "gy", "gz")
    owners = lax.axis_size(slab)
    devices = lax.axis_size(everyone)
    rows_local = old_basis.shape[1]
    highs = owners * rows_local // LOW
    cells = 4096
    tile = (8, 128)

    pops, g, zr, zl, y, cr, cl = call(
        init_kernel,
        (vmem(19, 2, 16, 128), vmem(2, 16, 128), vmem(3, *tile), vmem(3, *tile))
        + (vmem(2 * FIELDS, *tile), vmem(2, *tile), vmem(2, *tile)),
        (
            pltpu.SMEM(drag_table.shape, jnp.float32),
            pltpu.VMEM((19, 2, 16, 128), jnp.float32),
            pltpu.VMEM((2, 16, 128), jnp.int32),
            pltpu.VMEM((2, 16, 128), jnp.int32),
            pltpu.SemaphoreType.DMA((4,)),
        ),
        count=4,
        space=pltpu.HBM,
    )(*(pltpu.with_memory_space_constraint(v, pltpu.HBM) for v in (drag_table, pop_ratio, solid_flags, class_ids)))
    y = across(y, 0)
    left, right = shift(zr, "gz", 1), shift(zl, "gz", -1)
    cr, cl = across(cr, 1), across(cl, -1)

    wide = pltpu.VMEM((19, 2, 24, 256), jnp.float32)
    side = pltpu.VMEM((2, 5, 24, 256), jnp.float32)
    big, wall, vel, face = vmem(19, 2, 24, 256), vmem(2, 24, 256), vmem(3, 2, 16, 128), vmem(16, *tile)
    loaded = vmem(17, *tile)
    relaxed, g_wide, v0 = call(inner_kernel, (big, wall, vel), (wide,), count=4)(
        *map(held, (pops, g, left, right))
    )
    relaxed, g_wide, xr, xl = call(
        outer_kernel, (big, wall, face, face), (wide,), count=5, aliases={0: 0, 1: 1}
    )(*map(held, (relaxed, g_wide, y, cr, cl)))
    vels = [v0]
    old, own = call(
        functools.partial(old_kernel, float(rows_local * devices)),
        (vmem(32, rows_local), vmem(*tile)),
        (pltpu.VMEM((32, 128), jnp.float32),),
        count=2,
    )(old_basis, old_sigma[:, None])
    ring = lax.axis_size("gx") == 4
    if not ring:
        own = lax.psum(own, "gx")
    none = jnp.zeros(tile, jnp.float32)
    step = jax.jit(call(step_kernel, (big, vel, loaded, loaded), (wide, side), count=6))
    onehot = call(onehot_kernel, pltpu.VMEM((LOW, cells), jnp.bfloat16), count=1)(row_map)
    riders, got = (own, own), [none] * 3
    for s in range(1, STEPS):
        xr, xl = shift(xr, "gx", 1), shift(xl, "gx", -1)
        if s == 2 and ring:
            got[0], got[1] = xr[16], xl[16]
            riders = (xr[16], none)
        if s == 3 and ring:
            got[2] = xr[16]
            riders = (none, none)
        relaxed, vel_s, xr, xl = step(*map(held, (relaxed, g_wide, xr, xl, *riders)))
        vels.append(vel_s)
    xr, xl = shift(xr, "gx", 1), shift(xl, "gx", -1)

    early = call(
        early_kernel, vmem(highs, 16, LOW), (pltpu.VMEM((32 * highs, cells), jnp.bfloat16),), count=5,
        limit=8 + highs // 2,
    )(*map(held, vels[:3]), row_map, held(onehot))
    term = call(
        late_kernel, f32(highs, 16, LOW), (pltpu.VMEM((6 * highs, cells), jnp.bfloat16),), count=8,
        limit=8 + highs // 2,
    )(held(vels[3]), row_map, *map(held, (onehot, early, own, *got)))
    parts = lax.all_to_all(term.reshape(16 * highs, LOW), slab, 0, 0, tiled=True)
    snap, old_tile, gram = call(
        functools.partial(gram_kernel, float(rows_local * devices)),
        (vmem(16, rows_local), vmem(*tile), f32(devices, *tile)),
        (pltpu.VMEM((128, rows_local), jnp.float32),),
        count=2,
    )(held(parts), held(old))
    grams = lax.all_to_all(gram, everyone, 0, 0, tiled=True)
    factor, head = call(old_factor_kernel, (vmem(32, 128), vmem(32, rows_local)), count=2)(held(old_tile), held(old))
    new_basis, upper = call(
        factor_kernel, (f32(44, rows_local), f32(44, 44)), (pltpu.VMEM((16, 128), jnp.float32),), count=4
    )(*map(held, (grams, factor, head, snap)))
    populations = call(last_kernel, f32(19, 2, 16, 128), (side,), count=3)(*map(held, (relaxed, xr, xl)))
    return (populations, new_basis, upper)


def solution(mesh):
    in_specs = (
        P(None, "gx", "gy", "gz"),
        P("gx", "gy", "gz"),
        P("gx", "gy", "gz"),
        P(),
        P("gx", "gy", "gz"),
        P(None, ("gx", "gy", "gz")),
        P(),
    )
    out_specs = (P(None, "gx", "gy", "gz"), P(None, ("gx", "gy", "gz")), P())

    return jax.shard_map(on_device, mesh=mesh, in_specs=in_specs, out_specs=out_specs, check_vma=False)
```

```python
import functools

import jax
import jax.numpy as jnp
import numpy as np
from jax import lax
from jax.experimental import pallas as pl
from jax.experimental.pallas import tpu as pltpu
from jax.sharding import PartitionSpec as P


STEPS = 4
VOX_ROW = 8
LATTICE = np.array(
    [
        [0, 0, 0],
        [1, 0, 0],
        [-1, 0, 0],
        [0, 1, 0],
        [0, -1, 0],
        [0, 0, 1],
        [0, 0, -1],
        [1, 1, 0],
        [-1, -1, 0],
        [1, -1, 0],
        [-1, 1, 0],
        [1, 0, 1],
        [-1, 0, -1],
        [1, 0, -1],
        [-1, 0, 1],
        [0, 1, 1],
        [0, -1, -1],
        [0, 1, -1],
        [0, -1, 1],
    ]
)
OPPOSITE = [0, 2, 1, 4, 3, 6, 5, 8, 7, 10, 9, 12, 11, 14, 13, 16, 15, 18, 17]
WEIGHTS = [1.0 / 3.0] + [1.0 / 18.0] * 6 + [1.0 / 36.0] * 12
PAIRS = [(q, OPPOSITE[q]) for q in range(1, 19) if q < OPPOSITE[q]]
PLUS_X = [q for q in range(19) if LATTICE[q, 0] == 1]
MINUS_X = [q for q in range(19) if LATTICE[q, 0] == -1]
relax_time = 0.9
vel_scale = 16.0

FIELDS = 20
LOW = 256


def lanes(shape=(8, 128)):
    return lax.broadcasted_iota(jnp.int32, shape, len(shape) - 1)


def subs(shape=(8, 128)):
    return lax.broadcasted_iota(jnp.int32, shape, len(shape) - 2)


def roll(value, shift, axis):
    size = value.shape[axis]
    shift = shift % size
    return value if shift == 0 else pltpu.roll(value, shift, axis)


def init_kernel(
    table_hbm, ratio_hbm, solid_hbm, cls_hbm,
    pops_ref, g_ref, zr_ref, zl_ref, y_ref, cr_ref, cl_ref,
    table, ratio, solid, cls, sems,
):
    pairs = ((ratio_hbm, ratio), (table_hbm, table), (solid_hbm, solid), (cls_hbm, cls))
    copies = [pltpu.make_async_copy(src, dst, sems.at[i]) for i, (src, dst) in enumerate(pairs)]
    for copy in copies:
        copy.start()
    for copy in copies:
        copy.wait()
    lane, sub = lanes(), subs()
    blank = jnp.zeros((8, 128), jnp.float32)
    zr, zl = [blank] * 3, [blank] * 3
    cr, cl = [blank] * 2, [blank] * 2
    for f in range(FIELDS):
        tiles = {}
        for x in range(2):
            for yt in range(2):
                rows = pl.ds(8 * yt, 8)
                if f < 19:
                    tile = ratio[f, x, rows, :] * WEIGHTS[f]
                    pops_ref[f, x, rows, :] = tile
                else:
                    ids = cls[x, rows, :]
                    drag = jnp.zeros((8, 128), jnp.float32)
                    for c in range(table.shape[0]):
                        drag = jnp.where(ids == c, table[c], drag)
                    tile = jnp.where(solid[x, rows, :] == 1, -1.0, 1.0 + 0.5 * drag)
                    g_ref[x, rows, :] = tile
                tiles[x, yt] = tile
                at, k = divmod(f * 4 + x * 2 + yt, 32)
                here = (lane >= 4 * k) & (lane < 4 * k + 4)
                zr[at] = jnp.where(here, roll(tile, 4 * k - 124, 1), zr[at])
                zl[at] = jnp.where(here, roll(tile, 4 * k, 1), zl[at])
        up = jnp.where(sub < 4, roll(tiles[0, 1], 4, 0), tiles[1, 1])
        down = jnp.where(sub < 4, tiles[0, 0], roll(tiles[1, 0], 4, 0))
        y_ref[f] = up
        y_ref[FIELDS + f] = down
        here = (lane >= 4 * f) & (lane < 4 * f + 4)
        for i, tile in enumerate((up, down)):
            cr[i] = jnp.where(here, roll(tile, 4 * f - 124, 1), cr[i])
            cl[i] = jnp.where(here, roll(tile, 4 * f, 1), cl[i])
    for at in range(3):
        zr_ref[at] = zr[at]
        zl_ref[at] = zl[at]
    for at in range(2):
        cr_ref[at] = cr[at]
        cl_ref[at] = cl[at]


def collide(pops, g):
    density = pops[0]
    for q in range(1, 19):
        density = density + pops[q]
    scale = 1.0 / (density * jnp.abs(g))
    speeds = []
    for a in range(3):
        total = None
        for q in range(19):
            c = LATTICE[q, a]
            if c == 1:
                total = pops[q] if total is None else total + pops[q]
            elif c == -1:
                total = total - pops[q]
        speeds.append(total * scale)
    square = speeds[0] * speeds[0] + speeds[1] * speeds[1] + speeds[2] * speeds[2]
    solid = g < 0.0
    keep = 1.0 - 1.0 / relax_time
    base = 1.0 - 1.5 * square
    part = {w: density * (w / relax_time) for w in sorted(set(WEIGHTS))}
    relaxed = [None] * 19
    rest = pops[0] * keep + part[WEIGHTS[0]] * base
    relaxed[0] = jnp.where(solid, pops[0], rest)
    for q, o in PAIRS:
        along = None
        for a in range(3):
            c = LATTICE[q, a]
            if c == 1:
                along = speeds[a] if along is None else along + speeds[a]
            elif c == -1:
                along = -speeds[a] if along is None else along - speeds[a]
        even = part[WEIGHTS[q]] * (base + 4.5 * along * along)
        odd = part[WEIGHTS[q]] * (3.0 * along)
        relaxed[q] = jnp.where(solid, pops[o], pops[q] * keep + (even + odd))
        relaxed[o] = jnp.where(solid, pops[q], pops[o] * keep + (even - odd))
    factor = jnp.where(solid, 0.0, vel_scale / VOX_ROW)
    return relaxed, [s * factor for s in speeds]


def collide_all(source, g_of, out, vel_ref, tiles=range(3)):
    for x in range(2):
        for yt in tiles:
            for lt in range(2):
                rows, cols = pl.ds(8 * yt, 8), pl.ds(128 * lt, 128)
                pops = [source[q, x, rows, cols] for q in range(19)]
                relaxed, vel = collide(pops, g_of[x, rows, cols])
                for q in range(19):
                    out[q, x, rows, cols] = relaxed[q]
                if yt < 2 and lt == 0:
                    for a in range(3):
                        vel_ref[a, x, rows, :] = vel[a]


def pack_x(out, xr_ref, xl_ref):
    lane = lanes()
    for ref, directions, x in ((xr_ref, PLUS_X, 1), (xl_ref, MINUS_X, 0)):
        extra = jnp.zeros((8, 128), jnp.float32)
        for i, q in enumerate(directions):
            for yt in range(3):
                j = 3 * i + yt
                ref[j] = out[q, x, pl.ds(8 * yt, 8), pl.ds(0, 128)]
                tile = out[q, x, pl.ds(8 * yt, 8), pl.ds(128, 128)]
                here = (lane >= 8 * j) & (lane < 8 * j + 8)
                extra = jnp.where(here, roll(tile, 4 + 8 * j, 1), extra)
        ref[15] = extra


def inner_kernel(pops, g_in, left, right, out, g_ref, vel_ref, wide):
    lane = lanes()
    for f in range(FIELDS):
        ref = wide.at[f] if f < 19 else g_ref
        for x in range(2):
            for yt in range(2):
                rows = pl.ds(8 * yt, 8)
                own = pops[f, x, rows, :] if f < 19 else g_in[x, rows, :]
                at, k = divmod(f * 4 + x * 2 + yt, 32)
                tile = jnp.where(lane < 4, roll(right[at], -4 * k, 1), own)
                tile = jnp.where(lane >= 124, roll(left[at], 124 - 4 * k, 1), tile)
                ref[x, rows, pl.ds(0, 128)] = own
                ref[x, rows, pl.ds(128, 128)] = tile
    collide_all(wide, g_ref, out, vel_ref, range(2))


def outer_kernel(out_in, g_in, y, cr, cl, out, g_ref, xr_ref, xl_ref, wide):
    lane, sub = lanes(), subs()
    for f in range(FIELDS):
        ref = wide.at[f] if f < 19 else g_ref
        pairs = []
        for i in range(2):
            own = y[FIELDS * i + f]
            tile = jnp.where(lane < 4, roll(cl[i], -4 * f, 1), own)
            pairs.append((own, jnp.where(lane >= 124, roll(cr[i], 124 - 4 * f, 1), tile)))
        high, low = pairs
        for lt in range(2):
            cols = pl.ds(128 * lt, 128)
            ref[0, pl.ds(16, 8), cols] = jnp.where(sub < 4, low[lt], roll(high[lt], 4, 0))
            ref[1, pl.ds(16, 8), cols] = jnp.where(sub < 4, roll(low[lt], 4, 0), high[lt])
    collide_all(wide, g_ref, out, None, (2,))
    pack_x(out, xr_ref, xl_ref)


def unpack_x(xr, xl, side):
    for s, ref in enumerate((xr, xl)):
        for i in range(5):
            for yt in range(3):
                j = 3 * i + yt
                side[s, i, pl.ds(8 * yt, 8), pl.ds(0, 128)] = ref[j]
                side[s, i, pl.ds(8 * yt, 8), pl.ds(128, 128)] = roll(ref[15], -(8 * j + 4), 1)


def streamed(prev, side, q, x):
    c = [int(v) for v in LATTICE[q]]
    if c[0] == 1 and x == 0:
        value = side[0, PLUS_X.index(q)]
    elif c[0] == -1 and x == 1:
        value = side[1, MINUS_X.index(q)]
    else:
        value = prev[q, x - c[0]]
    return roll(roll(value, c[1], 0), c[2], 1)


def step_kernel(prev, g_ref, xr, xl, rider_r, rider_l, out, vel_ref, xr_ref, xl_ref, wide, side):
    unpack_x(xr, xl, side)
    for q in range(19):
        for x in range(2):
            wide[q, x] = streamed(prev, side, q, x)
    collide_all(wide, g_ref, out, vel_ref)
    pack_x(out, xr_ref, xl_ref)
    xr_ref[16] = rider_r[...]
    xl_ref[16] = rider_l[...]


def last_kernel(prev, xr, xl, out, side):
    unpack_x(xr, xl, side)
    for q in range(19):
        for x in range(2):
            out[q, x] = streamed(prev, side, q, x)[:16, :128]


def split(value):
    big = value.astype(jnp.bfloat16).astype(jnp.float32)
    return big, value - big


def onehot_kernel(row_map, right):
    low_at = lax.broadcasted_iota(jnp.int32, (LOW, 128), 0)
    for x in range(2):
        for y in range(16):
            rows = row_map[x, pl.ds(y, 1), :]
            low = rows - (rows // LOW) * LOW
            cols = pl.ds(128 * (16 * x + y), 128)
            right[:, cols] = jnp.where(low_at == low, 1.0, 0.0).astype(jnp.bfloat16)


def times_onehot(left, right):
    return lax.dot_general(
        left[...], right[...], (((1,), (1,)), ((), ())), preferred_element_type=jnp.float32
    )


def early_kernel(v0, v1, v2, row_map, right, out, left):
    highs = out.shape[0]
    vels = (v0, v1, v2)

    def row(i, carry):
        x, y = i // 16, i % 16
        cols = pl.ds(pl.multiple_of(128 * i, 128), 128)
        high = row_map[x, pl.ds(y, 1), :] // LOW
        vals = [v[a, x, pl.ds(y, 1), :] for v in vels for a in range(3)]
        vals = jnp.concatenate(vals + [jnp.zeros((7, 128), jnp.float32)], 0)
        big, rest = split(vals)
        for h in range(highs):
            here = high == h
            left[pl.ds(16 * h, 16), cols] = jnp.where(here, big, 0.0).astype(jnp.bfloat16)
            left[pl.ds(16 * (highs + h), 16), cols] = jnp.where(here, rest, 0.0).astype(jnp.bfloat16)
        return carry

    lax.fori_loop(0, 32, row, 0)
    both = times_onehot(left, right)
    half = 16 * highs
    for h in range(highs):
        out[h] = both[16 * h : 16 * h + 16] + both[half + 16 * h : half + 16 * h + 16]


def old_kernel(total_rows, basis, sigma, scaled_ref, tile_ref, work):
    scaled = basis[...] * sigma[...]
    scaled_ref[...] = scaled
    work[...] = jnp.zeros((32, 128), jnp.float32)
    work[:, pl.ds(0, 32)] = dot(scaled, scaled, 1) * (1.0 / total_rows)
    lane = lanes()
    tile = work[pl.ds(0, 8), :]
    for k in range(1, 4):
        here = (lane >= 32 * k) & (lane < 32 * k + 32)
        tile = jnp.where(here, roll(work[pl.ds(8 * k, 8), :], 32 * k, 1), tile)
    tile_ref[...] = tile


def dot(a, b, dim):
    return lax.dot_general(
        a,
        b,
        (((1,), (dim,)), ((), ())),
        precision=lax.Precision.HIGHEST,
        preferred_element_type=jnp.float32,
    )


def late_kernel(v3, row_map, right, early, own, near_r, near_l, far, out, left):
    highs = out.shape[0]
    high_at = lax.broadcasted_iota(jnp.int32, (highs, 128), 0)
    for x in range(2):
        for y in range(16):
            cols = pl.ds(128 * (16 * x + y), 128)
            here = high_at == row_map[x, pl.ds(y, 1), :] // LOW
            for a in range(3):
                for i, part in enumerate(split(v3[a, x, pl.ds(y, 1), :])):
                    left[pl.ds(highs * (3 * i + a), highs), cols] = jnp.where(here, part, 0.0).astype(jnp.bfloat16)
    both = times_onehot(left, right)
    half = 3 * highs
    both = both[:half] + both[half:]
    out[...] = early[...]
    old = (own[...] + far[...]) + (near_r[...] + near_l[...])
    for h in range(highs):
        for a in range(3):
            out[h, pl.ds(9 + a, 1), :] = both[highs * a + h : highs * a + h + 1]
        if h % 2 == 0:
            out[h, pl.ds(12, 4), pl.ds(0, 128)] = old[:4]
            out[h, pl.ds(12, 4), pl.ds(128, 128)] = old[4:]


def gram_kernel(total_rows, parts, scaled, snap_ref, tile_ref, out, aug):
    owners = parts.shape[0] // 32
    total = parts[pl.ds(0, 32), :]
    for o in range(1, owners):
        total = total + parts[pl.ds(32 * o, 32), :]
    tile_ref[pl.ds(0, 4), :] = total[12:16, :128]
    tile_ref[pl.ds(4, 4), :] = total[12:16, 128:]
    used = lax.broadcasted_iota(jnp.int32, (16, LOW), 0) < 12
    aug[pl.ds(0, 32), :] = scaled[...]
    aug[pl.ds(32, 16), pl.ds(0, LOW)] = jnp.where(used, total[:16], 0.0)
    aug[pl.ds(32, 16), pl.ds(LOW, LOW)] = jnp.where(used, total[16:], 0.0)
    aug[pl.ds(48, 80), :] = jnp.zeros((80, 2 * LOW), jnp.float32)
    snap = aug[pl.ds(32, 16), :]
    snap_ref[...] = snap
    product = dot(snap, aug[...], 1) * (1.0 / total_rows)
    lane = lanes()
    tail = jnp.where(lane < 120, roll(product[8:], 88, 1), roll(product[8:], 80, 1))
    packed = jnp.where(lane < 44, product[:8], jnp.where(lane < 88, roll(roll(product[:8], 4, 0), 44, 1), tail))
    twice = jnp.where(subs() < 4, packed, roll(packed, 4, 0))
    for d in range(out.shape[0] // 8):
        out[pl.ds(8 * d, 8), :] = twice


def eliminate(tiles, count):
    sub = subs()
    done = list(tiles)

    def spread(value, row):
        return jnp.broadcast_to(value[row : row + 1, :], (8, 128))

    for k in range(0, count, 2):
        t, r = divmod(k, 8)
        row0, row1 = spread(tiles[t], r), spread(tiles[t], r + 1)
        cols = {
            u: [jnp.broadcast_to(tiles[u][:, k + i : k + i + 1], (8, 128)) for i in range(2)]
            for u in range(t, len(tiles))
        }
        a, b, c = spread(cols[t][0], r), spread(cols[t][1], r), spread(cols[t][1], r + 1)
        inv = 1.0 / (a * c - b * b)
        part0 = (c * row0 - b * row1) * inv
        part1 = (a * row1 - b * row0) * inv
        ratio = b / a
        first = row0 * (1.0 / jnp.sqrt(a))
        second = (row1 - ratio * row0) * (1.0 / jnp.sqrt(c - ratio * b))
        done[t] = jnp.where(sub == r, first, jnp.where(sub == r + 1, second, done[t]))
        for u in range(t, len(tiles)):
            tiles[u] = tiles[u] - (cols[u][0] * part0 + cols[u][1] * part1)
    return [jnp.where((lanes() >= 64) | (lanes() >= sub + 8 * t), tile, 0.0) for t, tile in enumerate(done)]


def old_factor_kernel(tile, scaled, work, head_ref):
    lane, sub = lanes(), subs()
    tiles = []
    for k in range(4):
        own = jnp.where(lane < 32, roll(tile[...], -32 * k, 1), 0.0)
        tiles.append(own + jnp.where(lane == sub + 8 * k + 64, 1.0, 0.0))
    for k, value in enumerate(eliminate(tiles, 32)):
        work[pl.ds(8 * k, 8), :] = value
    head_ref[...] = dot(work[:, pl.ds(64, 32)], scaled[...], 0)


def factor_kernel(parts, factor, head, snap, basis_ref, tri_ref, work):
    lane, sub = lanes(), subs()
    sums = [parts[pl.ds(8 * d, 8), :] for d in range(parts.shape[0] // 8)]
    while len(sums) > 1:
        sums = [sums[i] + sums[i + 1] for i in range(0, len(sums), 2)]
    total = sums[0] + roll(sums[0], 4, 0)
    top = jnp.where(lane < 44, jnp.where(sub < 4, total, roll(total, -44, 1)), 0.0)
    low = jnp.where(lane < 32, roll(total, -88, 1), roll(total, -80, 1))
    work[pl.ds(0, 8), :] = top
    work[pl.ds(8, 8), :] = jnp.where((sub < 4) & (lane < 44), low, 0.0)
    work[pl.ds(8, 8), pl.ds(32, 8)] = top.T[40:48]
    cross = work[:, pl.ds(0, 32)]
    inner = work[:, pl.ds(32, 16)]
    inverse = factor[:, pl.ds(64, 32)]
    below = dot(cross, inverse, 1)
    rest = snap[...] - dot(below, head[...], 0)
    inner = inner - dot(below, below, 1)
    work[...] = jnp.zeros((16, 128), jnp.float32)
    work[:, pl.ds(0, 16)] = inner
    tiles = [work[pl.ds(8 * t, 8), :] + jnp.where(lane == sub + 8 * t + 64, 1.0, 0.0) for t in range(2)]
    for t, value in enumerate(eliminate(tiles, 12)):
        work[pl.ds(8 * t, 8), :] = value
    tri_ref[pl.ds(0, 32), pl.ds(0, 32)] = factor[:, pl.ds(0, 32)]
    tri_ref[pl.ds(0, 32), pl.ds(32, 12)] = dot(inverse, cross, 1)[:, :12]
    tri_ref[pl.ds(32, 12), pl.ds(0, 32)] = jnp.zeros((12, 32), jnp.float32)
    tri_ref[pl.ds(32, 12), pl.ds(32, 12)] = work[pl.ds(0, 12), pl.ds(0, 12)]
    basis_ref[pl.ds(0, 32), :] = head[...]
    basis_ref[pl.ds(32, 12), :] = dot(work[:, pl.ds(64, 16)], rest, 0)[:12]


def f32(*shape):
    return jax.ShapeDtypeStruct(shape, jnp.float32)


def vmem(*shape):
    return pltpu.VMEM(shape, jnp.float32)


def held(value):
    return pltpu.with_memory_space_constraint(value, pltpu.VMEM)


def call(kernel, outs, scratch=(), count=None, aliases=None, limit=16, space=pltpu.VMEM):
    specs = [pl.BlockSpec(memory_space=space) for _ in range(count)]
    many = isinstance(outs, (tuple, list))
    out_specs = [pl.BlockSpec(memory_space=pltpu.VMEM)] * len(outs) if many else pl.BlockSpec(memory_space=pltpu.VMEM)
    return pl.pallas_call(
        kernel, out_shape=outs, in_specs=specs, out_specs=out_specs, scratch_shapes=list(scratch),
        input_output_aliases=aliases or {},
        compiler_params=pltpu.CompilerParams(vmem_limit_bytes=limit * 2**20),
    )


def shift(value, axis, step):
    count = lax.axis_size(axis)
    return lax.ppermute(value, axis, [(i, (i + step) % count) for i in range(count)])


def shift_both(value, step_y, step_z):
    ny, nz = lax.axis_size("gy"), lax.axis_size("gz")
    pairs = [
        (y * nz + z, (y + step_y) % ny * nz + (z + step_z) % nz) for y in range(ny) for z in range(nz)
    ]
    return lax.ppermute(value, ("gy", "gz"), pairs)


def across(value, step_z):
    if lax.axis_size("gy") == 2:
        return shift_both(value, 1, step_z)
    half = value.shape[0] // 2
    return jnp.concatenate([shift_both(value[:half], 1, step_z), shift_both(value[half:], -1, step_z)], 0)


def on_device(pop_ratio, solid_flags, class_ids, drag_table, row_map, old_basis, old_sigma):
    slab = ("gy", "gz")
    everyone = ("gx", "gy", "gz")
    owners = lax.axis_size(slab)
    devices = lax.axis_size(everyone)
    rows_local = old_basis.shape[1]
    highs = owners * rows_local // LOW
    cells = 4096
    tile = (8, 128)

    pops, g, zr, zl, y, cr, cl = call(
        init_kernel,
        (vmem(19, 2, 16, 128), vmem(2, 16, 128), vmem(3, *tile), vmem(3, *tile))
        + (vmem(2 * FIELDS, *tile), vmem(2, *tile), vmem(2, *tile)),
        (
            pltpu.SMEM(drag_table.shape, jnp.float32),
            pltpu.VMEM((19, 2, 16, 128), jnp.float32),
            pltpu.VMEM((2, 16, 128), jnp.int32),
            pltpu.VMEM((2, 16, 128), jnp.int32),
            pltpu.SemaphoreType.DMA((4,)),
        ),
        count=4,
        space=pltpu.HBM,
    )(*(pltpu.with_memory_space_constraint(v, pltpu.HBM) for v in (drag_table, pop_ratio, solid_flags, class_ids)))
    y = across(y, 0)
    left, right = shift(zr, "gz", 1), shift(zl, "gz", -1)
    cr, cl = across(cr, 1), across(cl, -1)

    wide = pltpu.VMEM((19, 2, 24, 256), jnp.float32)
    side = pltpu.VMEM((2, 5, 24, 256), jnp.float32)
    big, wall, vel, face = vmem(19, 2, 24, 256), vmem(2, 24, 256), vmem(3, 2, 16, 128), vmem(16, *tile)
    loaded = vmem(17, *tile)
    relaxed, g_wide, v0 = call(inner_kernel, (big, wall, vel), (wide,), count=4)(
        *map(held, (pops, g, left, right))
    )
    relaxed, g_wide, xr, xl = call(
        outer_kernel, (big, wall, face, face), (wide,), count=5, aliases={0: 0, 1: 1}
    )(*map(held, (relaxed, g_wide, y, cr, cl)))
    vels = [v0]
    old, own = call(
        functools.partial(old_kernel, float(rows_local * devices)),
        (vmem(32, rows_local), vmem(*tile)),
        (pltpu.VMEM((32, 128), jnp.float32),),
        count=2,
    )(old_basis, old_sigma[:, None])
    ring = lax.axis_size("gx") == 4
    if not ring:
        own = lax.psum(own, "gx")
    none = jnp.zeros(tile, jnp.float32)
    step = jax.jit(call(step_kernel, (big, vel, loaded, loaded), (wide, side), count=6))
    onehot = call(onehot_kernel, pltpu.VMEM((LOW, cells), jnp.bfloat16), count=1)(row_map)
    riders, got = (own, own), [none] * 3
    for s in range(1, STEPS):
        xr, xl = shift(xr, "gx", 1), shift(xl, "gx", -1)
        if s == 2 and ring:
            got[0], got[1] = xr[16], xl[16]
            riders = (xr[16], none)
        if s == 3 and ring:
            got[2] = xr[16]
            riders = (none, none)
        relaxed, vel_s, xr, xl = step(*map(held, (relaxed, g_wide, xr, xl, *riders)))
        vels.append(vel_s)
    xr, xl = shift(xr, "gx", 1), shift(xl, "gx", -1)

    early = call(
        early_kernel, vmem(highs, 16, LOW), (pltpu.VMEM((32 * highs, cells), jnp.bfloat16),), count=5,
        limit=8 + highs // 2,
    )(*map(held, vels[:3]), row_map, held(onehot))
    term = call(
        late_kernel, f32(highs, 16, LOW), (pltpu.VMEM((6 * highs, cells), jnp.bfloat16),), count=8,
        limit=8 + highs // 2,
    )(held(vels[3]), row_map, *map(held, (onehot, early, own, *got)))
    parts = lax.all_to_all(term.reshape(16 * highs, LOW), slab, 0, 0, tiled=True)
    snap, old_tile, gram = call(
        functools.partial(gram_kernel, float(rows_local * devices)),
        (vmem(16, rows_local), vmem(*tile), f32(4 * devices, 128)),
        (pltpu.VMEM((128, rows_local), jnp.float32),),
        count=2,
    )(held(parts), held(old))
    grams = lax.all_to_all(gram, everyone, 0, 0, tiled=True)
    factor, head = call(old_factor_kernel, (vmem(32, 128), vmem(32, rows_local)), count=2)(held(old_tile), held(old))
    new_basis, upper = call(
        factor_kernel, (f32(44, rows_local), f32(44, 44)), (pltpu.VMEM((16, 128), jnp.float32),), count=4
    )(*map(held, (grams, factor, head, snap)))
    populations = call(last_kernel, f32(19, 2, 16, 128), (side,), count=3)(*map(held, (relaxed, xr, xl)))
    return (populations, new_basis, upper)


def solution(mesh):
    in_specs = (
        P(None, "gx", "gy", "gz"),
        P("gx", "gy", "gz"),
        P("gx", "gy", "gz"),
        P(),
        P("gx", "gy", "gz"),
        P(None, ("gx", "gy", "gz")),
        P(),
    )
    out_specs = (P(None, "gx", "gy", "gz"), P(None, ("gx", "gy", "gz")), P())

    return jax.shard_map(on_device, mesh=mesh, in_specs=in_specs, out_specs=out_specs, check_vma=False)
```

```python
import functools

import jax
import jax.numpy as jnp
import numpy as np
from jax import lax
from jax.experimental import pallas as pl
from jax.experimental.pallas import tpu as pltpu
from jax.sharding import PartitionSpec as P


STEPS = 4
VOX_ROW = 8
LATTICE = np.array(
    [
        [0, 0, 0],
        [1, 0, 0],
        [-1, 0, 0],
        [0, 1, 0],
        [0, -1, 0],
        [0, 0, 1],
        [0, 0, -1],
        [1, 1, 0],
        [-1, -1, 0],
        [1, -1, 0],
        [-1, 1, 0],
        [1, 0, 1],
        [-1, 0, -1],
        [1, 0, -1],
        [-1, 0, 1],
        [0, 1, 1],
        [0, -1, -1],
        [0, 1, -1],
        [0, -1, 1],
    ]
)
OPPOSITE = [0, 2, 1, 4, 3, 6, 5, 8, 7, 10, 9, 12, 11, 14, 13, 16, 15, 18, 17]
WEIGHTS = [1.0 / 3.0] + [1.0 / 18.0] * 6 + [1.0 / 36.0] * 12
PAIRS = [(q, OPPOSITE[q]) for q in range(1, 19) if q < OPPOSITE[q]]
PLUS_X = [q for q in range(19) if LATTICE[q, 0] == 1]
MINUS_X = [q for q in range(19) if LATTICE[q, 0] == -1]
relax_time = 0.9
vel_scale = 16.0

FIELDS = 20
LOW = 256


def lanes(shape=(8, 128)):
    return lax.broadcasted_iota(jnp.int32, shape, len(shape) - 1)


def subs(shape=(8, 128)):
    return lax.broadcasted_iota(jnp.int32, shape, len(shape) - 2)


def roll(value, shift, axis):
    size = value.shape[axis]
    shift = shift % size
    return value if shift == 0 else pltpu.roll(value, shift, axis)


def init_kernel(
    table_hbm, ratio_hbm, solid_hbm, cls_hbm,
    pops_ref, g_ref, zr_ref, zl_ref, y_ref, cr_ref, cl_ref,
    table, ratio, solid, cls, sems,
):
    pairs = ((ratio_hbm, ratio), (table_hbm, table), (solid_hbm, solid), (cls_hbm, cls))
    copies = [pltpu.make_async_copy(src, dst, sems.at[i]) for i, (src, dst) in enumerate(pairs)]
    for copy in copies:
        copy.start()
    for copy in copies:
        copy.wait()
    lane, sub = lanes(), subs()
    blank = jnp.zeros((8, 128), jnp.float32)
    zr, zl = [blank] * 3, [blank] * 3
    cr, cl = [blank] * 2, [blank] * 2
    for f in range(FIELDS):
        tiles = {}
        for x in range(2):
            for yt in range(2):
                rows = pl.ds(8 * yt, 8)
                if f < 19:
                    tile = ratio[f, x, rows, :] * WEIGHTS[f]
                    pops_ref[f, x, rows, :] = tile
                else:
                    ids = cls[x, rows, :]
                    drag = jnp.zeros((8, 128), jnp.float32)
                    for c in range(table.shape[0]):
                        drag = jnp.where(ids == c, table[c], drag)
                    tile = jnp.where(solid[x, rows, :] == 1, -1.0, 1.0 + 0.5 * drag)
                    g_ref[x, rows, :] = tile
                tiles[x, yt] = tile
                at, k = divmod(f * 4 + x * 2 + yt, 32)
                here = (lane >= 4 * k) & (lane < 4 * k + 4)
                zr[at] = jnp.where(here, roll(tile, 4 * k - 124, 1), zr[at])
                zl[at] = jnp.where(here, roll(tile, 4 * k, 1), zl[at])
        up = jnp.where(sub < 4, roll(tiles[0, 1], 4, 0), tiles[1, 1])
        down = jnp.where(sub < 4, tiles[0, 0], roll(tiles[1, 0], 4, 0))
        y_ref[f] = up
        y_ref[FIELDS + f] = down
        here = (lane >= 4 * f) & (lane < 4 * f + 4)
        for i, tile in enumerate((up, down)):
            cr[i] = jnp.where(here, roll(tile, 4 * f - 124, 1), cr[i])
            cl[i] = jnp.where(here, roll(tile, 4 * f, 1), cl[i])
    for at in range(3):
        zr_ref[at] = zr[at]
        zl_ref[at] = zl[at]
    for at in range(2):
        cr_ref[at] = cr[at]
        cl_ref[at] = cl[at]


def moments(pops, g):
    density = pops[0]
    for q in range(1, 19):
        density = density + pops[q]
    scale = 1.0 / (density * jnp.abs(g))
    speeds = []
    for a in range(3):
        total = None
        for q in range(19):
            c = LATTICE[q, a]
            if c == 1:
                total = pops[q] if total is None else total + pops[q]
            elif c == -1:
                total = total - pops[q]
        speeds.append(total * scale)
    return density, speeds


def collide(pops, g):
    density, speeds = moments(pops, g)
    square = speeds[0] * speeds[0] + speeds[1] * speeds[1] + speeds[2] * speeds[2]
    solid = g < 0.0
    keep = 1.0 - 1.0 / relax_time
    base = 1.0 - 1.5 * square
    part = {w: density * (w / relax_time) for w in sorted(set(WEIGHTS))}
    relaxed = [None] * 19
    rest = pops[0] * keep + part[WEIGHTS[0]] * base
    relaxed[0] = jnp.where(solid, pops[0], rest)
    for q, o in PAIRS:
        along = None
        for a in range(3):
            c = LATTICE[q, a]
            if c == 1:
                along = speeds[a] if along is None else along + speeds[a]
            elif c == -1:
                along = -speeds[a] if along is None else along - speeds[a]
        even = part[WEIGHTS[q]] * (base + 4.5 * along * along)
        odd = part[WEIGHTS[q]] * (3.0 * along)
        relaxed[q] = jnp.where(solid, pops[o], pops[q] * keep + (even + odd))
        relaxed[o] = jnp.where(solid, pops[q], pops[o] * keep + (even - odd))
    factor = jnp.where(solid, 0.0, vel_scale / VOX_ROW)
    return relaxed, [s * factor for s in speeds]


def collide_all(source, g_of, out, vel_ref, tiles=range(3)):
    for x in range(2):
        for yt in tiles:
            for lt in range(2):
                rows, cols = pl.ds(8 * yt, 8), pl.ds(128 * lt, 128)
                pops = [source(q, x, rows, cols) for q in range(19)]
                relaxed, vel = collide(pops, g_of[x, rows, cols])
                for q in range(19):
                    out[q, x, rows, cols] = relaxed[q]
                if vel_ref is not None and yt < 2 and lt == 0:
                    for a in range(3):
                        vel_ref[a, x, rows, :] = vel[a]


def pack_x(out, xr_ref, xl_ref):
    lane = lanes()
    for ref, directions, x in ((xr_ref, PLUS_X, 1), (xl_ref, MINUS_X, 0)):
        extra = jnp.zeros((8, 128), jnp.float32)
        for i, q in enumerate(directions):
            for yt in range(3):
                j = 3 * i + yt
                ref[j] = out[q, x, pl.ds(8 * yt, 8), pl.ds(0, 128)]
                tile = out[q, x, pl.ds(8 * yt, 8), pl.ds(128, 128)]
                here = (lane >= 8 * j) & (lane < 8 * j + 8)
                extra = jnp.where(here, roll(tile, 4 + 8 * j, 1), extra)
        ref[15] = extra


def inner_kernel(pops, g_in, left, right, out, g_ref, vel_ref, wide):
    lane = lanes()
    for f in range(FIELDS):
        ref = wide.at[f] if f < 19 else g_ref
        for x in range(2):
            for yt in range(2):
                rows = pl.ds(8 * yt, 8)
                own = pops[f, x, rows, :] if f < 19 else g_in[x, rows, :]
                at, k = divmod(f * 4 + x * 2 + yt, 32)
                tile = jnp.where(lane < 4, roll(right[at], -4 * k, 1), own)
                tile = jnp.where(lane >= 124, roll(left[at], 124 - 4 * k, 1), tile)
                ref[x, rows, pl.ds(0, 128)] = own
                ref[x, rows, pl.ds(128, 128)] = tile
    collide_all(lambda q, x, rows, cols: wide[q, x, rows, cols], g_ref, out, vel_ref, range(2))


def outer_kernel(out_in, g_in, y, cr, cl, out, g_ref, xr_ref, xl_ref, wide):
    lane, sub = lanes(), subs()
    for f in range(FIELDS):
        ref = wide.at[f] if f < 19 else g_ref
        pairs = []
        for i in range(2):
            own = y[FIELDS * i + f]
            tile = jnp.where(lane < 4, roll(cl[i], -4 * f, 1), own)
            pairs.append((own, jnp.where(lane >= 124, roll(cr[i], 124 - 4 * f, 1), tile)))
        high, low = pairs
        for lt in range(2):
            cols = pl.ds(128 * lt, 128)
            ref[0, pl.ds(16, 8), cols] = jnp.where(sub < 4, low[lt], roll(high[lt], 4, 0))
            ref[1, pl.ds(16, 8), cols] = jnp.where(sub < 4, roll(low[lt], 4, 0), high[lt])
    collide_all(lambda q, x, rows, cols: wide[q, x, rows, cols], g_ref, out, None, (2,))
    pack_x(out, xr_ref, xl_ref)


def unpack_x(xr, xl, side):
    for s, ref in enumerate((xr, xl)):
        for i in range(5):
            for yt in range(3):
                j = 3 * i + yt
                side[s, i, pl.ds(8 * yt, 8), pl.ds(0, 128)] = ref[j]
                side[s, i, pl.ds(8 * yt, 8), pl.ds(128, 128)] = roll(ref[15], -(8 * j + 4), 1)


def turned(value, q):
    return roll(roll(value, int(LATTICE[q, 1]), 0), int(LATTICE[q, 2]), 1)


def remote(q, x):
    if LATTICE[q, 0] == 1 and x == 0:
        return 0, PLUS_X.index(q)
    if LATTICE[q, 0] == -1 and x == 1:
        return 1, MINUS_X.index(q)
    return None


def local_kernel(prev, ahead):
    for q in range(19):
        for x in range(2):
            if remote(q, x) is None:
                ahead[q, x] = turned(prev[q, x - int(LATTICE[q, 0])], q)


def take_faces(xr, xl, side):
    unpack_x(xr, xl, side)
    for s, directions in enumerate((PLUS_X, MINUS_X)):
        for i, q in enumerate(directions):
            side[s, i] = turned(side[s, i], q)


def chooser(ahead, side):
    def pick(q, x, rows, cols):
        at = remote(q, x)
        return ahead[q, x, rows, cols] if at is None else side[at[0], at[1], rows, cols]

    return pick


def step_kernel(ahead, g_ref, xr, xl, rider_r, rider_l, out, vel_ref, xr_ref, xl_ref, side):
    take_faces(xr, xl, side)
    collide_all(chooser(ahead, side), g_ref, out, vel_ref)
    pack_x(out, xr_ref, xl_ref)
    xr_ref[16] = rider_r[...]
    xl_ref[16] = rider_l[...]


def end_step_kernel(ahead, g_ref, xr, xl, out, xr_ref, xl_ref, side):
    take_faces(xr, xl, side)
    collide_all(chooser(ahead, side), g_ref, out, None)
    pack_x(out, xr_ref, xl_ref)


def last_kernel(prev, xr, xl, out, side):
    take_faces(xr, xl, side)
    for q in range(19):
        for x in range(2):
            at = remote(q, x)
            value = turned(prev[q, x - int(LATTICE[q, 0])], q) if at is None else side[at[0], at[1]]
            out[q, x] = value[:16, :128]


def split(value):
    big = value.astype(jnp.bfloat16).astype(jnp.float32)
    return big, value - big


def onehot_kernel(row_map, right):
    low_at = lax.broadcasted_iota(jnp.int32, (LOW, 128), 0)
    for x in range(2):
        for y in range(16):
            rows = row_map[x, pl.ds(y, 1), :]
            low = rows - (rows // LOW) * LOW
            cols = pl.ds(128 * (16 * x + y), 128)
            right[:, cols] = jnp.where(low_at == low, 1.0, 0.0).astype(jnp.bfloat16)


def times_onehot(left, right):
    return lax.dot_general(
        left[...], right[...], (((1,), (1,)), ((), ())), preferred_element_type=jnp.float32
    )


def restricted(v, row_map, right, left):
    highs = left.shape[0] // 6
    high_at = lax.broadcasted_iota(jnp.int32, (highs, 128), 0)
    for x in range(2):
        for y in range(16):
            cols = pl.ds(128 * (16 * x + y), 128)
            here = high_at == row_map[x, pl.ds(y, 1), :] // LOW
            for a in range(3):
                for i, part in enumerate(split(v[a, x, pl.ds(y, 1), :])):
                    left[pl.ds(highs * (3 * i + a), highs), cols] = jnp.where(here, part, 0.0).astype(jnp.bfloat16)
    both = times_onehot(left, right)
    half = 3 * highs
    return both[:half] + both[half:]


def part_kernel(v, row_map, right, out, left):
    out[...] = restricted(v, row_map, right, left)


def early_kernel(v2, row_map, right, part0, part1, out, left):
    highs = out.shape[0]
    parts = (part0[...], part1[...], restricted(v2, row_map, right, left))
    for h in range(highs):
        for s, part in enumerate(parts):
            for a in range(3):
                out[h, pl.ds(3 * s + a, 1), :] = part[highs * a + h : highs * a + h + 1]
        out[h, pl.ds(9, 7), :] = jnp.zeros((7, LOW), jnp.float32)


def old_kernel(total_rows, basis, sigma, scaled_ref, tile_ref, work):
    scaled = basis[...] * sigma[...]
    scaled_ref[...] = scaled
    work[...] = jnp.zeros((32, 128), jnp.float32)
    work[:, pl.ds(0, 32)] = dot(scaled, scaled, 1) * (1.0 / total_rows)
    lane = lanes()
    tile = work[pl.ds(0, 8), :]
    for k in range(1, 4):
        here = (lane >= 32 * k) & (lane < 32 * k + 32)
        tile = jnp.where(here, roll(work[pl.ds(8 * k, 8), :], 32 * k, 1), tile)
    tile_ref[...] = tile


def dot(a, b, dim):
    return lax.dot_general(
        a,
        b,
        (((1,), (dim,)), ((), ())),
        precision=lax.Precision.HIGHEST,
        preferred_element_type=jnp.float32,
    )


def late_kernel(ahead, g_ref, xr, xl, row_map, right, early, own, near_r, near_l, far, out, left, side, v3):
    take_faces(xr, xl, side)
    pick = chooser(ahead, side)
    for x in range(2):
        for yt in range(2):
            rows, cols = pl.ds(8 * yt, 8), pl.ds(0, 128)
            g = g_ref[x, rows, cols]
            _, speeds = moments([pick(q, x, rows, cols) for q in range(19)], g)
            factor = jnp.where(g < 0.0, 0.0, vel_scale / VOX_ROW)
            for a in range(3):
                v3[a, x, rows, :] = speeds[a] * factor
    highs = out.shape[0]
    both = restricted(v3, row_map, right, left)
    out[...] = early[...]
    old = (own[...] + far[...]) + (near_r[...] + near_l[...])
    for h in range(highs):
        for a in range(3):
            out[h, pl.ds(9 + a, 1), :] = both[highs * a + h : highs * a + h + 1]
        if h % 2 == 0:
            out[h, pl.ds(12, 4), pl.ds(0, 128)] = old[:4]
            out[h, pl.ds(12, 4), pl.ds(128, 128)] = old[4:]


def gram_kernel(total_rows, parts, scaled, snap_ref, tile_ref, out, aug):
    owners = parts.shape[0] // 32
    total = parts[pl.ds(0, 32), :]
    for o in range(1, owners):
        total = total + parts[pl.ds(32 * o, 32), :]
    tile_ref[pl.ds(0, 4), :] = total[12:16, :128]
    tile_ref[pl.ds(4, 4), :] = total[12:16, 128:]
    used = lax.broadcasted_iota(jnp.int32, (16, LOW), 0) < 12
    aug[pl.ds(0, 32), :] = scaled[...]
    aug[pl.ds(32, 16), pl.ds(0, LOW)] = jnp.where(used, total[:16], 0.0)
    aug[pl.ds(32, 16), pl.ds(LOW, LOW)] = jnp.where(used, total[16:], 0.0)
    aug[pl.ds(48, 80), :] = jnp.zeros((80, 2 * LOW), jnp.float32)
    snap = aug[pl.ds(32, 16), :]
    snap_ref[...] = snap
    product = dot(snap, aug[...], 1) * (1.0 / total_rows)
    lane = lanes()
    tail = jnp.where(lane < 120, roll(product[8:], 88, 1), roll(product[8:], 80, 1))
    packed = jnp.where(lane < 44, product[:8], jnp.where(lane < 88, roll(roll(product[:8], 4, 0), 44, 1), tail))
    twice = jnp.where(subs() < 4, packed, roll(packed, 4, 0))
    for d in range(out.shape[0] // 8):
        out[pl.ds(8 * d, 8), :] = twice


def eliminate(tiles, count):
    sub = subs()
    done = list(tiles)

    def spread(value, row):
        return jnp.broadcast_to(value[row : row + 1, :], (8, 128))

    for k in range(0, count, 2):
        t, r = divmod(k, 8)
        row0, row1 = spread(tiles[t], r), spread(tiles[t], r + 1)
        cols = {
            u: [jnp.broadcast_to(tiles[u][:, k + i : k + i + 1], (8, 128)) for i in range(2)]
            for u in range(t, len(tiles))
        }
        a, b, c = spread(cols[t][0], r), spread(cols[t][1], r), spread(cols[t][1], r + 1)
        inv = 1.0 / (a * c - b * b)
        part0 = (c * row0 - b * row1) * inv
        part1 = (a * row1 - b * row0) * inv
        ratio = b / a
        first = row0 * (1.0 / jnp.sqrt(a))
        second = (row1 - ratio * row0) * (1.0 / jnp.sqrt(c - ratio * b))
        done[t] = jnp.where(sub == r, first, jnp.where(sub == r + 1, second, done[t]))
        for u in range(t, len(tiles)):
            tiles[u] = tiles[u] - (cols[u][0] * part0 + cols[u][1] * part1)
    return [jnp.where((lanes() >= 64) | (lanes() >= sub + 8 * t), tile, 0.0) for t, tile in enumerate(done)]


def old_factor_kernel(tile, scaled, work, head_ref):
    lane, sub = lanes(), subs()
    tiles = []
    for k in range(4):
        own = jnp.where(lane < 32, roll(tile[...], -32 * k, 1), 0.0)
        tiles.append(own + jnp.where(lane == sub + 8 * k + 64, 1.0, 0.0))
    for k, value in enumerate(eliminate(tiles, 32)):
        work[pl.ds(8 * k, 8), :] = value
    head_ref[...] = dot(work[:, pl.ds(64, 32)], scaled[...], 0)


def factor_kernel(parts, factor, head, snap, basis_ref, tri_ref, work):
    lane, sub = lanes(), subs()
    sums = [parts[pl.ds(8 * d, 8), :] for d in range(parts.shape[0] // 8)]
    while len(sums) > 1:
        sums = [sums[i] + sums[i + 1] for i in range(0, len(sums), 2)]
    total = sums[0] + roll(sums[0], 4, 0)
    top = jnp.where(lane < 44, jnp.where(sub < 4, total, roll(total, -44, 1)), 0.0)
    low = jnp.where(lane < 32, roll(total, -88, 1), roll(total, -80, 1))
    work[pl.ds(0, 8), :] = top
    work[pl.ds(8, 8), :] = jnp.where((sub < 4) & (lane < 44), low, 0.0)
    work[pl.ds(8, 8), pl.ds(32, 8)] = top.T[40:48]
    cross = work[:, pl.ds(0, 32)]
    inner = work[:, pl.ds(32, 16)]
    inverse = factor[:, pl.ds(64, 32)]
    below = dot(cross, inverse, 1)
    rest = snap[...] - dot(below, head[...], 0)
    inner = inner - dot(below, below, 1)
    work[...] = jnp.zeros((16, 128), jnp.float32)
    work[:, pl.ds(0, 16)] = inner
    tiles = [work[pl.ds(8 * t, 8), :] + jnp.where(lane == sub + 8 * t + 64, 1.0, 0.0) for t in range(2)]
    for t, value in enumerate(eliminate(tiles, 12)):
        work[pl.ds(8 * t, 8), :] = value
    tri_ref[pl.ds(0, 32), pl.ds(0, 32)] = factor[:, pl.ds(0, 32)]
    tri_ref[pl.ds(0, 32), pl.ds(32, 12)] = dot(inverse, cross, 1)[:, :12]
    tri_ref[pl.ds(32, 12), pl.ds(0, 32)] = jnp.zeros((12, 32), jnp.float32)
    tri_ref[pl.ds(32, 12), pl.ds(32, 12)] = work[pl.ds(0, 12), pl.ds(0, 12)]
    basis_ref[pl.ds(0, 32), :] = head[...]
    basis_ref[pl.ds(32, 12), :] = dot(work[:, pl.ds(64, 16)], rest, 0)[:12]


def f32(*shape):
    return jax.ShapeDtypeStruct(shape, jnp.float32)


def vmem(*shape):
    return pltpu.VMEM(shape, jnp.float32)


def held(value):
    return pltpu.with_memory_space_constraint(value, pltpu.VMEM)


def call(kernel, outs, scratch=(), count=None, aliases=None, limit=16, space=pltpu.VMEM):
    specs = [pl.BlockSpec(memory_space=space) for _ in range(count)]
    many = isinstance(outs, (tuple, list))
    out_specs = [pl.BlockSpec(memory_space=pltpu.VMEM)] * len(outs) if many else pl.BlockSpec(memory_space=pltpu.VMEM)
    return pl.pallas_call(
        kernel, out_shape=outs, in_specs=specs, out_specs=out_specs, scratch_shapes=list(scratch),
        input_output_aliases=aliases or {},
        compiler_params=pltpu.CompilerParams(vmem_limit_bytes=limit * 2**20),
    )


def shift(value, axis, step):
    count = lax.axis_size(axis)
    return lax.ppermute(value, axis, [(i, (i + step) % count) for i in range(count)])


def shift_both(value, step_y, step_z):
    ny, nz = lax.axis_size("gy"), lax.axis_size("gz")
    pairs = [
        (y * nz + z, (y + step_y) % ny * nz + (z + step_z) % nz) for y in range(ny) for z in range(nz)
    ]
    return lax.ppermute(value, ("gy", "gz"), pairs)


def across(value, step_z):
    if lax.axis_size("gy") == 2:
        return shift_both(value, 1, step_z)
    half = value.shape[0] // 2
    return jnp.concatenate([shift_both(value[:half], 1, step_z), shift_both(value[half:], -1, step_z)], 0)


def on_device(pop_ratio, solid_flags, class_ids, drag_table, row_map, old_basis, old_sigma):
    slab = ("gy", "gz")
    everyone = ("gx", "gy", "gz")
    owners = lax.axis_size(slab)
    devices = lax.axis_size(everyone)
    rows_local = old_basis.shape[1]
    highs = owners * rows_local // LOW
    cells = 4096
    tile = (8, 128)

    pops, g, zr, zl, y, cr, cl = call(
        init_kernel,
        (vmem(19, 2, 16, 128), vmem(2, 16, 128), vmem(3, *tile), vmem(3, *tile))
        + (vmem(2 * FIELDS, *tile), vmem(2, *tile), vmem(2, *tile)),
        (
            pltpu.SMEM(drag_table.shape, jnp.float32),
            pltpu.VMEM((19, 2, 16, 128), jnp.float32),
            pltpu.VMEM((2, 16, 128), jnp.int32),
            pltpu.VMEM((2, 16, 128), jnp.int32),
            pltpu.SemaphoreType.DMA((4,)),
        ),
        count=4,
        space=pltpu.HBM,
    )(*(pltpu.with_memory_space_constraint(v, pltpu.HBM) for v in (drag_table, pop_ratio, solid_flags, class_ids)))
    y = across(y, 0)
    left, right = shift(zr, "gz", 1), shift(zl, "gz", -1)
    cr, cl = across(cr, 1), across(cl, -1)

    wide = pltpu.VMEM((19, 2, 24, 256), jnp.float32)
    side = pltpu.VMEM((2, 5, 24, 256), jnp.float32)
    big, wall, vel, face = vmem(19, 2, 24, 256), vmem(2, 24, 256), vmem(3, 2, 16, 128), vmem(16, *tile)
    loaded = vmem(17, *tile)
    relaxed, g_wide, v0 = call(inner_kernel, (big, wall, vel), (wide,), count=4)(
        *map(held, (pops, g, left, right))
    )
    relaxed, g_wide, xr, xl = call(
        outer_kernel, (big, wall, face, face), (wide,), count=5, aliases={0: 0, 1: 1}
    )(*map(held, (relaxed, g_wide, y, cr, cl)))
    vels = [v0]
    old, own = call(
        functools.partial(old_kernel, float(rows_local * devices)),
        (vmem(32, rows_local), vmem(*tile)),
        (pltpu.VMEM((32, 128), jnp.float32),),
        count=2,
    )(old_basis, old_sigma[:, None])
    ring = lax.axis_size("gx") == 4
    if not ring:
        own = lax.psum(own, "gx")
    none = jnp.zeros(tile, jnp.float32)
    step = jax.jit(call(step_kernel, (big, vel, loaded, loaded), (side,), count=6))
    local = jax.jit(call(local_kernel, big, count=1))
    onehot = call(onehot_kernel, pltpu.VMEM((LOW, cells), jnp.bfloat16), count=1)(row_map)
    riders, got = (own, own), [none] * 3
    for s in range(1, STEPS):
        xr, xl = shift(xr, "gx", 1), shift(xl, "gx", -1)
        if s == 2 and ring:
            got[0], got[1] = xr[16], xl[16]
            riders = (xr[16], none)
        if s == 3 and ring:
            got[2] = xr[16]
        ahead = local(held(relaxed))
        if s < 3:
            relaxed, vel_s, xr, xl = step(*map(held, (ahead, g_wide, xr, xl, *riders)))
            vels.append(vel_s)
    state = tuple(map(held, (ahead, g_wide, xr, xl)))
    relaxed, xr, xl = call(end_step_kernel, (big, face, face), (side,), count=4)(*state)
    xr, xl = shift(xr, "gx", 1), shift(xl, "gx", -1)

    part = jax.jit(
        call(
            part_kernel,
            vmem(3 * highs, LOW),
            (pltpu.VMEM((6 * highs, cells), jnp.bfloat16),),
            count=3,
            limit=8 + highs // 2,
        )
    )
    parts = []
    for i in range(2):
        parts.append(part(held(vels[i]), row_map, held(onehot)))
    early = call(
        early_kernel,
        vmem(highs, 16, LOW),
        (pltpu.VMEM((6 * highs, cells), jnp.bfloat16),),
        count=5,
        limit=8 + highs // 2,
    )(held(vels[2]), row_map, *map(held, (onehot, *parts)))
    term = call(
        late_kernel,
        f32(highs, 16, LOW),
        (pltpu.VMEM((6 * highs, cells), jnp.bfloat16), side, pltpu.VMEM((3, 2, 16, 128), jnp.float32)),
        count=11,
        limit=8 + highs // 2,
    )(*state, row_map, *map(held, (onehot, early, own, *got)))
    parts = lax.all_to_all(term.reshape(16 * highs, LOW), slab, 0, 0, tiled=True)
    snap, old_tile, gram = call(
        functools.partial(gram_kernel, float(rows_local * devices)),
        (vmem(16, rows_local), vmem(*tile), f32(4 * devices, 128)),
        (pltpu.VMEM((128, rows_local), jnp.float32),),
        count=2,
    )(held(parts), held(old))
    grams = lax.all_to_all(gram, everyone, 0, 0, tiled=True)
    factor, head = call(old_factor_kernel, (vmem(32, 128), vmem(32, rows_local)), count=2)(held(old_tile), held(old))
    new_basis, upper = call(
        factor_kernel, (f32(44, rows_local), f32(44, 44)), (pltpu.VMEM((16, 128), jnp.float32),), count=4
    )(*map(held, (grams, factor, head, snap)))
    populations = call(last_kernel, f32(19, 2, 16, 128), (side,), count=3)(*map(held, (relaxed, xr, xl)))
    return (populations, new_basis, upper)


def solution(mesh):
    in_specs = (
        P(None, "gx", "gy", "gz"),
        P("gx", "gy", "gz"),
        P("gx", "gy", "gz"),
        P(),
        P("gx", "gy", "gz"),
        P(None, ("gx", "gy", "gz")),
        P(),
    )
    out_specs = (P(None, "gx", "gy", "gz"), P(None, ("gx", "gy", "gz")), P())

    return jax.shard_map(on_device, mesh=mesh, in_specs=in_specs, out_specs=out_specs, check_vma=False)
```

```python
import functools

import jax
import jax.numpy as jnp
import numpy as np
from jax import lax
from jax.experimental import pallas as pl
from jax.experimental.pallas import tpu as pltpu
from jax.sharding import PartitionSpec as P


VOX_ROW = 8
LATTICE = np.array(
    [
        [0, 0, 0],
        [1, 0, 0],
        [-1, 0, 0],
        [0, 1, 0],
        [0, -1, 0],
        [0, 0, 1],
        [0, 0, -1],
        [1, 1, 0],
        [-1, -1, 0],
        [1, -1, 0],
        [-1, 1, 0],
        [1, 0, 1],
        [-1, 0, -1],
        [1, 0, -1],
        [-1, 0, 1],
        [0, 1, 1],
        [0, -1, -1],
        [0, 1, -1],
        [0, -1, 1],
    ]
)
OPPOSITE = [0, 2, 1, 4, 3, 6, 5, 8, 7, 10, 9, 12, 11, 14, 13, 16, 15, 18, 17]
WEIGHTS = [1.0 / 3.0] + [1.0 / 18.0] * 6 + [1.0 / 36.0] * 12
PAIRS = [(q, OPPOSITE[q]) for q in range(1, 19) if q < OPPOSITE[q]]
PLUS_X = [q for q in range(19) if LATTICE[q, 0] == 1]
MINUS_X = [q for q in range(19) if LATTICE[q, 0] == -1]
relax_time = 0.9
vel_scale = 16.0

FIELDS = 20
LOW = 256


def lanes(shape=(8, 128)):
    return lax.broadcasted_iota(jnp.int32, shape, len(shape) - 1)


def subs(shape=(8, 128)):
    return lax.broadcasted_iota(jnp.int32, shape, len(shape) - 2)


def roll(value, shift, axis):
    size = value.shape[axis]
    shift = shift % size
    return value if shift == 0 else pltpu.roll(value, shift, axis)


def init_kernel(
    table_hbm, ratio_hbm, solid_hbm, cls_hbm,
    pops_ref, g_ref, zr_ref, zl_ref, y_ref, cr_ref, cl_ref,
    table, ratio, solid, cls, sems,
):
    pairs = ((ratio_hbm, ratio), (table_hbm, table), (solid_hbm, solid), (cls_hbm, cls))
    copies = [pltpu.make_async_copy(src, dst, sems.at[i]) for i, (src, dst) in enumerate(pairs)]
    for copy in copies:
        copy.start()
    for copy in copies:
        copy.wait()
    lane, sub = lanes(), subs()
    blank = jnp.zeros((8, 128), jnp.float32)
    zr, zl = [blank] * 3, [blank] * 3
    cr, cl = [blank] * 2, [blank] * 2
    for f in range(FIELDS):
        tiles = {}
        for x in range(2):
            for yt in range(2):
                rows = pl.ds(8 * yt, 8)
                if f < 19:
                    tile = ratio[f, x, rows, :] * WEIGHTS[f]
                    pops_ref[f, x, rows, :] = tile
                else:
                    ids = cls[x, rows, :]
                    drag = jnp.zeros((8, 128), jnp.float32)
                    for c in range(table.shape[0]):
                        drag = jnp.where(ids == c, table[c], drag)
                    tile = jnp.where(solid[x, rows, :] == 1, -1.0, 1.0 + 0.5 * drag)
                    g_ref[x, rows, :] = tile
                tiles[x, yt] = tile
                at, k = divmod(f * 4 + x * 2 + yt, 32)
                here = (lane >= 4 * k) & (lane < 4 * k + 4)
                zr[at] = jnp.where(here, roll(tile, 4 * k - 124, 1), zr[at])
                zl[at] = jnp.where(here, roll(tile, 4 * k, 1), zl[at])
        up = jnp.where(sub < 4, roll(tiles[0, 1], 4, 0), tiles[1, 1])
        down = jnp.where(sub < 4, tiles[0, 0], roll(tiles[1, 0], 4, 0))
        y_ref[f] = up
        y_ref[FIELDS + f] = down
        here = (lane >= 4 * f) & (lane < 4 * f + 4)
        for i, tile in enumerate((up, down)):
            cr[i] = jnp.where(here, roll(tile, 4 * f - 124, 1), cr[i])
            cl[i] = jnp.where(here, roll(tile, 4 * f, 1), cl[i])
    for at in range(3):
        zr_ref[at] = zr[at]
        zl_ref[at] = zl[at]
    for at in range(2):
        cr_ref[at] = cr[at]
        cl_ref[at] = cl[at]


def moments(pops, g):
    density = pops[0]
    for q in range(1, 19):
        density = density + pops[q]
    scale = 1.0 / (density * jnp.abs(g))
    speeds = []
    for a in range(3):
        total = None
        for q in range(19):
            c = LATTICE[q, a]
            if c == 1:
                total = pops[q] if total is None else total + pops[q]
            elif c == -1:
                total = total - pops[q]
        speeds.append(total * scale)
    return density, speeds


def collide(pops, g):
    density, speeds = moments(pops, g)
    square = speeds[0] * speeds[0] + speeds[1] * speeds[1] + speeds[2] * speeds[2]
    solid = g < 0.0
    keep = 1.0 - 1.0 / relax_time
    base = 1.0 - 1.5 * square
    part = {w: density * (w / relax_time) for w in sorted(set(WEIGHTS))}
    relaxed = [None] * 19
    rest = pops[0] * keep + part[WEIGHTS[0]] * base
    relaxed[0] = jnp.where(solid, pops[0], rest)
    for q, o in PAIRS:
        along = None
        for a in range(3):
            c = LATTICE[q, a]
            if c == 1:
                along = speeds[a] if along is None else along + speeds[a]
            elif c == -1:
                along = -speeds[a] if along is None else along - speeds[a]
        even = part[WEIGHTS[q]] * (base + 4.5 * along * along)
        odd = part[WEIGHTS[q]] * (3.0 * along)
        relaxed[q] = jnp.where(solid, pops[o], pops[q] * keep + (even + odd))
        relaxed[o] = jnp.where(solid, pops[q], pops[o] * keep + (even - odd))
    factor = jnp.where(solid, 0.0, vel_scale / VOX_ROW)
    return relaxed, [s * factor for s in speeds]


def collide_all(source, g_of, out, vel_ref, tiles=range(3)):
    for x in range(2):
        for yt in tiles:
            for lt in range(2):
                rows, cols = pl.ds(8 * yt, 8), pl.ds(128 * lt, 128)
                pops = [source(q, x, rows, cols) for q in range(19)]
                relaxed, vel = collide(pops, g_of[x, rows, cols])
                for q in range(19):
                    out[q, x, rows, cols] = relaxed[q]
                if vel_ref is not None and yt < 2 and lt == 0:
                    for a in range(3):
                        vel_ref[a, x, rows, :] = vel[a]


def pack_x(out, xr_ref, xl_ref):
    lane = lanes()
    for ref, directions, x in ((xr_ref, PLUS_X, 1), (xl_ref, MINUS_X, 0)):
        extra = jnp.zeros((8, 128), jnp.float32)
        for i, q in enumerate(directions):
            for yt in range(3):
                j = 3 * i + yt
                ref[j] = out[q, x, pl.ds(8 * yt, 8), pl.ds(0, 128)]
                tile = out[q, x, pl.ds(8 * yt, 8), pl.ds(128, 128)]
                here = (lane >= 8 * j) & (lane < 8 * j + 8)
                extra = jnp.where(here, roll(tile, 4 + 8 * j, 1), extra)
        ref[15] = extra


STILL = [q for q in range(19) if LATTICE[q, 0] == 0]
DEEP = 14
DEEP_TILES = 38


def still_sums(pops):
    total = pops[0]
    for value in pops[1:]:
        total = total + value
    sums = [total]
    for a in (1, 2):
        plus = [p for p, q in zip(pops, STILL) if LATTICE[q, a] == 1]
        minus = [p for p, q in zip(pops, STILL) if LATTICE[q, a] == -1]
        sums.append(((plus[0] + plus[1]) + plus[2]) - ((minus[0] + minus[1]) + minus[2]))
    return sums


def pack_deep(ahead, going, g_ref, refs):
    lane, sub = lanes(), subs()
    for side, ref in enumerate(refs):
        x = 1 - side
        edges = [jnp.zeros((8, 128), jnp.float32)] * 3
        directions = (PLUS_X, MINUS_X)[side]

        def entries(yt, lt):
            at = (pl.ds(8 * yt, 8), pl.ds(128 * lt, 128))
            tiles = [going[side, i, at[0], at[1]] for i in range(5)]
            tiles += [ahead[q, x, at[0], at[1]] for q in directions]
            tiles += still_sums([ahead[q, x, at[0], at[1]] for q in STILL])
            return tiles + [g_ref[x, at[0], at[1]]]

        def edge(j, tile):
            at, k = divmod(j, 16)
            here = (lane >= 8 * k) & (lane < 8 * k + 8)
            edges[at] = jnp.where(here, roll(tile, 4 + 8 * k, 1), edges[at])

        for yt in range(2):
            for e, (inner, outer) in enumerate(zip(entries(yt, 0), entries(yt, 1))):
                ref[2 * e + yt] = inner
                edge(2 * e + yt, outer)
        halos = [entries(2, lt) for lt in range(2)]
        for e in range(0, DEEP, 2):
            pair = [jnp.where(sub < 4, roll(h[e], 2, 0), roll(h[e + 1], 6, 0)) for h in halos]
            ref[28 + e // 2] = pair[0]
            edge(28 + e // 2, pair[1])
        for at in range(3):
            ref[35 + at] = edges[at]


def take_deep(refs, deep):
    for side, ref in enumerate(refs):

        def edge(j):
            return roll(ref[35 + j // 16], -(8 * (j % 16) + 4), 1)

        for e in range(DEEP):
            back = -2 if e % 2 == 0 else -6
            for yt in range(2):
                deep[side, e, pl.ds(8 * yt, 8), pl.ds(0, 128)] = ref[2 * e + yt]
                deep[side, e, pl.ds(8 * yt, 8), pl.ds(128, 128)] = edge(2 * e + yt)
            deep[side, e, pl.ds(16, 8), pl.ds(0, 128)] = roll(ref[28 + e // 2], back, 0)
            deep[side, e, pl.ds(16, 8), pl.ds(128, 128)] = roll(edge(28 + e // 2), back, 0)


def collide_side(toward, away, sums, g, side):
    ahead, back = ((PLUS_X, MINUS_X), (MINUS_X, PLUS_X))[side]
    into, out_of = toward[0], away[0]
    for value in toward[1:]:
        into = into + value
    for value in away[1:]:
        out_of = out_of + value
    density = sums[0] + (into + out_of)
    flows = [into - out_of if side == 0 else out_of - into, sums[1], sums[2]]
    for directions, pops in ((ahead, toward), (back, away)):
        for q, value in zip(directions, pops):
            for a in (1, 2):
                if LATTICE[q, a] == 1:
                    flows[a] = flows[a] + value
                elif LATTICE[q, a] == -1:
                    flows[a] = flows[a] - value
    scale = 1.0 / (density * jnp.abs(g))
    speeds = [flow * scale for flow in flows]
    square = speeds[0] * speeds[0] + speeds[1] * speeds[1] + speeds[2] * speeds[2]
    keep = 1.0 - 1.0 / relax_time
    base = 1.0 - 1.5 * square
    solid = g < 0.0
    part = {w: density * (w / relax_time) for w in sorted({WEIGHTS[q] for q in ahead})}
    relaxed = []
    for q, value in zip(ahead, toward):
        along = None
        for a in range(3):
            c = LATTICE[q, a]
            if c == 1:
                along = speeds[a] if along is None else along + speeds[a]
            elif c == -1:
                along = -speeds[a] if along is None else along - speeds[a]
        moved = value * keep + part[WEIGHTS[q]] * ((base + 4.5 * along * along) + 3.0 * along)
        relaxed.append(jnp.where(solid, away[back.index(OPPOSITE[q])], moved))
    return relaxed


def inner_kernel(pops, g_in, left, right, out, g_ref, vel_ref, wide):
    lane = lanes()
    for f in range(FIELDS):
        ref = wide.at[f] if f < 19 else g_ref
        for x in range(2):
            for yt in range(2):
                rows = pl.ds(8 * yt, 8)
                own = pops[f, x, rows, :] if f < 19 else g_in[x, rows, :]
                at, k = divmod(f * 4 + x * 2 + yt, 32)
                tile = jnp.where(lane < 4, roll(right[at], -4 * k, 1), own)
                tile = jnp.where(lane >= 124, roll(left[at], 124 - 4 * k, 1), tile)
                ref[x, rows, pl.ds(0, 128)] = own
                ref[x, rows, pl.ds(128, 128)] = tile
    collide_all(lambda q, x, rows, cols: wide[q, x, rows, cols], g_ref, out, vel_ref, range(2))


def outer_kernel(out_in, g_in, y, cr, cl, out, g_ref, xr_ref, xl_ref, wide):
    lane, sub = lanes(), subs()
    for f in range(FIELDS):
        ref = wide.at[f] if f < 19 else g_ref
        pairs = []
        for i in range(2):
            own = y[FIELDS * i + f]
            tile = jnp.where(lane < 4, roll(cl[i], -4 * f, 1), own)
            pairs.append((own, jnp.where(lane >= 124, roll(cr[i], 124 - 4 * f, 1), tile)))
        high, low = pairs
        for lt in range(2):
            cols = pl.ds(128 * lt, 128)
            ref[0, pl.ds(16, 8), cols] = jnp.where(sub < 4, low[lt], roll(high[lt], 4, 0))
            ref[1, pl.ds(16, 8), cols] = jnp.where(sub < 4, roll(low[lt], 4, 0), high[lt])
    collide_all(lambda q, x, rows, cols: wide[q, x, rows, cols], g_ref, out, None, (2,))
    pack_x(out, xr_ref, xl_ref)


def unpack_x(xr, xl, side):
    for s, ref in enumerate((xr, xl)):
        for i in range(5):
            for yt in range(3):
                j = 3 * i + yt
                side[s, i, pl.ds(8 * yt, 8), pl.ds(0, 128)] = ref[j]
                side[s, i, pl.ds(8 * yt, 8), pl.ds(128, 128)] = roll(ref[15], -(8 * j + 4), 1)


def turned(value, q):
    return roll(roll(value, int(LATTICE[q, 1]), 0), int(LATTICE[q, 2]), 1)


def remote(q, x):
    if LATTICE[q, 0] == 1 and x == 0:
        return 0, PLUS_X.index(q)
    if LATTICE[q, 0] == -1 and x == 1:
        return 1, MINUS_X.index(q)
    return None


def local_kernel(prev, ahead):
    for q in range(19):
        for x in range(2):
            if remote(q, x) is None:
                ahead[q, x] = turned(prev[q, x - int(LATTICE[q, 0])], q)


def take_faces(xr, xl, side):
    unpack_x(xr, xl, side)
    for s, directions in enumerate((PLUS_X, MINUS_X)):
        for i, q in enumerate(directions):
            side[s, i] = turned(side[s, i], q)


def chooser(ahead, side):
    def pick(q, x, rows, cols):
        at = remote(q, x)
        return ahead[q, x, rows, cols] if at is None else side[at[0], at[1], rows, cols]

    return pick


def step_kernel(ahead_in, g_ref, xr, xl, rider, ahead, going, vel_ref, xr_ref, xl_ref, side, out):
    take_faces(xr, xl, side)
    collide_all(chooser(ahead_in, side), g_ref, out, vel_ref)
    local_kernel(out, ahead)
    for i in range(5):
        going[0, i] = turned(out[PLUS_X[i], 1], PLUS_X[i])
        going[1, i] = turned(out[MINUS_X[i], 0], MINUS_X[i])
    pack_deep(ahead, going, g_ref, (xr_ref, xl_ref))
    xr_ref[DEEP_TILES] = rider[...]
    xl_ref[DEEP_TILES] = rider[...]


def pair_kernel(ahead, going, g_ref, xr, xl, ahead_ref, side_ref, vel_ref, deep, out):
    take_deep((xr, xl), deep)

    def pick(q, x, rows, cols):
        at = remote(q, x)
        return ahead[q, x, rows, cols] if at is None else deep[at[0], at[1], rows, cols]

    collide_all(pick, g_ref, out, vel_ref)
    for side, directions in enumerate((PLUS_X, MINUS_X)):
        for yt in range(3):
            for lt in range(2):
                rows, cols = pl.ds(8 * yt, 8), pl.ds(128 * lt, 128)
                toward = [deep[side, 5 + i, rows, cols] for i in range(5)]
                away = [going[1 - side, i, rows, cols] for i in range(5)]
                sums = [deep[side, 10 + i, rows, cols] for i in range(3)]
                relaxed = collide_side(toward, away, sums, deep[side, 13, rows, cols], side)
                for i in range(5):
                    side_ref[side, i, rows, cols] = relaxed[i]
        for i, q in enumerate(directions):
            side_ref[side, i] = turned(side_ref[side, i], q)
    local_kernel(out, ahead_ref)


def end_step_kernel(ahead, g_ref, side, out, xr_ref, xl_ref):
    collide_all(chooser(ahead, side), g_ref, out, None)
    pack_x(out, xr_ref, xl_ref)


def last_kernel(prev, xr, xl, out, side):
    take_faces(xr, xl, side)
    for q in range(19):
        for x in range(2):
            at = remote(q, x)
            value = turned(prev[q, x - int(LATTICE[q, 0])], q) if at is None else side[at[0], at[1]]
            out[q, x] = value[:16, :128]


def split(value):
    big = value.astype(jnp.bfloat16).astype(jnp.float32)
    return big, value - big


def onehot_kernel(row_map, right):
    low_at = lax.broadcasted_iota(jnp.int32, (LOW, 128), 0)
    for x in range(2):
        for y in range(16):
            rows = row_map[x, pl.ds(y, 1), :]
            low = rows - (rows // LOW) * LOW
            cols = pl.ds(128 * (16 * x + y), 128)
            right[:, cols] = jnp.where(low_at == low, 1.0, 0.0).astype(jnp.bfloat16)


def times_onehot(left, right):
    return lax.dot_general(
        left[...], right[...], (((1,), (1,)), ((), ())), preferred_element_type=jnp.float32
    )


def restricted(vels, row_map, right, left):
    count = 3 * len(vels)
    highs = left.shape[0] // (2 * count)
    high_at = lax.broadcasted_iota(jnp.int32, (highs, 128), 0)
    for x in range(2):
        for y in range(16):
            cols = pl.ds(128 * (16 * x + y), 128)
            here = high_at == row_map[x, pl.ds(y, 1), :] // LOW
            for j in range(count):
                for i, part in enumerate(split(vels[j // 3][j % 3, x, pl.ds(y, 1), :])):
                    left[pl.ds(highs * (count * i + j), highs), cols] = jnp.where(here, part, 0.0).astype(jnp.bfloat16)
    both = times_onehot(left, right)
    half = count * highs
    return both[:half] + both[half:]


def early_kernel(v0, v1, row_map, right, out, left):
    highs = out.shape[0]
    both = restricted((v0, v1), row_map, right, left)
    for h in range(highs):
        for j in range(6):
            out[h, pl.ds(j, 1), :] = both[highs * j + h : highs * j + h + 1]
        out[h, pl.ds(6, 10), :] = jnp.zeros((10, LOW), jnp.float32)


def old_kernel(total_rows, basis, sigma, scaled_ref, tile_ref, work):
    scaled = basis[...] * sigma[...]
    scaled_ref[...] = scaled
    work[...] = jnp.zeros((32, 128), jnp.float32)
    work[:, pl.ds(0, 32)] = dot(scaled, scaled, 1) * (1.0 / total_rows)
    lane = lanes()
    tile = work[pl.ds(0, 8), :]
    for k in range(1, 4):
        here = (lane >= 32 * k) & (lane < 32 * k + 32)
        tile = jnp.where(here, roll(work[pl.ds(8 * k, 8), :], 32 * k, 1), tile)
    tile_ref[...] = tile


def dot(a, b, dim):
    return lax.dot_general(
        a,
        b,
        (((1,), (dim,)), ((), ())),
        precision=lax.Precision.HIGHEST,
        preferred_element_type=jnp.float32,
    )


def late_kernel(ahead, g_ref, side, v2, row_map, right, early, own, near_r, near_l, far, out, left, v3):
    pick = chooser(ahead, side)
    for x in range(2):
        for yt in range(2):
            rows, cols = pl.ds(8 * yt, 8), pl.ds(0, 128)
            g = g_ref[x, rows, cols]
            _, speeds = moments([pick(q, x, rows, cols) for q in range(19)], g)
            factor = jnp.where(g < 0.0, 0.0, vel_scale / VOX_ROW)
            for a in range(3):
                v3[a, x, rows, :] = speeds[a] * factor
    highs = out.shape[0]
    both = restricted((v2, v3), row_map, right, left)
    out[...] = early[...]
    old = (own[...] + far[...]) + (near_r[...] + near_l[...])
    for h in range(highs):
        for j in range(6):
            out[h, pl.ds(6 + j, 1), :] = both[highs * j + h : highs * j + h + 1]
        if h % 2 == 0:
            out[h, pl.ds(12, 4), pl.ds(0, 128)] = old[:4]
            out[h, pl.ds(12, 4), pl.ds(128, 128)] = old[4:]


def gram_kernel(total_rows, parts, scaled, snap_ref, tile_ref, out, aug):
    owners = parts.shape[0] // 32
    total = parts[pl.ds(0, 32), :]
    for o in range(1, owners):
        total = total + parts[pl.ds(32 * o, 32), :]
    tile_ref[pl.ds(0, 4), :] = total[12:16, :128]
    tile_ref[pl.ds(4, 4), :] = total[12:16, 128:]
    used = lax.broadcasted_iota(jnp.int32, (16, LOW), 0) < 12
    aug[pl.ds(0, 32), :] = scaled[...]
    aug[pl.ds(32, 16), pl.ds(0, LOW)] = jnp.where(used, total[:16], 0.0)
    aug[pl.ds(32, 16), pl.ds(LOW, LOW)] = jnp.where(used, total[16:], 0.0)
    aug[pl.ds(48, 80), :] = jnp.zeros((80, 2 * LOW), jnp.float32)
    snap = aug[pl.ds(32, 16), :]
    snap_ref[...] = snap
    product = dot(snap, aug[...], 1) * (1.0 / total_rows)
    lane = lanes()
    tail = jnp.where(lane < 120, roll(product[8:], 88, 1), roll(product[8:], 80, 1))
    packed = jnp.where(lane < 44, product[:8], jnp.where(lane < 88, roll(roll(product[:8], 4, 0), 44, 1), tail))
    twice = jnp.where(subs() < 4, packed, roll(packed, 4, 0))
    for d in range(out.shape[0] // 8):
        out[pl.ds(8 * d, 8), :] = twice


def eliminate(tiles, count):
    sub = subs()
    done = list(tiles)

    def spread(value, row):
        return jnp.broadcast_to(value[row : row + 1, :], (8, 128))

    for k in range(0, count, 2):
        t, r = divmod(k, 8)
        row0, row1 = spread(tiles[t], r), spread(tiles[t], r + 1)
        cols = {
            u: [jnp.broadcast_to(tiles[u][:, k + i : k + i + 1], (8, 128)) for i in range(2)]
            for u in range(t, len(tiles))
        }
        a, b, c = spread(cols[t][0], r), spread(cols[t][1], r), spread(cols[t][1], r + 1)
        inv = 1.0 / (a * c - b * b)
        part0 = (c * row0 - b * row1) * inv
        part1 = (a * row1 - b * row0) * inv
        ratio = b / a
        first = row0 * (1.0 / jnp.sqrt(a))
        second = (row1 - ratio * row0) * (1.0 / jnp.sqrt(c - ratio * b))
        done[t] = jnp.where(sub == r, first, jnp.where(sub == r + 1, second, done[t]))
        for u in range(t, len(tiles)):
            tiles[u] = tiles[u] - (cols[u][0] * part0 + cols[u][1] * part1)
    return [jnp.where((lanes() >= 64) | (lanes() >= sub + 8 * t), tile, 0.0) for t, tile in enumerate(done)]


def old_factor_kernel(tile, scaled, work, head_ref):
    lane, sub = lanes(), subs()
    tiles = []
    for k in range(4):
        own = jnp.where(lane < 32, roll(tile[...], -32 * k, 1), 0.0)
        tiles.append(own + jnp.where(lane == sub + 8 * k + 64, 1.0, 0.0))
    for k, value in enumerate(eliminate(tiles, 32)):
        work[pl.ds(8 * k, 8), :] = value
    head_ref[...] = dot(work[:, pl.ds(64, 32)], scaled[...], 0)


def factor_kernel(parts, factor, head, snap, basis_ref, tri_ref, work):
    lane, sub = lanes(), subs()
    sums = [parts[pl.ds(8 * d, 8), :] for d in range(parts.shape[0] // 8)]
    while len(sums) > 1:
        sums = [sums[i] + sums[i + 1] for i in range(0, len(sums), 2)]
    total = sums[0] + roll(sums[0], 4, 0)
    top = jnp.where(lane < 44, jnp.where(sub < 4, total, roll(total, -44, 1)), 0.0)
    low = jnp.where(lane < 32, roll(total, -88, 1), roll(total, -80, 1))
    work[pl.ds(0, 8), :] = top
    work[pl.ds(8, 8), :] = jnp.where((sub < 4) & (lane < 44), low, 0.0)
    work[pl.ds(8, 8), pl.ds(32, 8)] = top.T[40:48]
    cross = work[:, pl.ds(0, 32)]
    inner = work[:, pl.ds(32, 16)]
    inverse = factor[:, pl.ds(64, 32)]
    below = dot(cross, inverse, 1)
    rest = snap[...] - dot(below, head[...], 0)
    inner = inner - dot(below, below, 1)
    work[...] = jnp.zeros((16, 128), jnp.float32)
    work[:, pl.ds(0, 16)] = inner
    tiles = [work[pl.ds(8 * t, 8), :] + jnp.where(lane == sub + 8 * t + 64, 1.0, 0.0) for t in range(2)]
    for t, value in enumerate(eliminate(tiles, 12)):
        work[pl.ds(8 * t, 8), :] = value
    tri_ref[pl.ds(0, 32), pl.ds(0, 32)] = factor[:, pl.ds(0, 32)]
    tri_ref[pl.ds(0, 32), pl.ds(32, 12)] = dot(inverse, cross, 1)[:, :12]
    tri_ref[pl.ds(32, 12), pl.ds(0, 32)] = jnp.zeros((12, 32), jnp.float32)
    tri_ref[pl.ds(32, 12), pl.ds(32, 12)] = work[pl.ds(0, 12), pl.ds(0, 12)]
    basis_ref[pl.ds(0, 32), :] = head[...]
    basis_ref[pl.ds(32, 12), :] = dot(work[:, pl.ds(64, 16)], rest, 0)[:12]


def f32(*shape):
    return jax.ShapeDtypeStruct(shape, jnp.float32)


def vmem(*shape):
    return pltpu.VMEM(shape, jnp.float32)


def held(value):
    return pltpu.with_memory_space_constraint(value, pltpu.VMEM)


def call(kernel, outs, scratch=(), count=None, aliases=None, limit=16, space=pltpu.VMEM):
    specs = [pl.BlockSpec(memory_space=space) for _ in range(count)]
    many = isinstance(outs, (tuple, list))
    out_specs = [pl.BlockSpec(memory_space=pltpu.VMEM)] * len(outs) if many else pl.BlockSpec(memory_space=pltpu.VMEM)
    return pl.pallas_call(
        kernel, out_shape=outs, in_specs=specs, out_specs=out_specs, scratch_shapes=list(scratch),
        input_output_aliases=aliases or {},
        compiler_params=pltpu.CompilerParams(vmem_limit_bytes=limit * 2**20),
    )


def shift(value, axis, step):
    count = lax.axis_size(axis)
    return lax.ppermute(value, axis, [(i, (i + step) % count) for i in range(count)])


def shift_both(value, step_y, step_z):
    ny, nz = lax.axis_size("gy"), lax.axis_size("gz")
    pairs = [
        (y * nz + z, (y + step_y) % ny * nz + (z + step_z) % nz) for y in range(ny) for z in range(nz)
    ]
    return lax.ppermute(value, ("gy", "gz"), pairs)


def across(value, step_z):
    if lax.axis_size("gy") == 2:
        return shift_both(value, 1, step_z)
    half = value.shape[0] // 2
    return jnp.concatenate([shift_both(value[:half], 1, step_z), shift_both(value[half:], -1, step_z)], 0)


def on_device(pop_ratio, solid_flags, class_ids, drag_table, row_map, old_basis, old_sigma):
    slab = ("gy", "gz")
    everyone = ("gx", "gy", "gz")
    owners = lax.axis_size(slab)
    devices = lax.axis_size(everyone)
    rows_local = old_basis.shape[1]
    highs = owners * rows_local // LOW
    cells = 4096
    tile = (8, 128)

    pops, g, zr, zl, y, cr, cl = call(
        init_kernel,
        (vmem(19, 2, 16, 128), vmem(2, 16, 128), vmem(3, *tile), vmem(3, *tile))
        + (vmem(2 * FIELDS, *tile), vmem(2, *tile), vmem(2, *tile)),
        (
            pltpu.SMEM(drag_table.shape, jnp.float32),
            pltpu.VMEM((19, 2, 16, 128), jnp.float32),
            pltpu.VMEM((2, 16, 128), jnp.int32),
            pltpu.VMEM((2, 16, 128), jnp.int32),
            pltpu.SemaphoreType.DMA((4,)),
        ),
        count=4,
        space=pltpu.HBM,
    )(*(pltpu.with_memory_space_constraint(v, pltpu.HBM) for v in (drag_table, pop_ratio, solid_flags, class_ids)))
    y = across(y, 0)
    left, right = shift(zr, "gz", 1), shift(zl, "gz", -1)
    cr, cl = across(cr, 1), across(cl, -1)

    wide = pltpu.VMEM((19, 2, 24, 256), jnp.float32)
    side = pltpu.VMEM((2, 5, 24, 256), jnp.float32)
    big, wall, vel, face = vmem(19, 2, 24, 256), vmem(2, 24, 256), vmem(3, 2, 16, 128), vmem(16, *tile)
    loaded, sides = vmem(DEEP_TILES + 1, *tile), vmem(2, 5, 24, 256)
    relaxed, g_wide, v0 = call(inner_kernel, (big, wall, vel), (wide,), count=4)(
        *map(held, (pops, g, left, right))
    )
    relaxed, g_wide, xr, xl = call(
        outer_kernel, (big, wall, face, face), (wide,), count=5, aliases={0: 0, 1: 1}
    )(*map(held, (relaxed, g_wide, y, cr, cl)))
    old, own = call(
        functools.partial(old_kernel, float(rows_local * devices)),
        (vmem(32, rows_local), vmem(*tile)),
        (pltpu.VMEM((32, 128), jnp.float32),),
        count=2,
    )(old_basis, old_sigma[:, None])
    ring = lax.axis_size("gx") == 4
    if not ring:
        own = lax.psum(own, "gx")
    none = jnp.zeros(tile, jnp.float32)
    onehot = call(onehot_kernel, pltpu.VMEM((LOW, cells), jnp.bfloat16), count=1)(row_map)
    xr, xl = shift(xr, "gx", 1), shift(xl, "gx", -1)
    ahead = call(local_kernel, big, count=1)(held(relaxed))
    ahead, going, v1, xr, xl = call(step_kernel, (big, sides, vel, loaded, loaded), (side, wide), count=5)(
        *map(held, (ahead, g_wide, xr, xl, own))
    )
    xr, xl = shift(xr, "gx", 1), shift(xl, "gx", -1)
    got = [none] * 3
    if ring:
        got = [xr[DEEP_TILES], xl[DEEP_TILES], shift(own, "gx", 2)]
    ahead, faces, v2 = call(
        pair_kernel, (big, sides, vel), (pltpu.VMEM((2, DEEP, 24, 256), jnp.float32), wide), count=5
    )(*map(held, (ahead, going, g_wide, xr, xl)))
    state = tuple(map(held, (ahead, g_wide, faces)))
    relaxed, xr, xl = call(end_step_kernel, (big, face, face), count=3)(*state)
    xr, xl = shift(xr, "gx", 1), shift(xl, "gx", -1)

    lefts = pltpu.VMEM((12 * highs, cells), jnp.bfloat16)
    early = call(early_kernel, vmem(highs, 16, LOW), (lefts,), count=4, limit=12 + highs // 2)(
        held(v0), held(v1), row_map, held(onehot)
    )
    term = call(
        late_kernel,
        f32(highs, 16, LOW),
        (lefts, pltpu.VMEM((3, 2, 16, 128), jnp.float32)),
        count=11,
        limit=12 + highs // 2,
    )(*state, held(v2), row_map, *map(held, (onehot, early, own, *got)))
    parts = lax.all_to_all(term.reshape(16 * highs, LOW), slab, 0, 0, tiled=True)
    snap, old_tile, gram = call(
        functools.partial(gram_kernel, float(rows_local * devices)),
        (vmem(16, rows_local), vmem(*tile), f32(4 * devices, 128)),
        (pltpu.VMEM((128, rows_local), jnp.float32),),
        count=2,
    )(held(parts), held(old))
    grams = lax.all_to_all(gram, everyone, 0, 0, tiled=True)
    factor, head = call(old_factor_kernel, (vmem(32, 128), vmem(32, rows_local)), count=2)(held(old_tile), held(old))
    new_basis, upper = call(
        factor_kernel, (f32(44, rows_local), f32(44, 44)), (pltpu.VMEM((16, 128), jnp.float32),), count=4
    )(*map(held, (grams, factor, head, snap)))
    populations = call(last_kernel, f32(19, 2, 16, 128), (side,), count=3)(*map(held, (relaxed, xr, xl)))
    return (populations, new_basis, upper)


def solution(mesh):
    in_specs = (
        P(None, "gx", "gy", "gz"),
        P("gx", "gy", "gz"),
        P("gx", "gy", "gz"),
        P(),
        P("gx", "gy", "gz"),
        P(None, ("gx", "gy", "gz")),
        P(),
    )
    out_specs = (P(None, "gx", "gy", "gz"), P(None, ("gx", "gy", "gz")), P())

    return jax.shard_map(on_device, mesh=mesh, in_specs=in_specs, out_specs=out_specs, check_vma=False)
```

```python
import functools

import jax
import jax.numpy as jnp
import numpy as np
from jax import lax
from jax.experimental import pallas as pl
from jax.experimental.pallas import tpu as pltpu
from jax.sharding import PartitionSpec as P


VOX_ROW = 8
LATTICE = np.array(
    [
        [0, 0, 0],
        [1, 0, 0],
        [-1, 0, 0],
        [0, 1, 0],
        [0, -1, 0],
        [0, 0, 1],
        [0, 0, -1],
        [1, 1, 0],
        [-1, -1, 0],
        [1, -1, 0],
        [-1, 1, 0],
        [1, 0, 1],
        [-1, 0, -1],
        [1, 0, -1],
        [-1, 0, 1],
        [0, 1, 1],
        [0, -1, -1],
        [0, 1, -1],
        [0, -1, 1],
    ]
)
OPPOSITE = [0, 2, 1, 4, 3, 6, 5, 8, 7, 10, 9, 12, 11, 14, 13, 16, 15, 18, 17]
WEIGHTS = [1.0 / 3.0] + [1.0 / 18.0] * 6 + [1.0 / 36.0] * 12
PAIRS = [(q, OPPOSITE[q]) for q in range(1, 19) if q < OPPOSITE[q]]
PLUS_X = [q for q in range(19) if LATTICE[q, 0] == 1]
MINUS_X = [q for q in range(19) if LATTICE[q, 0] == -1]
relax_time = 0.9
vel_scale = 16.0

FIELDS = 20
LOW = 256


def lanes(shape=(8, 128)):
    return lax.broadcasted_iota(jnp.int32, shape, len(shape) - 1)


def subs(shape=(8, 128)):
    return lax.broadcasted_iota(jnp.int32, shape, len(shape) - 2)


def roll(value, shift, axis):
    size = value.shape[axis]
    shift = shift % size
    return value if shift == 0 else pltpu.roll(value, shift, axis)


def init_kernel(
    table_hbm, ratio_hbm, solid_hbm, cls_hbm,
    pops_ref, g_ref, zr_ref, zl_ref, y_ref, cr_ref, cl_ref,
    table, ratio, solid, cls, sems,
):
    pairs = ((ratio_hbm, ratio), (table_hbm, table), (solid_hbm, solid), (cls_hbm, cls))
    copies = [pltpu.make_async_copy(src, dst, sems.at[i]) for i, (src, dst) in enumerate(pairs)]
    for copy in copies:
        copy.start()
    for copy in copies:
        copy.wait()
    lane, sub = lanes(), subs()
    blank = jnp.zeros((8, 128), jnp.float32)
    zr, zl = [blank] * 3, [blank] * 3
    cr, cl = [blank] * 2, [blank] * 2
    for f in range(FIELDS):
        tiles = {}
        for x in range(2):
            for yt in range(2):
                rows = pl.ds(8 * yt, 8)
                if f < 19:
                    tile = ratio[f, x, rows, :] * WEIGHTS[f]
                    pops_ref[f, x, rows, :] = tile
                else:
                    ids = cls[x, rows, :]
                    drag = jnp.zeros((8, 128), jnp.float32)
                    for c in range(table.shape[0]):
                        drag = jnp.where(ids == c, table[c], drag)
                    tile = jnp.where(solid[x, rows, :] == 1, -1.0, 1.0 + 0.5 * drag)
                    g_ref[x, rows, :] = tile
                tiles[x, yt] = tile
                at, k = divmod(f * 4 + x * 2 + yt, 32)
                here = (lane >= 4 * k) & (lane < 4 * k + 4)
                zr[at] = jnp.where(here, roll(tile, 4 * k - 124, 1), zr[at])
                zl[at] = jnp.where(here, roll(tile, 4 * k, 1), zl[at])
        up = jnp.where(sub < 4, roll(tiles[0, 1], 4, 0), tiles[1, 1])
        down = jnp.where(sub < 4, tiles[0, 0], roll(tiles[1, 0], 4, 0))
        y_ref[f] = up
        y_ref[FIELDS + f] = down
        here = (lane >= 4 * f) & (lane < 4 * f + 4)
        for i, tile in enumerate((up, down)):
            cr[i] = jnp.where(here, roll(tile, 4 * f - 124, 1), cr[i])
            cl[i] = jnp.where(here, roll(tile, 4 * f, 1), cl[i])
    for at in range(3):
        zr_ref[at] = zr[at]
        zl_ref[at] = zl[at]
    for at in range(2):
        cr_ref[at] = cr[at]
        cl_ref[at] = cl[at]


def moments(pops, g):
    density = pops[0]
    for q in range(1, 19):
        density = density + pops[q]
    scale = 1.0 / (density * jnp.abs(g))
    speeds = []
    for a in range(3):
        total = None
        for q in range(19):
            c = LATTICE[q, a]
            if c == 1:
                total = pops[q] if total is None else total + pops[q]
            elif c == -1:
                total = total - pops[q]
        speeds.append(total * scale)
    return density, speeds


def collide(pops, g):
    density, speeds = moments(pops, g)
    square = speeds[0] * speeds[0] + speeds[1] * speeds[1] + speeds[2] * speeds[2]
    solid = g < 0.0
    keep = 1.0 - 1.0 / relax_time
    base = 1.0 - 1.5 * square
    part = {w: density * (w / relax_time) for w in sorted(set(WEIGHTS))}
    relaxed = [None] * 19
    rest = pops[0] * keep + part[WEIGHTS[0]] * base
    relaxed[0] = jnp.where(solid, pops[0], rest)
    for q, o in PAIRS:
        along = None
        for a in range(3):
            c = LATTICE[q, a]
            if c == 1:
                along = speeds[a] if along is None else along + speeds[a]
            elif c == -1:
                along = -speeds[a] if along is None else along - speeds[a]
        even = part[WEIGHTS[q]] * (base + 4.5 * along * along)
        odd = part[WEIGHTS[q]] * (3.0 * along)
        relaxed[q] = jnp.where(solid, pops[o], pops[q] * keep + (even + odd))
        relaxed[o] = jnp.where(solid, pops[q], pops[o] * keep + (even - odd))
    factor = jnp.where(solid, 0.0, vel_scale / VOX_ROW)
    return relaxed, [s * factor for s in speeds]


def collide_all(source, g_of, out, vel_ref, tiles=range(3)):
    for x in range(2):
        for yt in tiles:
            for lt in range(2):
                rows, cols = pl.ds(8 * yt, 8), pl.ds(128 * lt, 128)
                pops = [source(q, x, rows, cols) for q in range(19)]
                relaxed, vel = collide(pops, g_of[x, rows, cols])
                for q in range(19):
                    out[q, x, rows, cols] = relaxed[q]
                if vel_ref is not None and yt < 2 and lt == 0:
                    for a in range(3):
                        vel_ref[a, x, rows, :] = vel[a]


def pack_x(out, xr_ref, xl_ref):
    lane = lanes()
    for ref, directions, x in ((xr_ref, PLUS_X, 1), (xl_ref, MINUS_X, 0)):
        extra = jnp.zeros((8, 128), jnp.float32)
        for i, q in enumerate(directions):
            for yt in range(3):
                j = 3 * i + yt
                ref[j] = out[q, x, pl.ds(8 * yt, 8), pl.ds(0, 128)]
                tile = out[q, x, pl.ds(8 * yt, 8), pl.ds(128, 128)]
                here = (lane >= 8 * j) & (lane < 8 * j + 8)
                extra = jnp.where(here, roll(tile, 4 + 8 * j, 1), extra)
        ref[15] = extra


STILL = [q for q in range(19) if LATTICE[q, 0] == 0]
DEEP = 14
DEEP_TILES = 38


def still_sums(pops):
    total = pops[0]
    for value in pops[1:]:
        total = total + value
    sums = [total]
    for a in (1, 2):
        plus = [p for p, q in zip(pops, STILL) if LATTICE[q, a] == 1]
        minus = [p for p, q in zip(pops, STILL) if LATTICE[q, a] == -1]
        sums.append(((plus[0] + plus[1]) + plus[2]) - ((minus[0] + minus[1]) + minus[2]))
    return sums


def pack_deep(ahead, going, g_ref, refs):
    lane, sub = lanes(), subs()
    for side, ref in enumerate(refs):
        x = 1 - side
        edges = [jnp.zeros((8, 128), jnp.float32)] * 3
        directions = (PLUS_X, MINUS_X)[side]

        def entries(yt, lt):
            at = (pl.ds(8 * yt, 8), pl.ds(128 * lt, 128))
            tiles = [going[side, i, at[0], at[1]] for i in range(5)]
            tiles += [ahead[q, x, at[0], at[1]] for q in directions]
            tiles += still_sums([ahead[q, x, at[0], at[1]] for q in STILL])
            return tiles + [g_ref[x, at[0], at[1]]]

        def edge(j, tile):
            at, k = divmod(j, 16)
            here = (lane >= 8 * k) & (lane < 8 * k + 8)
            edges[at] = jnp.where(here, roll(tile, 4 + 8 * k, 1), edges[at])

        for yt in range(2):
            for e, (inner, outer) in enumerate(zip(entries(yt, 0), entries(yt, 1))):
                ref[2 * e + yt] = inner
                edge(2 * e + yt, outer)
        halos = [entries(2, lt) for lt in range(2)]
        for e in range(0, DEEP, 2):
            pair = [jnp.where(sub < 4, roll(h[e], 2, 0), roll(h[e + 1], 6, 0)) for h in halos]
            ref[28 + e // 2] = pair[0]
            edge(28 + e // 2, pair[1])
        for at in range(3):
            ref[35 + at] = edges[at]


def take_deep(refs, deep):
    for side, ref in enumerate(refs):

        def edge(j):
            return roll(ref[35 + j // 16], -(8 * (j % 16) + 4), 1)

        for e in range(DEEP):
            back = -2 if e % 2 == 0 else -6
            for yt in range(2):
                deep[side, e, pl.ds(8 * yt, 8), pl.ds(0, 128)] = ref[2 * e + yt]
                deep[side, e, pl.ds(8 * yt, 8), pl.ds(128, 128)] = edge(2 * e + yt)
            deep[side, e, pl.ds(16, 8), pl.ds(0, 128)] = roll(ref[28 + e // 2], back, 0)
            deep[side, e, pl.ds(16, 8), pl.ds(128, 128)] = roll(edge(28 + e // 2), back, 0)


def collide_side(toward, away, sums, g, side):
    ahead, back = ((PLUS_X, MINUS_X), (MINUS_X, PLUS_X))[side]
    into, out_of = toward[0], away[0]
    for value in toward[1:]:
        into = into + value
    for value in away[1:]:
        out_of = out_of + value
    density = sums[0] + (into + out_of)
    flows = [into - out_of if side == 0 else out_of - into, sums[1], sums[2]]
    for directions, pops in ((ahead, toward), (back, away)):
        for q, value in zip(directions, pops):
            for a in (1, 2):
                if LATTICE[q, a] == 1:
                    flows[a] = flows[a] + value
                elif LATTICE[q, a] == -1:
                    flows[a] = flows[a] - value
    scale = 1.0 / (density * jnp.abs(g))
    speeds = [flow * scale for flow in flows]
    square = speeds[0] * speeds[0] + speeds[1] * speeds[1] + speeds[2] * speeds[2]
    keep = 1.0 - 1.0 / relax_time
    base = 1.0 - 1.5 * square
    solid = g < 0.0
    part = {w: density * (w / relax_time) for w in sorted({WEIGHTS[q] for q in ahead})}
    relaxed = []
    for q, value in zip(ahead, toward):
        along = None
        for a in range(3):
            c = LATTICE[q, a]
            if c == 1:
                along = speeds[a] if along is None else along + speeds[a]
            elif c == -1:
                along = -speeds[a] if along is None else along - speeds[a]
        moved = value * keep + part[WEIGHTS[q]] * ((base + 4.5 * along * along) + 3.0 * along)
        relaxed.append(jnp.where(solid, away[back.index(OPPOSITE[q])], moved))
    return relaxed


def inner_kernel(pops, g_in, left, right, out, g_ref, vel_ref, wide):
    lane = lanes()
    for f in range(FIELDS):
        ref = wide.at[f] if f < 19 else g_ref
        for x in range(2):
            for yt in range(2):
                rows = pl.ds(8 * yt, 8)
                own = pops[f, x, rows, :] if f < 19 else g_in[x, rows, :]
                at, k = divmod(f * 4 + x * 2 + yt, 32)
                tile = jnp.where(lane < 4, roll(right[at], -4 * k, 1), own)
                tile = jnp.where(lane >= 124, roll(left[at], 124 - 4 * k, 1), tile)
                ref[x, rows, pl.ds(0, 128)] = own
                ref[x, rows, pl.ds(128, 128)] = tile
    collide_all(lambda q, x, rows, cols: wide[q, x, rows, cols], g_ref, out, vel_ref, range(2))


def outer_kernel(out_in, g_in, y, cr, cl, out, g_ref, xr_ref, xl_ref, wide):
    lane, sub = lanes(), subs()
    for f in range(FIELDS):
        ref = wide.at[f] if f < 19 else g_ref
        pairs = []
        for i in range(2):
            own = y[FIELDS * i + f]
            tile = jnp.where(lane < 4, roll(cl[i], -4 * f, 1), own)
            pairs.append((own, jnp.where(lane >= 124, roll(cr[i], 124 - 4 * f, 1), tile)))
        high, low = pairs
        for lt in range(2):
            cols = pl.ds(128 * lt, 128)
            ref[0, pl.ds(16, 8), cols] = jnp.where(sub < 4, low[lt], roll(high[lt], 4, 0))
            ref[1, pl.ds(16, 8), cols] = jnp.where(sub < 4, roll(low[lt], 4, 0), high[lt])
    collide_all(lambda q, x, rows, cols: wide[q, x, rows, cols], g_ref, out, None, (2,))
    pack_x(out, xr_ref, xl_ref)


def unpack_x(xr, xl, side):
    for s, ref in enumerate((xr, xl)):
        for i in range(5):
            for yt in range(3):
                j = 3 * i + yt
                side[s, i, pl.ds(8 * yt, 8), pl.ds(0, 128)] = ref[j]
                side[s, i, pl.ds(8 * yt, 8), pl.ds(128, 128)] = roll(ref[15], -(8 * j + 4), 1)


def turned(value, q):
    return roll(roll(value, int(LATTICE[q, 1]), 0), int(LATTICE[q, 2]), 1)


def remote(q, x):
    if LATTICE[q, 0] == 1 and x == 0:
        return 0, PLUS_X.index(q)
    if LATTICE[q, 0] == -1 and x == 1:
        return 1, MINUS_X.index(q)
    return None


def local_kernel(prev, ahead):
    for q in range(19):
        for x in range(2):
            if remote(q, x) is None:
                ahead[q, x] = turned(prev[q, x - int(LATTICE[q, 0])], q)


def take_faces(xr, xl, side):
    unpack_x(xr, xl, side)
    for s, directions in enumerate((PLUS_X, MINUS_X)):
        for i, q in enumerate(directions):
            side[s, i] = turned(side[s, i], q)


def chooser(ahead, side):
    def pick(q, x, rows, cols):
        at = remote(q, x)
        return ahead[q, x, rows, cols] if at is None else side[at[0], at[1], rows, cols]

    return pick


def step_kernel(ahead_in, g_ref, xr, xl, ahead, going, vel_ref, xr_ref, xl_ref, side, out):
    take_faces(xr, xl, side)
    collide_all(chooser(ahead_in, side), g_ref, out, vel_ref)
    local_kernel(out, ahead)
    for i in range(5):
        going[0, i] = turned(out[PLUS_X[i], 1], PLUS_X[i])
        going[1, i] = turned(out[MINUS_X[i], 0], MINUS_X[i])
    pack_deep(ahead, going, g_ref, (xr_ref, xl_ref))


def pair_kernel(ahead, going, g_ref, xr, xl, ahead_ref, side_ref, vel_ref, deep, out):
    take_deep((xr, xl), deep)

    def pick(q, x, rows, cols):
        at = remote(q, x)
        return ahead[q, x, rows, cols] if at is None else deep[at[0], at[1], rows, cols]

    collide_all(pick, g_ref, out, vel_ref)
    for side, directions in enumerate((PLUS_X, MINUS_X)):
        for yt in range(3):
            for lt in range(2):
                rows, cols = pl.ds(8 * yt, 8), pl.ds(128 * lt, 128)
                toward = [deep[side, 5 + i, rows, cols] for i in range(5)]
                away = [going[1 - side, i, rows, cols] for i in range(5)]
                sums = [deep[side, 10 + i, rows, cols] for i in range(3)]
                relaxed = collide_side(toward, away, sums, deep[side, 13, rows, cols], side)
                for i in range(5):
                    side_ref[side, i, rows, cols] = relaxed[i]
        for i, q in enumerate(directions):
            side_ref[side, i] = turned(side_ref[side, i], q)
    local_kernel(out, ahead_ref)


def end_step_kernel(ahead, g_ref, side, rider, out, xr_ref, xl_ref):
    collide_all(chooser(ahead, side), g_ref, out, None)
    for ref, directions, x in ((xr_ref, PLUS_X, 1), (xl_ref, MINUS_X, 0)):
        for i, q in enumerate(directions):
            value = turned(out[q, x], q)
            for yt in range(2):
                ref[2 * i + yt] = value[8 * yt : 8 * yt + 8, :128]
        ref[10] = rider[...]


def last_kernel(prev, xr, xl, out):
    for q in range(19):
        for x in range(2):
            at = remote(q, x)
            if at is None:
                out[q, x] = turned(prev[q, x - int(LATTICE[q, 0])], q)[:16, :128]
            else:
                for yt in range(2):
                    out[q, x, pl.ds(8 * yt, 8), :] = (xr, xl)[at[0]][2 * at[1] + yt]


def split(value):
    big = value.astype(jnp.bfloat16).astype(jnp.float32)
    return big, value - big


def onehot_kernel(row_map, right):
    low_at = lax.broadcasted_iota(jnp.int32, (LOW, 128), 0)
    for x in range(2):
        for y in range(16):
            rows = row_map[x, pl.ds(y, 1), :]
            low = rows - (rows // LOW) * LOW
            cols = pl.ds(128 * (16 * x + y), 128)
            right[:, cols] = jnp.where(low_at == low, 1.0, 0.0).astype(jnp.bfloat16)


def times_onehot(left, right):
    return lax.dot_general(
        left[...], right[...], (((1,), (1,)), ((), ())), preferred_element_type=jnp.float32
    )


def restricted(vels, row_map, right, left):
    count = 3 * len(vels)
    highs = left.shape[0] // (2 * count)
    high_at = lax.broadcasted_iota(jnp.int32, (highs, 128), 0)
    for x in range(2):
        for y in range(16):
            cols = pl.ds(128 * (16 * x + y), 128)
            here = high_at == row_map[x, pl.ds(y, 1), :] // LOW
            for j in range(count):
                for i, part in enumerate(split(vels[j // 3][j % 3, x, pl.ds(y, 1), :])):
                    left[pl.ds(highs * (count * i + j), highs), cols] = jnp.where(here, part, 0.0).astype(jnp.bfloat16)
    both = times_onehot(left, right)
    half = count * highs
    return both[:half] + both[half:]


def early_kernel(v0, v1, row_map, right, out, left):
    highs = out.shape[0] // 12
    both = restricted((v0, v1), row_map, right, left)
    for h in range(highs):
        for j in range(6):
            out[pl.ds(12 * h + j, 1), :] = both[highs * j + h : highs * j + h + 1]
            out[pl.ds(12 * h + 6 + j, 1), :] = jnp.zeros((1, LOW), jnp.float32)


def old_kernel(total_rows, basis, sigma, scaled_ref, tile_ref, work):
    scaled = basis[...] * sigma[...]
    scaled_ref[...] = scaled
    work[...] = jnp.zeros((32, 128), jnp.float32)
    work[:, pl.ds(0, 32)] = dot(scaled, scaled, 1) * (1.0 / total_rows)
    lane = lanes()
    tile = work[pl.ds(0, 8), :]
    for k in range(1, 4):
        here = (lane >= 32 * k) & (lane < 32 * k + 32)
        tile = jnp.where(here, roll(work[pl.ds(8 * k, 8), :], 32 * k, 1), tile)
    tile_ref[...] = tile


def dot(a, b, dim):
    return lax.dot_general(
        a,
        b,
        (((1,), (dim,)), ((), ())),
        precision=lax.Precision.HIGHEST,
        preferred_element_type=jnp.float32,
    )


def late_kernel(ahead, g_ref, side, v2, row_map, right, early, out, left, v3):
    pick = chooser(ahead, side)
    for x in range(2):
        for yt in range(2):
            rows, cols = pl.ds(8 * yt, 8), pl.ds(0, 128)
            g = g_ref[x, rows, cols]
            _, speeds = moments([pick(q, x, rows, cols) for q in range(19)], g)
            factor = jnp.where(g < 0.0, 0.0, vel_scale / VOX_ROW)
            for a in range(3):
                v3[a, x, rows, :] = speeds[a] * factor
    highs = out.shape[0] // 12
    both = restricted((v2, v3), row_map, right, left)
    out[...] = early[...]
    for h in range(highs):
        for j in range(6):
            out[pl.ds(12 * h + 6 + j, 1), :] = both[highs * j + h : highs * j + h + 1]


def gram_kernel(total_rows, parts, scaled, snap_ref, out, aug):
    owners = parts.shape[0] // 24
    total = parts[pl.ds(0, 24), :]
    for o in range(1, owners):
        total = total + parts[pl.ds(24 * o, 24), :]
    aug[pl.ds(0, 32), :] = scaled[...]
    aug[pl.ds(40, 88), :] = jnp.zeros((88, 2 * LOW), jnp.float32)
    aug[pl.ds(32, 12), pl.ds(0, LOW)] = total[:12]
    aug[pl.ds(32, 12), pl.ds(LOW, LOW)] = total[12:]
    snap = aug[pl.ds(32, 16), :]
    snap_ref[...] = snap
    product = dot(snap, aug[...], 1) * (1.0 / total_rows)
    lane = lanes()
    tail = jnp.where(lane < 120, roll(product[8:], 88, 1), roll(product[8:], 80, 1))
    packed = jnp.where(lane < 44, product[:8], jnp.where(lane < 88, roll(roll(product[:8], 4, 0), 44, 1), tail))
    twice = jnp.where(subs() < 4, packed, roll(packed, 4, 0))
    for d in range(out.shape[0] // 8):
        out[pl.ds(8 * d, 8), :] = twice


def eliminate(tiles, count):
    sub = subs()
    done = list(tiles)

    def spread(value, row):
        return jnp.broadcast_to(value[row : row + 1, :], (8, 128))

    for k in range(0, count, 2):
        t, r = divmod(k, 8)
        row0, row1 = spread(tiles[t], r), spread(tiles[t], r + 1)
        cols = {
            u: [jnp.broadcast_to(tiles[u][:, k + i : k + i + 1], (8, 128)) for i in range(2)]
            for u in range(t, len(tiles))
        }
        a, b, c = spread(cols[t][0], r), spread(cols[t][1], r), spread(cols[t][1], r + 1)
        inv = 1.0 / (a * c - b * b)
        part0 = (c * row0 - b * row1) * inv
        part1 = (a * row1 - b * row0) * inv
        ratio = b / a
        first = row0 * (1.0 / jnp.sqrt(a))
        second = (row1 - ratio * row0) * (1.0 / jnp.sqrt(c - ratio * b))
        done[t] = jnp.where(sub == r, first, jnp.where(sub == r + 1, second, done[t]))
        for u in range(t, len(tiles)):
            tiles[u] = tiles[u] - (cols[u][0] * part0 + cols[u][1] * part1)
    return [jnp.where((lanes() >= 64) | (lanes() >= sub + 8 * t), tile, 0.0) for t, tile in enumerate(done)]


def old_factor_kernel(tile, scaled, work, head_ref):
    lane, sub = lanes(), subs()
    tiles = []
    for k in range(4):
        own = jnp.where(lane < 32, roll(tile[...], -32 * k, 1), 0.0)
        tiles.append(own + jnp.where(lane == sub + 8 * k + 64, 1.0, 0.0))
    for k, value in enumerate(eliminate(tiles, 32)):
        work[pl.ds(8 * k, 8), :] = value
    head_ref[...] = dot(work[:, pl.ds(64, 32)], scaled[...], 0)


def factor_kernel(parts, factor, head, snap, basis_ref, tri_ref, work):
    lane, sub = lanes(), subs()
    sums = [parts[pl.ds(8 * d, 8), :] for d in range(parts.shape[0] // 8)]
    while len(sums) > 1:
        sums = [sums[i] + sums[i + 1] for i in range(0, len(sums), 2)]
    total = sums[0] + roll(sums[0], 4, 0)
    top = jnp.where(lane < 44, jnp.where(sub < 4, total, roll(total, -44, 1)), 0.0)
    low = jnp.where(lane < 32, roll(total, -88, 1), roll(total, -80, 1))
    work[pl.ds(0, 8), :] = top
    work[pl.ds(8, 8), :] = jnp.where((sub < 4) & (lane < 44), low, 0.0)
    work[pl.ds(8, 8), pl.ds(32, 8)] = top.T[40:48]
    cross = work[:, pl.ds(0, 32)]
    inner = work[:, pl.ds(32, 16)]
    inverse = factor[:, pl.ds(64, 32)]
    below = dot(cross, inverse, 1)
    rest = snap[...] - dot(below, head[...], 0)
    inner = inner - dot(below, below, 1)
    work[...] = jnp.zeros((16, 128), jnp.float32)
    work[:, pl.ds(0, 16)] = inner
    tiles = [work[pl.ds(8 * t, 8), :] + jnp.where(lane == sub + 8 * t + 64, 1.0, 0.0) for t in range(2)]
    for t, value in enumerate(eliminate(tiles, 12)):
        work[pl.ds(8 * t, 8), :] = value
    tri_ref[pl.ds(0, 32), pl.ds(0, 32)] = factor[:, pl.ds(0, 32)]
    tri_ref[pl.ds(0, 32), pl.ds(32, 12)] = dot(inverse, cross, 1)[:, :12]
    tri_ref[pl.ds(32, 12), pl.ds(0, 32)] = jnp.zeros((12, 32), jnp.float32)
    tri_ref[pl.ds(32, 12), pl.ds(32, 12)] = work[pl.ds(0, 12), pl.ds(0, 12)]
    basis_ref[pl.ds(0, 32), :] = head[...]
    basis_ref[pl.ds(32, 12), :] = dot(work[:, pl.ds(64, 16)], rest, 0)[:12]


def f32(*shape):
    return jax.ShapeDtypeStruct(shape, jnp.float32)


def vmem(*shape):
    return pltpu.VMEM(shape, jnp.float32)


def held(value):
    return pltpu.with_memory_space_constraint(value, pltpu.VMEM)


def call(kernel, outs, scratch=(), count=None, aliases=None, limit=16, space=pltpu.VMEM):
    specs = [pl.BlockSpec(memory_space=space) for _ in range(count)]
    many = isinstance(outs, (tuple, list))
    out_specs = [pl.BlockSpec(memory_space=pltpu.VMEM)] * len(outs) if many else pl.BlockSpec(memory_space=pltpu.VMEM)
    return pl.pallas_call(
        kernel, out_shape=outs, in_specs=specs, out_specs=out_specs, scratch_shapes=list(scratch),
        input_output_aliases=aliases or {},
        compiler_params=pltpu.CompilerParams(vmem_limit_bytes=limit * 2**20),
    )


def shift(value, axis, step):
    count = lax.axis_size(axis)
    return lax.ppermute(value, axis, [(i, (i + step) % count) for i in range(count)])


def shift_both(value, step_y, step_z):
    ny, nz = lax.axis_size("gy"), lax.axis_size("gz")
    pairs = [
        (y * nz + z, (y + step_y) % ny * nz + (z + step_z) % nz) for y in range(ny) for z in range(nz)
    ]
    return lax.ppermute(value, ("gy", "gz"), pairs)


def across(value, step_z):
    if lax.axis_size("gy") == 2:
        return shift_both(value, 1, step_z)
    half = value.shape[0] // 2
    return jnp.concatenate([shift_both(value[:half], 1, step_z), shift_both(value[half:], -1, step_z)], 0)


def on_device(pop_ratio, solid_flags, class_ids, drag_table, row_map, old_basis, old_sigma):
    slab = ("gy", "gz")
    everyone = ("gx", "gy", "gz")
    owners = lax.axis_size(slab)
    devices = lax.axis_size(everyone)
    rows_local = old_basis.shape[1]
    highs = owners * rows_local // LOW
    cells = 4096
    tile = (8, 128)

    pops, g, zr, zl, y, cr, cl = call(
        init_kernel,
        (vmem(19, 2, 16, 128), vmem(2, 16, 128), vmem(3, *tile), vmem(3, *tile))
        + (vmem(2 * FIELDS, *tile), vmem(2, *tile), vmem(2, *tile)),
        (
            pltpu.SMEM(drag_table.shape, jnp.float32),
            pltpu.VMEM((19, 2, 16, 128), jnp.float32),
            pltpu.VMEM((2, 16, 128), jnp.int32),
            pltpu.VMEM((2, 16, 128), jnp.int32),
            pltpu.SemaphoreType.DMA((4,)),
        ),
        count=4,
        space=pltpu.HBM,
    )(*(pltpu.with_memory_space_constraint(v, pltpu.HBM) for v in (drag_table, pop_ratio, solid_flags, class_ids)))
    y = across(y, 0)
    left, right = shift(zr, "gz", 1), shift(zl, "gz", -1)
    cr, cl = across(cr, 1), across(cl, -1)

    wide = pltpu.VMEM((19, 2, 24, 256), jnp.float32)
    side = pltpu.VMEM((2, 5, 24, 256), jnp.float32)
    big, wall, vel, face = vmem(19, 2, 24, 256), vmem(2, 24, 256), vmem(3, 2, 16, 128), vmem(16, *tile)
    deep_face, loaded, sides = vmem(DEEP_TILES, *tile), vmem(11, *tile), vmem(2, 5, 24, 256)
    relaxed, g_wide, v0 = call(inner_kernel, (big, wall, vel), (wide,), count=4)(
        *map(held, (pops, g, left, right))
    )
    relaxed, g_wide, xr, xl = call(
        outer_kernel, (big, wall, face, face), (wide,), count=5, aliases={0: 0, 1: 1}
    )(*map(held, (relaxed, g_wide, y, cr, cl)))
    old, own = call(
        functools.partial(old_kernel, float(rows_local * devices)),
        (vmem(32, rows_local), vmem(*tile)),
        (pltpu.VMEM((32, 128), jnp.float32),),
        count=2,
    )(old_basis, old_sigma[:, None])
    small = tuple(lax.axis_size(a) for a in everyone) == (4, 2, 4)
    if not small:
        own = lax.psum(own, everyone)
    onehot = call(onehot_kernel, pltpu.VMEM((LOW, cells), jnp.bfloat16), count=1)(row_map)
    xr, xl = shift(xr, "gx", 1), shift(xl, "gx", -1)
    ahead = call(local_kernel, big, count=1)(held(relaxed))
    if small:
        own = own + shift(own, "gy", 1)
    ahead, going, v1, xr, xl = call(
        step_kernel, (big, sides, vel, deep_face, deep_face), (side, wide), count=4
    )(*map(held, (ahead, g_wide, xr, xl)))
    xr, xl = shift(xr, "gx", 1), shift(xl, "gx", -1)
    if small:
        own = (own + shift(own, "gz", 2)) + (shift(own, "gz", 1) + shift(own, "gz", -1))
    ahead, faces, v2 = call(
        pair_kernel, (big, sides, vel), (pltpu.VMEM((2, DEEP, 24, 256), jnp.float32), wide), count=5
    )(*map(held, (ahead, going, g_wide, xr, xl)))
    state = tuple(map(held, (ahead, g_wide, faces)))
    relaxed, xr, xl = call(end_step_kernel, (big, loaded, loaded), count=4)(*state, held(own))
    xr, xl = shift(xr, "gx", 1), shift(xl, "gx", -1)
    if small:
        own = (own + shift(own, "gx", 2)) + (xr[10] + xl[10])

    lefts = pltpu.VMEM((12 * highs, cells), jnp.bfloat16)
    early = call(early_kernel, vmem(12 * highs, LOW), (lefts,), count=4, limit=12 + highs // 2)(
        held(v0), held(v1), row_map, held(onehot)
    )
    term = call(
        late_kernel,
        f32(12 * highs, LOW),
        (lefts, pltpu.VMEM((3, 2, 16, 128), jnp.float32)),
        count=7,
        limit=12 + highs // 2,
    )(*state, held(v2), row_map, held(onehot), held(early))
    parts = lax.all_to_all(term, slab, 0, 0, tiled=True)
    snap, gram = call(
        functools.partial(gram_kernel, float(rows_local * devices)),
        (vmem(16, rows_local), f32(4 * devices, 128)),
        (pltpu.VMEM((128, rows_local), jnp.float32),),
        count=2,
    )(held(parts), held(old))
    grams = lax.all_to_all(gram, everyone, 0, 0, tiled=True)
    factor, head = call(old_factor_kernel, (vmem(32, 128), vmem(32, rows_local)), count=2)(
        held(own), held(old)
    )
    new_basis, upper = call(
        factor_kernel, (f32(44, rows_local), f32(44, 44)), (pltpu.VMEM((16, 128), jnp.float32),), count=4
    )(*map(held, (grams, factor, head, snap)))
    populations = call(last_kernel, f32(19, 2, 16, 128), count=3)(*map(held, (relaxed, xr, xl)))
    return (populations, new_basis, upper)


def solution(mesh):
    in_specs = (
        P(None, "gx", "gy", "gz"),
        P("gx", "gy", "gz"),
        P("gx", "gy", "gz"),
        P(),
        P("gx", "gy", "gz"),
        P(None, ("gx", "gy", "gz")),
        P(),
    )
    out_specs = (P(None, "gx", "gy", "gz"), P(None, ("gx", "gy", "gz")), P())

    return jax.shard_map(on_device, mesh=mesh, in_specs=in_specs, out_specs=out_specs, check_vma=False)
```

```python
import functools

import jax
import jax.numpy as jnp
import numpy as np
from jax import lax
from jax.experimental import pallas as pl
from jax.experimental.pallas import tpu as pltpu
from jax.sharding import PartitionSpec as P


VOX_ROW = 8
LATTICE = np.array(
    [
        [0, 0, 0],
        [1, 0, 0],
        [-1, 0, 0],
        [0, 1, 0],
        [0, -1, 0],
        [0, 0, 1],
        [0, 0, -1],
        [1, 1, 0],
        [-1, -1, 0],
        [1, -1, 0],
        [-1, 1, 0],
        [1, 0, 1],
        [-1, 0, -1],
        [1, 0, -1],
        [-1, 0, 1],
        [0, 1, 1],
        [0, -1, -1],
        [0, 1, -1],
        [0, -1, 1],
    ]
)
OPPOSITE = [0, 2, 1, 4, 3, 6, 5, 8, 7, 10, 9, 12, 11, 14, 13, 16, 15, 18, 17]
WEIGHTS = [1.0 / 3.0] + [1.0 / 18.0] * 6 + [1.0 / 36.0] * 12
PAIRS = [(q, OPPOSITE[q]) for q in range(1, 19) if q < OPPOSITE[q]]
PLUS_X = [q for q in range(19) if LATTICE[q, 0] == 1]
MINUS_X = [q for q in range(19) if LATTICE[q, 0] == -1]
relax_time = 0.9
vel_scale = 16.0

FIELDS = 20
LOW = 256


def lanes(shape=(8, 128)):
    return lax.broadcasted_iota(jnp.int32, shape, len(shape) - 1)


def subs(shape=(8, 128)):
    return lax.broadcasted_iota(jnp.int32, shape, len(shape) - 2)


def roll(value, shift, axis):
    size = value.shape[axis]
    shift = shift % size
    return value if shift == 0 else pltpu.roll(value, shift, axis)


def init_kernel(
    table_hbm, ratio_hbm, solid_hbm, cls_hbm,
    pops_ref, g_ref, zr_ref, zl_ref, y_ref, cr_ref, cl_ref,
    table, ratio, solid, cls, sems,
):
    pairs = ((ratio_hbm, ratio), (table_hbm, table), (solid_hbm, solid), (cls_hbm, cls))
    copies = [pltpu.make_async_copy(src, dst, sems.at[i]) for i, (src, dst) in enumerate(pairs)]
    for copy in copies:
        copy.start()
    for copy in copies:
        copy.wait()
    lane, sub = lanes(), subs()
    blank = jnp.zeros((8, 128), jnp.float32)
    zr, zl = [blank] * 3, [blank] * 3
    cr, cl = [blank] * 2, [blank] * 2
    for f in range(FIELDS):
        tiles = {}
        for x in range(2):
            for yt in range(2):
                rows = pl.ds(8 * yt, 8)
                if f < 19:
                    tile = ratio[f, x, rows, :] * WEIGHTS[f]
                    pops_ref[f, x, rows, :] = tile
                else:
                    ids = cls[x, rows, :]
                    drag = jnp.zeros((8, 128), jnp.float32)
                    for c in range(table.shape[0]):
                        drag = jnp.where(ids == c, table[c], drag)
                    tile = jnp.where(solid[x, rows, :] == 1, -1.0, 1.0 + 0.5 * drag)
                    g_ref[x, rows, :] = tile
                tiles[x, yt] = tile
                at, k = divmod(f * 4 + x * 2 + yt, 32)
                here = (lane >= 4 * k) & (lane < 4 * k + 4)
                zr[at] = jnp.where(here, roll(tile, 4 * k - 124, 1), zr[at])
                zl[at] = jnp.where(here, roll(tile, 4 * k, 1), zl[at])
        up = jnp.where(sub < 4, roll(tiles[0, 1], 4, 0), tiles[1, 1])
        down = jnp.where(sub < 4, tiles[0, 0], roll(tiles[1, 0], 4, 0))
        y_ref[f] = up
        y_ref[FIELDS + f] = down
        here = (lane >= 4 * f) & (lane < 4 * f + 4)
        for i, tile in enumerate((up, down)):
            cr[i] = jnp.where(here, roll(tile, 4 * f - 124, 1), cr[i])
            cl[i] = jnp.where(here, roll(tile, 4 * f, 1), cl[i])
    for at in range(3):
        zr_ref[at] = zr[at]
        zl_ref[at] = zl[at]
    for at in range(2):
        cr_ref[at] = cr[at]
        cl_ref[at] = cl[at]


def moments(pops, g):
    density = pops[0]
    for q in range(1, 19):
        density = density + pops[q]
    scale = 1.0 / (density * jnp.abs(g))
    speeds = []
    for a in range(3):
        total = None
        for q in range(19):
            c = LATTICE[q, a]
            if c == 1:
                total = pops[q] if total is None else total + pops[q]
            elif c == -1:
                total = total - pops[q]
        speeds.append(total * scale)
    return density, speeds


def collide(pops, g):
    density, speeds = moments(pops, g)
    square = speeds[0] * speeds[0] + speeds[1] * speeds[1] + speeds[2] * speeds[2]
    solid = g < 0.0
    keep = 1.0 - 1.0 / relax_time
    base = 1.0 - 1.5 * square
    part = {w: density * (w / relax_time) for w in sorted(set(WEIGHTS))}
    relaxed = [None] * 19
    rest = pops[0] * keep + part[WEIGHTS[0]] * base
    relaxed[0] = jnp.where(solid, pops[0], rest)
    for q, o in PAIRS:
        along = None
        for a in range(3):
            c = LATTICE[q, a]
            if c == 1:
                along = speeds[a] if along is None else along + speeds[a]
            elif c == -1:
                along = -speeds[a] if along is None else along - speeds[a]
        even = part[WEIGHTS[q]] * (base + 4.5 * along * along)
        odd = part[WEIGHTS[q]] * (3.0 * along)
        relaxed[q] = jnp.where(solid, pops[o], pops[q] * keep + (even + odd))
        relaxed[o] = jnp.where(solid, pops[q], pops[o] * keep + (even - odd))
    factor = jnp.where(solid, 0.0, vel_scale / VOX_ROW)
    return relaxed, [s * factor for s in speeds]


def collide_all(source, g_of, out, vel_ref, tiles=range(3)):
    for x in range(2):
        for yt in tiles:
            for lt in range(2):
                rows, cols = pl.ds(8 * yt, 8), pl.ds(128 * lt, 128)
                pops = [source(q, x, rows, cols) for q in range(19)]
                relaxed, vel = collide(pops, g_of[x, rows, cols])
                for q in range(19):
                    out[q, x, rows, cols] = relaxed[q]
                if vel_ref is not None and yt < 2 and lt == 0:
                    for a in range(3):
                        vel_ref[a, x, rows, :] = vel[a]


def pack_x(out, xr_ref, xl_ref):
    lane = lanes()
    for ref, directions, x in ((xr_ref, PLUS_X, 1), (xl_ref, MINUS_X, 0)):
        extra = jnp.zeros((8, 128), jnp.float32)
        for i, q in enumerate(directions):
            for yt in range(3):
                j = 3 * i + yt
                ref[j] = out[q, x, pl.ds(8 * yt, 8), pl.ds(0, 128)]
                tile = out[q, x, pl.ds(8 * yt, 8), pl.ds(128, 128)]
                here = (lane >= 8 * j) & (lane < 8 * j + 8)
                extra = jnp.where(here, roll(tile, 4 + 8 * j, 1), extra)
        ref[15] = extra


STILL = [q for q in range(19) if LATTICE[q, 0] == 0]
DEEP = 14
DEEP_TILES = 38


def still_sums(pops):
    total = pops[0]
    for value in pops[1:]:
        total = total + value
    sums = [total]
    for a in (1, 2):
        plus = [p for p, q in zip(pops, STILL) if LATTICE[q, a] == 1]
        minus = [p for p, q in zip(pops, STILL) if LATTICE[q, a] == -1]
        sums.append(((plus[0] + plus[1]) + plus[2]) - ((minus[0] + minus[1]) + minus[2]))
    return sums


def pack_deep(ahead, going, g_ref, refs):
    lane, sub = lanes(), subs()
    for side, ref in enumerate(refs):
        x = 1 - side
        edges = [jnp.zeros((8, 128), jnp.float32)] * 3
        directions = (PLUS_X, MINUS_X)[side]

        def entries(yt, lt):
            at = (pl.ds(8 * yt, 8), pl.ds(128 * lt, 128))
            tiles = [going[side, i, at[0], at[1]] for i in range(5)]
            tiles += [ahead[q, x, at[0], at[1]] for q in directions]
            tiles += still_sums([ahead[q, x, at[0], at[1]] for q in STILL])
            return tiles + [g_ref[x, at[0], at[1]]]

        def edge(j, tile):
            at, k = divmod(j, 16)
            here = (lane >= 8 * k) & (lane < 8 * k + 8)
            edges[at] = jnp.where(here, roll(tile, 4 + 8 * k, 1), edges[at])

        for yt in range(2):
            for e, (inner, outer) in enumerate(zip(entries(yt, 0), entries(yt, 1))):
                ref[2 * e + yt] = inner
                edge(2 * e + yt, outer)
        halos = [entries(2, lt) for lt in range(2)]
        for e in range(0, DEEP, 2):
            pair = [jnp.where(sub < 4, roll(h[e], 2, 0), roll(h[e + 1], 6, 0)) for h in halos]
            ref[28 + e // 2] = pair[0]
            edge(28 + e // 2, pair[1])
        for at in range(3):
            ref[35 + at] = edges[at]


def take_deep(refs, deep):
    for side, ref in enumerate(refs):

        def edge(j):
            return roll(ref[35 + j // 16], -(8 * (j % 16) + 4), 1)

        for e in range(DEEP):
            back = -2 if e % 2 == 0 else -6
            for yt in range(2):
                deep[side, e, pl.ds(8 * yt, 8), pl.ds(0, 128)] = ref[2 * e + yt]
                deep[side, e, pl.ds(8 * yt, 8), pl.ds(128, 128)] = edge(2 * e + yt)
            deep[side, e, pl.ds(16, 8), pl.ds(0, 128)] = roll(ref[28 + e // 2], back, 0)
            deep[side, e, pl.ds(16, 8), pl.ds(128, 128)] = roll(edge(28 + e // 2), back, 0)


def collide_side(toward, away, sums, g, side):
    ahead, back = ((PLUS_X, MINUS_X), (MINUS_X, PLUS_X))[side]
    into, out_of = toward[0], away[0]
    for value in toward[1:]:
        into = into + value
    for value in away[1:]:
        out_of = out_of + value
    density = sums[0] + (into + out_of)
    flows = [into - out_of if side == 0 else out_of - into, sums[1], sums[2]]
    for directions, pops in ((ahead, toward), (back, away)):
        for q, value in zip(directions, pops):
            for a in (1, 2):
                if LATTICE[q, a] == 1:
                    flows[a] = flows[a] + value
                elif LATTICE[q, a] == -1:
                    flows[a] = flows[a] - value
    scale = 1.0 / (density * jnp.abs(g))
    speeds = [flow * scale for flow in flows]
    square = speeds[0] * speeds[0] + speeds[1] * speeds[1] + speeds[2] * speeds[2]
    keep = 1.0 - 1.0 / relax_time
    base = 1.0 - 1.5 * square
    solid = g < 0.0
    part = {w: density * (w / relax_time) for w in sorted({WEIGHTS[q] for q in ahead})}
    relaxed = []
    for q, value in zip(ahead, toward):
        along = None
        for a in range(3):
            c = LATTICE[q, a]
            if c == 1:
                along = speeds[a] if along is None else along + speeds[a]
            elif c == -1:
                along = -speeds[a] if along is None else along - speeds[a]
        moved = value * keep + part[WEIGHTS[q]] * ((base + 4.5 * along * along) + 3.0 * along)
        relaxed.append(jnp.where(solid, away[back.index(OPPOSITE[q])], moved))
    return relaxed


def inner_kernel(pops, g_in, left, right, out, g_ref, vel_ref, wide):
    lane = lanes()
    for f in range(FIELDS):
        ref = wide.at[f] if f < 19 else g_ref
        for x in range(2):
            for yt in range(2):
                rows = pl.ds(8 * yt, 8)
                own = pops[f, x, rows, :] if f < 19 else g_in[x, rows, :]
                at, k = divmod(f * 4 + x * 2 + yt, 32)
                tile = jnp.where(lane < 4, roll(right[at], -4 * k, 1), own)
                tile = jnp.where(lane >= 124, roll(left[at], 124 - 4 * k, 1), tile)
                ref[x, rows, pl.ds(0, 128)] = own
                ref[x, rows, pl.ds(128, 128)] = tile
    collide_all(lambda q, x, rows, cols: wide[q, x, rows, cols], g_ref, out, vel_ref, range(2))


def outer_kernel(out_in, g_in, y, cr, cl, out, g_ref, xr_ref, xl_ref, wide):
    lane, sub = lanes(), subs()
    for f in range(FIELDS):
        ref = wide.at[f] if f < 19 else g_ref
        pairs = []
        for i in range(2):
            own = y[FIELDS * i + f]
            tile = jnp.where(lane < 4, roll(cl[i], -4 * f, 1), own)
            pairs.append((own, jnp.where(lane >= 124, roll(cr[i], 124 - 4 * f, 1), tile)))
        high, low = pairs
        for lt in range(2):
            cols = pl.ds(128 * lt, 128)
            ref[0, pl.ds(16, 8), cols] = jnp.where(sub < 4, low[lt], roll(high[lt], 4, 0))
            ref[1, pl.ds(16, 8), cols] = jnp.where(sub < 4, roll(low[lt], 4, 0), high[lt])
    collide_all(lambda q, x, rows, cols: wide[q, x, rows, cols], g_ref, out, None, (2,))
    pack_x(out, xr_ref, xl_ref)


def unpack_x(xr, xl, side):
    for s, ref in enumerate((xr, xl)):
        for i in range(5):
            for yt in range(3):
                j = 3 * i + yt
                side[s, i, pl.ds(8 * yt, 8), pl.ds(0, 128)] = ref[j]
                side[s, i, pl.ds(8 * yt, 8), pl.ds(128, 128)] = roll(ref[15], -(8 * j + 4), 1)


def turned(value, q):
    return roll(roll(value, int(LATTICE[q, 1]), 0), int(LATTICE[q, 2]), 1)


def remote(q, x):
    if LATTICE[q, 0] == 1 and x == 0:
        return 0, PLUS_X.index(q)
    if LATTICE[q, 0] == -1 and x == 1:
        return 1, MINUS_X.index(q)
    return None


def local_kernel(prev, ahead):
    for q in range(19):
        for x in range(2):
            if remote(q, x) is None:
                ahead[q, x] = turned(prev[q, x - int(LATTICE[q, 0])], q)


def take_faces(xr, xl, side):
    unpack_x(xr, xl, side)
    for s, directions in enumerate((PLUS_X, MINUS_X)):
        for i, q in enumerate(directions):
            side[s, i] = turned(side[s, i], q)


def chooser(ahead, side):
    def pick(q, x, rows, cols):
        at = remote(q, x)
        return ahead[q, x, rows, cols] if at is None else side[at[0], at[1], rows, cols]

    return pick


def step_kernel(ahead_in, g_ref, xr, xl, ahead, going, vel_ref, xr_ref, xl_ref, side, out):
    take_faces(xr, xl, side)
    collide_all(chooser(ahead_in, side), g_ref, out, vel_ref)
    local_kernel(out, ahead)
    for i in range(5):
        going[0, i] = turned(out[PLUS_X[i], 1], PLUS_X[i])
        going[1, i] = turned(out[MINUS_X[i], 0], MINUS_X[i])
    pack_deep(ahead, going, g_ref, (xr_ref, xl_ref))


def pair(ahead, going, g_ref, xr, xl, ahead_ref, side_ref, vel_ref, deep, out):
    take_deep((xr, xl), deep)

    def pick(q, x, rows, cols):
        at = remote(q, x)
        return ahead[q, x, rows, cols] if at is None else deep[at[0], at[1], rows, cols]

    collide_all(pick, g_ref, out, vel_ref)
    for side, directions in enumerate((PLUS_X, MINUS_X)):
        for yt in range(3):
            for lt in range(2):
                rows, cols = pl.ds(8 * yt, 8), pl.ds(128 * lt, 128)
                toward = [deep[side, 5 + i, rows, cols] for i in range(5)]
                away = [going[1 - side, i, rows, cols] for i in range(5)]
                sums = [deep[side, 10 + i, rows, cols] for i in range(3)]
                relaxed = collide_side(toward, away, sums, deep[side, 13, rows, cols], side)
                for i in range(5):
                    side_ref[side, i, rows, cols] = relaxed[i]
        for i, q in enumerate(directions):
            side_ref[side, i] = turned(side_ref[side, i], q)
    local_kernel(out, ahead_ref)


def end_step_kernel(ahead, g_ref, side, rider, out, xr_ref, xl_ref):
    collide_all(chooser(ahead, side), g_ref, out, None)
    for ref, directions, x in ((xr_ref, PLUS_X, 1), (xl_ref, MINUS_X, 0)):
        for i, q in enumerate(directions):
            value = turned(out[q, x], q)
            for yt in range(2):
                ref[2 * i + yt] = value[8 * yt : 8 * yt + 8, :128]
        ref[10] = rider[...]


def last_kernel(prev, xr, xl, out):
    for q in range(19):
        for x in range(2):
            at = remote(q, x)
            if at is None:
                out[q, x] = turned(prev[q, x - int(LATTICE[q, 0])], q)[:16, :128]
            else:
                for yt in range(2):
                    out[q, x, pl.ds(8 * yt, 8), :] = (xr, xl)[at[0]][2 * at[1] + yt]


def split(value):
    big = value.astype(jnp.bfloat16).astype(jnp.float32)
    return big, value - big


def onehot_kernel(row_map, right):
    low_at = lax.broadcasted_iota(jnp.int32, (LOW, 128), 0)
    for x in range(2):
        for y in range(16):
            rows = row_map[x, pl.ds(y, 1), :]
            low = rows - (rows // LOW) * LOW
            cols = pl.ds(128 * (16 * x + y), 128)
            right[:, cols] = jnp.where(low_at == low, 1.0, 0.0).astype(jnp.bfloat16)


def times_onehot(left, right):
    return lax.dot_general(
        left[...], right[...], (((1,), (1,)), ((), ())), preferred_element_type=jnp.float32
    )


def restricted(vels, row_map, right, left):
    count = 3 * len(vels)
    highs = left.shape[0] // (2 * count)
    high_at = lax.broadcasted_iota(jnp.int32, (highs, 128), 0)
    for x in range(2):
        for y in range(16):
            cols = pl.ds(128 * (16 * x + y), 128)
            here = high_at == row_map[x, pl.ds(y, 1), :] // LOW
            for j in range(count):
                for i, part in enumerate(split(vels[j // 3][j % 3, x, pl.ds(y, 1), :])):
                    left[pl.ds(highs * (count * i + j), highs), cols] = jnp.where(here, part, 0.0).astype(jnp.bfloat16)
    both = times_onehot(left, right)
    half = count * highs
    return both[:half] + both[half:]


def early_kernel(v0, v1, row_map, right, out, left):
    highs = out.shape[0] // 12
    both = restricted((v0, v1), row_map, right, left)
    for h in range(highs):
        for j in range(6):
            out[pl.ds(12 * h + j, 1), :] = both[highs * j + h : highs * j + h + 1]
            out[pl.ds(12 * h + 6 + j, 1), :] = jnp.zeros((1, LOW), jnp.float32)


def pair_late_kernel(
    ahead, going, g_ref, xr, xl, row_map, right, early, ahead_ref, side_ref, out, deep, relaxed, v2, v3, left
):
    pair(ahead, going, g_ref, xr, xl, ahead_ref, side_ref, v2, deep, relaxed)
    late(ahead_ref, g_ref, side_ref, v2, row_map, right, early, out, left, v3)


def old_kernel(total_rows, basis, sigma, scaled_ref, tile_ref, work):
    scaled = basis[...] * sigma[...]
    scaled_ref[...] = scaled
    work[...] = jnp.zeros((32, 128), jnp.float32)
    work[:, pl.ds(0, 32)] = dot(scaled, scaled, 1) * (1.0 / total_rows)
    lane = lanes()
    tile = work[pl.ds(0, 8), :]
    for k in range(1, 4):
        here = (lane >= 32 * k) & (lane < 32 * k + 32)
        tile = jnp.where(here, roll(work[pl.ds(8 * k, 8), :], 32 * k, 1), tile)
    tile_ref[...] = tile


def dot(a, b, dim):
    return lax.dot_general(
        a,
        b,
        (((1,), (dim,)), ((), ())),
        precision=lax.Precision.HIGHEST,
        preferred_element_type=jnp.float32,
    )


def late(ahead, g_ref, side, v2, row_map, right, early, out, left, v3):
    pick = chooser(ahead, side)
    for x in range(2):
        for yt in range(2):
            rows, cols = pl.ds(8 * yt, 8), pl.ds(0, 128)
            g = g_ref[x, rows, cols]
            _, speeds = moments([pick(q, x, rows, cols) for q in range(19)], g)
            factor = jnp.where(g < 0.0, 0.0, vel_scale / VOX_ROW)
            for a in range(3):
                v3[a, x, rows, :] = speeds[a] * factor
    highs = out.shape[0] // 12
    both = restricted((v2, v3), row_map, right, left)
    out[...] = early[...]
    for h in range(highs):
        for j in range(6):
            out[pl.ds(12 * h + 6 + j, 1), :] = both[highs * j + h : highs * j + h + 1]


def gram_kernel(total_rows, parts, scaled, snap_ref, out, aug):
    owners = parts.shape[0] // 24
    total = parts[pl.ds(0, 24), :]
    for o in range(1, owners):
        total = total + parts[pl.ds(24 * o, 24), :]
    aug[pl.ds(0, 32), :] = scaled[...]
    aug[pl.ds(40, 88), :] = jnp.zeros((88, 2 * LOW), jnp.float32)
    aug[pl.ds(32, 12), pl.ds(0, LOW)] = total[:12]
    aug[pl.ds(32, 12), pl.ds(LOW, LOW)] = total[12:]
    snap = aug[pl.ds(32, 16), :]
    snap_ref[...] = snap
    product = dot(snap, aug[...], 1) * (1.0 / total_rows)
    lane = lanes()
    tail = jnp.where(lane < 120, roll(product[8:], 88, 1), roll(product[8:], 80, 1))
    packed = jnp.where(lane < 44, product[:8], jnp.where(lane < 88, roll(roll(product[:8], 4, 0), 44, 1), tail))
    twice = jnp.where(subs() < 4, packed, roll(packed, 4, 0))
    for d in range(out.shape[0] // 8):
        out[pl.ds(8 * d, 8), :] = twice


def eliminate(tiles, count):
    sub = subs()
    done = list(tiles)

    def spread(value, row):
        return jnp.broadcast_to(value[row : row + 1, :], (8, 128))

    for k in range(0, count, 2):
        t, r = divmod(k, 8)
        row0, row1 = spread(tiles[t], r), spread(tiles[t], r + 1)
        cols = {
            u: [jnp.broadcast_to(tiles[u][:, k + i : k + i + 1], (8, 128)) for i in range(2)]
            for u in range(t, len(tiles))
        }
        a, b, c = spread(cols[t][0], r), spread(cols[t][1], r), spread(cols[t][1], r + 1)
        inv = 1.0 / (a * c - b * b)
        part0 = (c * row0 - b * row1) * inv
        part1 = (a * row1 - b * row0) * inv
        ratio = b / a
        first = row0 * (1.0 / jnp.sqrt(a))
        second = (row1 - ratio * row0) * (1.0 / jnp.sqrt(c - ratio * b))
        done[t] = jnp.where(sub == r, first, jnp.where(sub == r + 1, second, done[t]))
        for u in range(t, len(tiles)):
            tiles[u] = tiles[u] - (cols[u][0] * part0 + cols[u][1] * part1)
    return [jnp.where((lanes() >= 64) | (lanes() >= sub + 8 * t), tile, 0.0) for t, tile in enumerate(done)]


def old_factor_kernel(tile, scaled, work, head_ref):
    lane, sub = lanes(), subs()
    tiles = []
    for k in range(4):
        own = jnp.where(lane < 32, roll(tile[...], -32 * k, 1), 0.0)
        tiles.append(own + jnp.where(lane == sub + 8 * k + 64, 1.0, 0.0))
    for k, value in enumerate(eliminate(tiles, 32)):
        work[pl.ds(8 * k, 8), :] = value
    head_ref[...] = dot(work[:, pl.ds(64, 32)], scaled[...], 0)


def factor_kernel(parts, factor, head, snap, basis_ref, tri_ref, work):
    lane, sub = lanes(), subs()
    sums = [parts[pl.ds(8 * d, 8), :] for d in range(parts.shape[0] // 8)]
    while len(sums) > 1:
        sums = [sums[i] + sums[i + 1] for i in range(0, len(sums), 2)]
    total = sums[0] + roll(sums[0], 4, 0)
    top = jnp.where(lane < 44, jnp.where(sub < 4, total, roll(total, -44, 1)), 0.0)
    low = jnp.where(lane < 32, roll(total, -88, 1), roll(total, -80, 1))
    work[pl.ds(0, 8), :] = top
    work[pl.ds(8, 8), :] = jnp.where((sub < 4) & (lane < 44), low, 0.0)
    work[pl.ds(8, 8), pl.ds(32, 8)] = top.T[40:48]
    cross = work[:, pl.ds(0, 32)]
    inner = work[:, pl.ds(32, 16)]
    inverse = factor[:, pl.ds(64, 32)]
    below = dot(cross, inverse, 1)
    rest = snap[...] - dot(below, head[...], 0)
    inner = inner - dot(below, below, 1)
    work[...] = jnp.zeros((16, 128), jnp.float32)
    work[:, pl.ds(0, 16)] = inner
    tiles = [work[pl.ds(8 * t, 8), :] + jnp.where(lane == sub + 8 * t + 64, 1.0, 0.0) for t in range(2)]
    for t, value in enumerate(eliminate(tiles, 12)):
        work[pl.ds(8 * t, 8), :] = value
    tri_ref[pl.ds(0, 32), pl.ds(0, 32)] = factor[:, pl.ds(0, 32)]
    tri_ref[pl.ds(0, 32), pl.ds(32, 12)] = dot(inverse, cross, 1)[:, :12]
    tri_ref[pl.ds(32, 12), pl.ds(0, 32)] = jnp.zeros((12, 32), jnp.float32)
    tri_ref[pl.ds(32, 12), pl.ds(32, 12)] = work[pl.ds(0, 12), pl.ds(0, 12)]
    basis_ref[pl.ds(0, 32), :] = head[...]
    basis_ref[pl.ds(32, 12), :] = dot(work[:, pl.ds(64, 16)], rest, 0)[:12]


def f32(*shape):
    return jax.ShapeDtypeStruct(shape, jnp.float32)


def vmem(*shape):
    return pltpu.VMEM(shape, jnp.float32)


def held(value):
    return pltpu.with_memory_space_constraint(value, pltpu.VMEM)


def call(kernel, outs, scratch=(), count=None, aliases=None, limit=16, space=pltpu.VMEM):
    specs = [pl.BlockSpec(memory_space=space) for _ in range(count)]
    many = isinstance(outs, (tuple, list))
    out_specs = [pl.BlockSpec(memory_space=pltpu.VMEM)] * len(outs) if many else pl.BlockSpec(memory_space=pltpu.VMEM)
    return pl.pallas_call(
        kernel, out_shape=outs, in_specs=specs, out_specs=out_specs, scratch_shapes=list(scratch),
        input_output_aliases=aliases or {},
        compiler_params=pltpu.CompilerParams(vmem_limit_bytes=limit * 2**20),
    )


def shift(value, axis, step):
    count = lax.axis_size(axis)
    return lax.ppermute(value, axis, [(i, (i + step) % count) for i in range(count)])


def shift_both(value, step_y, step_z):
    ny, nz = lax.axis_size("gy"), lax.axis_size("gz")
    pairs = [
        (y * nz + z, (y + step_y) % ny * nz + (z + step_z) % nz) for y in range(ny) for z in range(nz)
    ]
    return lax.ppermute(value, ("gy", "gz"), pairs)


def across(value, step_z):
    if lax.axis_size("gy") == 2:
        return shift_both(value, 1, step_z)
    half = value.shape[0] // 2
    return jnp.concatenate([shift_both(value[:half], 1, step_z), shift_both(value[half:], -1, step_z)], 0)


def on_device(pop_ratio, solid_flags, class_ids, drag_table, row_map, old_basis, old_sigma):
    slab = ("gy", "gz")
    everyone = ("gx", "gy", "gz")
    owners = lax.axis_size(slab)
    devices = lax.axis_size(everyone)
    rows_local = old_basis.shape[1]
    highs = owners * rows_local // LOW
    cells = 4096
    tile = (8, 128)

    pops, g, zr, zl, y, cr, cl = call(
        init_kernel,
        (vmem(19, 2, 16, 128), vmem(2, 16, 128), vmem(3, *tile), vmem(3, *tile))
        + (vmem(2 * FIELDS, *tile), vmem(2, *tile), vmem(2, *tile)),
        (
            pltpu.SMEM(drag_table.shape, jnp.float32),
            pltpu.VMEM((19, 2, 16, 128), jnp.float32),
            pltpu.VMEM((2, 16, 128), jnp.int32),
            pltpu.VMEM((2, 16, 128), jnp.int32),
            pltpu.SemaphoreType.DMA((4,)),
        ),
        count=4,
        space=pltpu.HBM,
    )(*(pltpu.with_memory_space_constraint(v, pltpu.HBM) for v in (drag_table, pop_ratio, solid_flags, class_ids)))
    y = across(y, 0)
    left, right = shift(zr, "gz", 1), shift(zl, "gz", -1)
    cr, cl = across(cr, 1), across(cl, -1)

    wide = pltpu.VMEM((19, 2, 24, 256), jnp.float32)
    side = pltpu.VMEM((2, 5, 24, 256), jnp.float32)
    big, wall, vel, face = vmem(19, 2, 24, 256), vmem(2, 24, 256), vmem(3, 2, 16, 128), vmem(16, *tile)
    deep_face, loaded, sides = vmem(DEEP_TILES, *tile), vmem(11, *tile), vmem(2, 5, 24, 256)
    relaxed, g_wide, v0 = call(inner_kernel, (big, wall, vel), (wide,), count=4)(
        *map(held, (pops, g, left, right))
    )
    relaxed, g_wide, xr, xl = call(
        outer_kernel, (big, wall, face, face), (wide,), count=5, aliases={0: 0, 1: 1}
    )(*map(held, (relaxed, g_wide, y, cr, cl)))
    old, own = call(
        functools.partial(old_kernel, float(rows_local * devices)),
        (vmem(32, rows_local), vmem(*tile)),
        (pltpu.VMEM((32, 128), jnp.float32),),
        count=2,
    )(old_basis, old_sigma[:, None])
    small = tuple(lax.axis_size(a) for a in everyone) == (4, 2, 4)
    if not small:
        own = lax.psum(own, everyone)
    onehot = call(onehot_kernel, pltpu.VMEM((LOW, cells), jnp.bfloat16), count=1)(row_map)
    xr, xl = shift(xr, "gx", 1), shift(xl, "gx", -1)
    ahead = call(local_kernel, big, count=1)(held(relaxed))
    if small:
        own = own + shift(own, "gy", 1)
    ahead, going, v1, xr, xl = call(
        step_kernel, (big, sides, vel, deep_face, deep_face), (side, wide), count=4
    )(*map(held, (ahead, g_wide, xr, xl)))
    xr, xl = shift(xr, "gx", 1), shift(xl, "gx", -1)
    if small:
        own = (own + shift(own, "gz", 2)) + (shift(own, "gz", 1) + shift(own, "gz", -1))
    lefts = pltpu.VMEM((12 * highs, cells), jnp.bfloat16)
    early = call(early_kernel, vmem(12 * highs, LOW), (lefts,), count=4, limit=12 + highs // 2)(
        held(v0), held(v1), row_map, held(onehot)
    )
    small_vel = pltpu.VMEM((3, 2, 16, 128), jnp.float32)
    ahead, faces, term = call(
        pair_late_kernel,
        (big, sides, f32(12 * highs, LOW)),
        (pltpu.VMEM((2, DEEP, 24, 256), jnp.float32), wide, small_vel, small_vel, lefts),
        count=8,
        limit=16 + highs // 2,
    )(*map(held, (ahead, going, g_wide, xr, xl)), row_map, held(onehot), held(early))
    state = tuple(map(held, (ahead, g_wide, faces)))
    relaxed, xr, xl = call(end_step_kernel, (big, loaded, loaded), count=4)(*state, held(own))
    xr, xl = shift(xr, "gx", 1), shift(xl, "gx", -1)
    if small:
        own = (own + shift(own, "gx", 2)) + (xr[10] + xl[10])

    parts = lax.all_to_all(term, slab, 0, 0, tiled=True)
    snap, gram = call(
        functools.partial(gram_kernel, float(rows_local * devices)),
        (vmem(16, rows_local), f32(4 * devices, 128)),
        (pltpu.VMEM((128, rows_local), jnp.float32),),
        count=2,
    )(held(parts), held(old))
    grams = lax.all_to_all(gram, everyone, 0, 0, tiled=True)
    factor, head = call(old_factor_kernel, (vmem(32, 128), vmem(32, rows_local)), count=2)(
        held(own), held(old)
    )
    new_basis, upper = call(
        factor_kernel, (f32(44, rows_local), f32(44, 44)), (pltpu.VMEM((16, 128), jnp.float32),), count=4
    )(*map(held, (grams, factor, head, snap)))
    populations = call(last_kernel, f32(19, 2, 16, 128), count=3)(*map(held, (relaxed, xr, xl)))
    return (populations, new_basis, upper)


def solution(mesh):
    in_specs = (
        P(None, "gx", "gy", "gz"),
        P("gx", "gy", "gz"),
        P("gx", "gy", "gz"),
        P(),
        P("gx", "gy", "gz"),
        P(None, ("gx", "gy", "gz")),
        P(),
    )
    out_specs = (P(None, "gx", "gy", "gz"), P(None, ("gx", "gy", "gz")), P())

    return jax.shard_map(on_device, mesh=mesh, in_specs=in_specs, out_specs=out_specs, check_vma=False)
```

```python
import functools

import jax
import jax.numpy as jnp
import numpy as np
from jax import lax
from jax.experimental import pallas as pl
from jax.experimental.pallas import tpu as pltpu
from jax.sharding import PartitionSpec as P


VOX_ROW = 8
LATTICE = np.array(
    [
        [0, 0, 0],
        [1, 0, 0],
        [-1, 0, 0],
        [0, 1, 0],
        [0, -1, 0],
        [0, 0, 1],
        [0, 0, -1],
        [1, 1, 0],
        [-1, -1, 0],
        [1, -1, 0],
        [-1, 1, 0],
        [1, 0, 1],
        [-1, 0, -1],
        [1, 0, -1],
        [-1, 0, 1],
        [0, 1, 1],
        [0, -1, -1],
        [0, 1, -1],
        [0, -1, 1],
    ]
)
OPPOSITE = [0, 2, 1, 4, 3, 6, 5, 8, 7, 10, 9, 12, 11, 14, 13, 16, 15, 18, 17]
WEIGHTS = [1.0 / 3.0] + [1.0 / 18.0] * 6 + [1.0 / 36.0] * 12
PAIRS = [(q, OPPOSITE[q]) for q in range(1, 19) if q < OPPOSITE[q]]
PLUS_X = [q for q in range(19) if LATTICE[q, 0] == 1]
MINUS_X = [q for q in range(19) if LATTICE[q, 0] == -1]
relax_time = 0.9
vel_scale = 16.0

FIELDS = 20
LOW = 256


def lanes(shape=(8, 128)):
    return lax.broadcasted_iota(jnp.int32, shape, len(shape) - 1)


def subs(shape=(8, 128)):
    return lax.broadcasted_iota(jnp.int32, shape, len(shape) - 2)


def roll(value, shift, axis):
    size = value.shape[axis]
    shift = shift % size
    return value if shift == 0 else pltpu.roll(value, shift, axis)


def init_kernel(
    table_hbm, ratio_hbm, solid_hbm, cls_hbm,
    pops_ref, g_ref, zr_ref, zl_ref, y_ref, cr_ref, cl_ref,
    table, ratio, solid, cls, sems,
):
    pairs = ((ratio_hbm, ratio), (table_hbm, table), (solid_hbm, solid), (cls_hbm, cls))
    copies = [pltpu.make_async_copy(src, dst, sems.at[i]) for i, (src, dst) in enumerate(pairs)]
    for copy in copies:
        copy.start()
    for copy in copies:
        copy.wait()
    lane, sub = lanes(), subs()
    blank = jnp.zeros((8, 128), jnp.float32)
    zr, zl = [blank] * 3, [blank] * 3
    cr, cl = [blank] * 2, [blank] * 2
    for f in range(FIELDS):
        tiles = {}
        for x in range(2):
            for yt in range(2):
                rows = pl.ds(8 * yt, 8)
                if f < 19:
                    tile = ratio[f, x, rows, :] * WEIGHTS[f]
                    pops_ref[f, x, rows, :] = tile
                else:
                    ids = cls[x, rows, :]
                    drag = jnp.zeros((8, 128), jnp.float32)
                    for c in range(table.shape[0]):
                        drag = jnp.where(ids == c, table[c], drag)
                    tile = jnp.where(solid[x, rows, :] == 1, -1.0, 1.0 + 0.5 * drag)
                    g_ref[x, rows, :] = tile
                tiles[x, yt] = tile
                at, k = divmod(f * 4 + x * 2 + yt, 32)
                here = (lane >= 4 * k) & (lane < 4 * k + 4)
                zr[at] = jnp.where(here, roll(tile, 4 * k - 124, 1), zr[at])
                zl[at] = jnp.where(here, roll(tile, 4 * k, 1), zl[at])
        up = jnp.where(sub < 4, roll(tiles[0, 1], 4, 0), tiles[1, 1])
        down = jnp.where(sub < 4, tiles[0, 0], roll(tiles[1, 0], 4, 0))
        y_ref[f] = up
        y_ref[FIELDS + f] = down
        here = (lane >= 4 * f) & (lane < 4 * f + 4)
        for i, tile in enumerate((up, down)):
            cr[i] = jnp.where(here, roll(tile, 4 * f - 124, 1), cr[i])
            cl[i] = jnp.where(here, roll(tile, 4 * f, 1), cl[i])
    for at in range(3):
        zr_ref[at] = zr[at]
        zl_ref[at] = zl[at]
    for at in range(2):
        cr_ref[at] = cr[at]
        cl_ref[at] = cl[at]


def moments(pops, g):
    density = pops[0]
    for q in range(1, 19):
        density = density + pops[q]
    scale = 1.0 / (density * jnp.abs(g))
    speeds = []
    for a in range(3):
        total = None
        for q in range(19):
            c = LATTICE[q, a]
            if c == 1:
                total = pops[q] if total is None else total + pops[q]
            elif c == -1:
                total = total - pops[q]
        speeds.append(total * scale)
    return density, speeds


def collide(pops, g):
    density, speeds = moments(pops, g)
    square = speeds[0] * speeds[0] + speeds[1] * speeds[1] + speeds[2] * speeds[2]
    solid = g < 0.0
    keep = 1.0 - 1.0 / relax_time
    base = 1.0 - 1.5 * square
    part = {w: density * (w / relax_time) for w in sorted(set(WEIGHTS))}
    relaxed = [None] * 19
    rest = pops[0] * keep + part[WEIGHTS[0]] * base
    relaxed[0] = jnp.where(solid, pops[0], rest)
    for q, o in PAIRS:
        along = None
        for a in range(3):
            c = LATTICE[q, a]
            if c == 1:
                along = speeds[a] if along is None else along + speeds[a]
            elif c == -1:
                along = -speeds[a] if along is None else along - speeds[a]
        even = part[WEIGHTS[q]] * (base + 4.5 * along * along)
        odd = part[WEIGHTS[q]] * (3.0 * along)
        relaxed[q] = jnp.where(solid, pops[o], pops[q] * keep + (even + odd))
        relaxed[o] = jnp.where(solid, pops[q], pops[o] * keep + (even - odd))
    factor = jnp.where(solid, 0.0, vel_scale / VOX_ROW)
    return relaxed, [s * factor for s in speeds]


def collide_all(source, g_of, out, vel_ref, tiles=range(3)):
    for x in range(2):
        for yt in tiles:
            for lt in range(2):
                rows, cols = pl.ds(8 * yt, 8), pl.ds(128 * lt, 128)
                pops = [source(q, x, rows, cols) for q in range(19)]
                relaxed, vel = collide(pops, g_of[x, rows, cols])
                for q in range(19):
                    out[q, x, rows, cols] = relaxed[q]
                if vel_ref is not None and yt < 2 and lt == 0:
                    for a in range(3):
                        vel_ref[a, x, rows, :] = vel[a]


def pack_x(out, xr_ref, xl_ref):
    lane = lanes()
    for ref, directions, x in ((xr_ref, PLUS_X, 1), (xl_ref, MINUS_X, 0)):
        extra = jnp.zeros((8, 128), jnp.float32)
        for i, q in enumerate(directions):
            for yt in range(3):
                j = 3 * i + yt
                ref[j] = out[q, x, pl.ds(8 * yt, 8), pl.ds(0, 128)]
                tile = out[q, x, pl.ds(8 * yt, 8), pl.ds(128, 128)]
                here = (lane >= 8 * j) & (lane < 8 * j + 8)
                extra = jnp.where(here, roll(tile, 4 + 8 * j, 1), extra)
        ref[15] = extra


STILL = [q for q in range(19) if LATTICE[q, 0] == 0]
DEEP = 14
DEEP_TILES = 37


def still_sums(pops):
    total = pops[0]
    for value in pops[1:]:
        total = total + value
    sums = [total]
    for a in (1, 2):
        plus = [p for p, q in zip(pops, STILL) if LATTICE[q, a] == 1]
        minus = [p for p, q in zip(pops, STILL) if LATTICE[q, a] == -1]
        sums.append(((plus[0] + plus[1]) + plus[2]) - ((minus[0] + minus[1]) + minus[2]))
    return sums


def pack_deep(ahead, going, g_ref, refs):
    lane, sub = lanes(), subs()
    for side, ref in enumerate(refs):
        x = 1 - side
        edges = [jnp.zeros((8, 128), jnp.float32)] * 2
        directions = (PLUS_X, MINUS_X)[side]

        def entries(yt, lt):
            at = (pl.ds(8 * yt, 8), pl.ds(128 * lt, 128))
            tiles = [going[side, i, at[0], at[1]] for i in range(5)]
            tiles += [ahead[q, x, at[0], at[1]] for q in directions]
            tiles += still_sums([ahead[q, x, at[0], at[1]] for q in STILL])
            return tiles + [g_ref[x, at[0], at[1]]]

        def edge(j, tile):
            at, k = divmod(j, 32)
            here = (lane >= 4 * k) & (lane < 4 * k + 4)
            edges[at] = jnp.where(here, roll(tile, 2 + 4 * k, 1), edges[at])

        for yt in range(2):
            for e, (inner, outer) in enumerate(zip(entries(yt, 0), entries(yt, 1))):
                ref[2 * e + yt] = inner
                edge(2 * e + yt, outer)
        halos = [entries(2, lt) for lt in range(2)]
        for e in range(0, DEEP, 2):
            pair = [jnp.where(sub < 4, roll(h[e], 2, 0), roll(h[e + 1], 6, 0)) for h in halos]
            ref[28 + e // 2] = pair[0]
            edge(28 + e // 2, pair[1])
        for at in range(2):
            ref[35 + at] = edges[at]


def take_deep(refs, deep):
    for side, ref in enumerate(refs):

        def edge(j):
            return roll(ref[35 + j // 32], -(4 * (j % 32) + 2), 1)

        for e in range(DEEP):
            back = -2 if e % 2 == 0 else -6
            for yt in range(2):
                deep[side, e, pl.ds(8 * yt, 8), pl.ds(0, 128)] = ref[2 * e + yt]
                deep[side, e, pl.ds(8 * yt, 8), pl.ds(128, 128)] = edge(2 * e + yt)
            deep[side, e, pl.ds(16, 8), pl.ds(0, 128)] = roll(ref[28 + e // 2], back, 0)
            deep[side, e, pl.ds(16, 8), pl.ds(128, 128)] = roll(edge(28 + e // 2), back, 0)


def collide_side(toward, away, sums, g, side):
    ahead, back = ((PLUS_X, MINUS_X), (MINUS_X, PLUS_X))[side]
    into, out_of = toward[0], away[0]
    for value in toward[1:]:
        into = into + value
    for value in away[1:]:
        out_of = out_of + value
    density = sums[0] + (into + out_of)
    flows = [into - out_of if side == 0 else out_of - into, sums[1], sums[2]]
    for directions, pops in ((ahead, toward), (back, away)):
        for q, value in zip(directions, pops):
            for a in (1, 2):
                if LATTICE[q, a] == 1:
                    flows[a] = flows[a] + value
                elif LATTICE[q, a] == -1:
                    flows[a] = flows[a] - value
    scale = 1.0 / (density * jnp.abs(g))
    speeds = [flow * scale for flow in flows]
    square = speeds[0] * speeds[0] + speeds[1] * speeds[1] + speeds[2] * speeds[2]
    keep = 1.0 - 1.0 / relax_time
    base = 1.0 - 1.5 * square
    solid = g < 0.0
    part = {w: density * (w / relax_time) for w in sorted({WEIGHTS[q] for q in ahead})}
    relaxed = []
    for q, value in zip(ahead, toward):
        along = None
        for a in range(3):
            c = LATTICE[q, a]
            if c == 1:
                along = speeds[a] if along is None else along + speeds[a]
            elif c == -1:
                along = -speeds[a] if along is None else along - speeds[a]
        moved = value * keep + part[WEIGHTS[q]] * ((base + 4.5 * along * along) + 3.0 * along)
        relaxed.append(jnp.where(solid, away[back.index(OPPOSITE[q])], moved))
    return relaxed


def inner_kernel(pops, g_in, left, right, out, g_ref, vel_ref, wide):
    lane = lanes()
    for f in range(FIELDS):
        ref = wide.at[f] if f < 19 else g_ref
        for x in range(2):
            for yt in range(2):
                rows = pl.ds(8 * yt, 8)
                own = pops[f, x, rows, :] if f < 19 else g_in[x, rows, :]
                at, k = divmod(f * 4 + x * 2 + yt, 32)
                tile = jnp.where(lane < 4, roll(right[at], -4 * k, 1), own)
                tile = jnp.where(lane >= 124, roll(left[at], 124 - 4 * k, 1), tile)
                ref[x, rows, pl.ds(0, 128)] = own
                ref[x, rows, pl.ds(128, 128)] = tile
    collide_all(lambda q, x, rows, cols: wide[q, x, rows, cols], g_ref, out, vel_ref, range(2))


def outer_kernel(out_in, g_in, y, cr, cl, out, g_ref, xr_ref, xl_ref, wide):
    lane, sub = lanes(), subs()
    for f in range(FIELDS):
        ref = wide.at[f] if f < 19 else g_ref
        pairs = []
        for i in range(2):
            own = y[FIELDS * i + f]
            tile = jnp.where(lane < 4, roll(cl[i], -4 * f, 1), own)
            pairs.append((own, jnp.where(lane >= 124, roll(cr[i], 124 - 4 * f, 1), tile)))
        high, low = pairs
        for lt in range(2):
            cols = pl.ds(128 * lt, 128)
            ref[0, pl.ds(16, 8), cols] = jnp.where(sub < 4, low[lt], roll(high[lt], 4, 0))
            ref[1, pl.ds(16, 8), cols] = jnp.where(sub < 4, roll(low[lt], 4, 0), high[lt])
    collide_all(lambda q, x, rows, cols: wide[q, x, rows, cols], g_ref, out, None, (2,))
    pack_x(out, xr_ref, xl_ref)


def unpack_x(xr, xl, side):
    for s, ref in enumerate((xr, xl)):
        for i in range(5):
            for yt in range(3):
                j = 3 * i + yt
                side[s, i, pl.ds(8 * yt, 8), pl.ds(0, 128)] = ref[j]
                side[s, i, pl.ds(8 * yt, 8), pl.ds(128, 128)] = roll(ref[15], -(8 * j + 4), 1)


def turned(value, q):
    return roll(roll(value, int(LATTICE[q, 1]), 0), int(LATTICE[q, 2]), 1)


def remote(q, x):
    if LATTICE[q, 0] == 1 and x == 0:
        return 0, PLUS_X.index(q)
    if LATTICE[q, 0] == -1 and x == 1:
        return 1, MINUS_X.index(q)
    return None


def local_kernel(prev, ahead):
    for q in range(19):
        for x in range(2):
            if remote(q, x) is None:
                ahead[q, x] = turned(prev[q, x - int(LATTICE[q, 0])], q)


def take_faces(xr, xl, side):
    unpack_x(xr, xl, side)
    for s, directions in enumerate((PLUS_X, MINUS_X)):
        for i, q in enumerate(directions):
            side[s, i] = turned(side[s, i], q)


def chooser(ahead, side):
    def pick(q, x, rows, cols):
        at = remote(q, x)
        return ahead[q, x, rows, cols] if at is None else side[at[0], at[1], rows, cols]

    return pick


def step_kernel(ahead_in, g_ref, xr, xl, ahead, going, vel_ref, xr_ref, xl_ref, side, out):
    take_faces(xr, xl, side)
    collide_all(chooser(ahead_in, side), g_ref, out, vel_ref)
    local_kernel(out, ahead)
    for i in range(5):
        going[0, i] = turned(out[PLUS_X[i], 1], PLUS_X[i])
        going[1, i] = turned(out[MINUS_X[i], 0], MINUS_X[i])
    pack_deep(ahead, going, g_ref, (xr_ref, xl_ref))


def pair(ahead, going, g_ref, xr, xl, ahead_ref, side_ref, vel_ref, deep, out):
    take_deep((xr, xl), deep)

    def pick(q, x, rows, cols):
        at = remote(q, x)
        return ahead[q, x, rows, cols] if at is None else deep[at[0], at[1], rows, cols]

    collide_all(pick, g_ref, out, vel_ref)
    for side, directions in enumerate((PLUS_X, MINUS_X)):
        for yt in range(3):
            for lt in range(2):
                rows, cols = pl.ds(8 * yt, 8), pl.ds(128 * lt, 128)
                toward = [deep[side, 5 + i, rows, cols] for i in range(5)]
                away = [going[1 - side, i, rows, cols] for i in range(5)]
                sums = [deep[side, 10 + i, rows, cols] for i in range(3)]
                relaxed = collide_side(toward, away, sums, deep[side, 13, rows, cols], side)
                for i in range(5):
                    side_ref[side, i, rows, cols] = relaxed[i]
        for i, q in enumerate(directions):
            side_ref[side, i] = turned(side_ref[side, i], q)
    local_kernel(out, ahead_ref)


def end_step_kernel(ahead, g_ref, side, rider, out, xr_ref, xl_ref):
    collide_all(chooser(ahead, side), g_ref, out, None)
    for ref, directions, x in ((xr_ref, PLUS_X, 1), (xl_ref, MINUS_X, 0)):
        for i, q in enumerate(directions):
            value = turned(out[q, x], q)
            for yt in range(2):
                ref[2 * i + yt] = value[8 * yt : 8 * yt + 8, :128]
        ref[10] = rider[...]


def last_kernel(prev, xr, xl, out):
    for q in range(19):
        for x in range(2):
            at = remote(q, x)
            if at is None:
                out[q, x] = turned(prev[q, x - int(LATTICE[q, 0])], q)[:16, :128]
            else:
                for yt in range(2):
                    out[q, x, pl.ds(8 * yt, 8), :] = (xr, xl)[at[0]][2 * at[1] + yt]


def split(value):
    big = value.astype(jnp.bfloat16).astype(jnp.float32)
    return big, value - big


def onehot_kernel(row_map, right):
    low_at = lax.broadcasted_iota(jnp.int32, (LOW, 128), 0)
    for x in range(2):
        for y in range(16):
            rows = row_map[x, pl.ds(y, 1), :]
            low = rows - (rows // LOW) * LOW
            cols = pl.ds(128 * (16 * x + y), 128)
            right[:, cols] = jnp.where(low_at == low, 1.0, 0.0).astype(jnp.bfloat16)


def times_onehot(left, right):
    return lax.dot_general(
        left[...], right[...], (((1,), (1,)), ((), ())), preferred_element_type=jnp.float32
    )


def restricted(vels, row_map, right, left):
    count = 3 * len(vels)
    highs = left.shape[0] // (2 * count)
    high_at = lax.broadcasted_iota(jnp.int32, (highs, 128), 0)
    for x in range(2):
        for y in range(16):
            cols = pl.ds(128 * (16 * x + y), 128)
            here = high_at == row_map[x, pl.ds(y, 1), :] // LOW
            for j in range(count):
                for i, part in enumerate(split(vels[j // 3][j % 3, x, pl.ds(y, 1), :])):
                    left[pl.ds(highs * (count * i + j), highs), cols] = jnp.where(here, part, 0.0).astype(jnp.bfloat16)
    both = times_onehot(left, right)
    half = count * highs
    return both[:half] + both[half:]


def early_kernel(v0, v1, row_map, right, out, left):
    highs = out.shape[0] // 12
    both = restricted((v0, v1), row_map, right, left)
    for h in range(highs):
        for j in range(6):
            out[pl.ds(12 * h + j, 1), :] = both[highs * j + h : highs * j + h + 1]
            out[pl.ds(12 * h + 6 + j, 1), :] = jnp.zeros((1, LOW), jnp.float32)


def pair_late_kernel(
    ahead, going, g_ref, xr, xl, row_map, right, early, ahead_ref, side_ref, out, deep, relaxed, v2, v3, left
):
    pair(ahead, going, g_ref, xr, xl, ahead_ref, side_ref, v2, deep, relaxed)
    late(ahead_ref, g_ref, side_ref, v2, row_map, right, early, out, left, v3)


def old_kernel(total_rows, basis, sigma, scaled_ref, tile_ref, work):
    scaled = basis[...] * sigma[...]
    scaled_ref[...] = scaled
    work[...] = jnp.zeros((32, 128), jnp.float32)
    work[:, pl.ds(0, 32)] = dot(scaled, scaled, 1) * (1.0 / total_rows)
    lane = lanes()
    tile = work[pl.ds(0, 8), :]
    for k in range(1, 4):
        here = (lane >= 32 * k) & (lane < 32 * k + 32)
        tile = jnp.where(here, roll(work[pl.ds(8 * k, 8), :], 32 * k, 1), tile)
    tile_ref[...] = tile


def dot(a, b, dim):
    return lax.dot_general(
        a,
        b,
        (((1,), (dim,)), ((), ())),
        precision=lax.Precision.HIGHEST,
        preferred_element_type=jnp.float32,
    )


def late(ahead, g_ref, side, v2, row_map, right, early, out, left, v3):
    pick = chooser(ahead, side)
    for x in range(2):
        for yt in range(2):
            rows, cols = pl.ds(8 * yt, 8), pl.ds(0, 128)
            g = g_ref[x, rows, cols]
            _, speeds = moments([pick(q, x, rows, cols) for q in range(19)], g)
            factor = jnp.where(g < 0.0, 0.0, vel_scale / VOX_ROW)
            for a in range(3):
                v3[a, x, rows, :] = speeds[a] * factor
    highs = out.shape[0] // 12
    both = restricted((v2, v3), row_map, right, left)
    out[...] = early[...]
    for h in range(highs):
        for j in range(6):
            out[pl.ds(12 * h + 6 + j, 1), :] = both[highs * j + h : highs * j + h + 1]


def gram_kernel(total_rows, parts, scaled, snap_ref, out, aug):
    owners = parts.shape[0] // 24
    total = parts[pl.ds(0, 24), :]
    for o in range(1, owners):
        total = total + parts[pl.ds(24 * o, 24), :]
    aug[pl.ds(0, 32), :] = scaled[...]
    aug[pl.ds(40, 88), :] = jnp.zeros((88, 2 * LOW), jnp.float32)
    aug[pl.ds(32, 12), pl.ds(0, LOW)] = total[:12]
    aug[pl.ds(32, 12), pl.ds(LOW, LOW)] = total[12:]
    snap = aug[pl.ds(32, 16), :]
    snap_ref[...] = snap
    product = dot(snap, aug[...], 1) * (1.0 / total_rows)
    lane = lanes()
    tail = jnp.where(lane < 120, roll(product[8:], 88, 1), roll(product[8:], 80, 1))
    packed = jnp.where(lane < 44, product[:8], jnp.where(lane < 88, roll(roll(product[:8], 4, 0), 44, 1), tail))
    twice = jnp.where(subs() < 4, packed, roll(packed, 4, 0))
    for d in range(out.shape[0] // 8):
        out[pl.ds(8 * d, 8), :] = twice


def eliminate(tiles, count):
    sub = subs()
    done = list(tiles)

    def spread(value, row):
        return jnp.broadcast_to(value[row : row + 1, :], (8, 128))

    for k in range(0, count, 2):
        t, r = divmod(k, 8)
        row0, row1 = spread(tiles[t], r), spread(tiles[t], r + 1)
        cols = {
            u: [jnp.broadcast_to(tiles[u][:, k + i : k + i + 1], (8, 128)) for i in range(2)]
            for u in range(t, len(tiles))
        }
        a, b, c = spread(cols[t][0], r), spread(cols[t][1], r), spread(cols[t][1], r + 1)
        inv = 1.0 / (a * c - b * b)
        part0 = (c * row0 - b * row1) * inv
        part1 = (a * row1 - b * row0) * inv
        ratio = b / a
        first = row0 * (1.0 / jnp.sqrt(a))
        second = (row1 - ratio * row0) * (1.0 / jnp.sqrt(c - ratio * b))
        done[t] = jnp.where(sub == r, first, jnp.where(sub == r + 1, second, done[t]))
        for u in range(t, len(tiles)):
            tiles[u] = tiles[u] - (cols[u][0] * part0 + cols[u][1] * part1)
    return [jnp.where((lanes() >= 64) | (lanes() >= sub + 8 * t), tile, 0.0) for t, tile in enumerate(done)]


def old_factor_kernel(tile, scaled, work, head_ref):
    lane, sub = lanes(), subs()
    tiles = []
    for k in range(4):
        own = jnp.where(lane < 32, roll(tile[...], -32 * k, 1), 0.0)
        tiles.append(own + jnp.where(lane == sub + 8 * k + 64, 1.0, 0.0))
    for k, value in enumerate(eliminate(tiles, 32)):
        work[pl.ds(8 * k, 8), :] = value
    head_ref[...] = dot(work[:, pl.ds(64, 32)], scaled[...], 0)


def factor_kernel(parts, factor, head, snap, basis_ref, tri_ref, work):
    lane, sub = lanes(), subs()
    sums = [parts[pl.ds(8 * d, 8), :] for d in range(parts.shape[0] // 8)]
    while len(sums) > 1:
        sums = [sums[i] + sums[i + 1] for i in range(0, len(sums), 2)]
    total = sums[0] + roll(sums[0], 4, 0)
    top = jnp.where(lane < 44, jnp.where(sub < 4, total, roll(total, -44, 1)), 0.0)
    low = jnp.where(lane < 32, roll(total, -88, 1), roll(total, -80, 1))
    work[pl.ds(0, 8), :] = top
    work[pl.ds(8, 8), :] = jnp.where((sub < 4) & (lane < 44), low, 0.0)
    work[pl.ds(8, 8), pl.ds(32, 8)] = top.T[40:48]
    cross = work[:, pl.ds(0, 32)]
    inner = work[:, pl.ds(32, 16)]
    inverse = factor[:, pl.ds(64, 32)]
    below = dot(cross, inverse, 1)
    rest = snap[...] - dot(below, head[...], 0)
    inner = inner - dot(below, below, 1)
    work[...] = jnp.zeros((16, 128), jnp.float32)
    work[:, pl.ds(0, 16)] = inner
    tiles = [work[pl.ds(8 * t, 8), :] + jnp.where(lane == sub + 8 * t + 64, 1.0, 0.0) for t in range(2)]
    for t, value in enumerate(eliminate(tiles, 12)):
        work[pl.ds(8 * t, 8), :] = value
    tri_ref[pl.ds(0, 32), pl.ds(0, 32)] = factor[:, pl.ds(0, 32)]
    tri_ref[pl.ds(0, 32), pl.ds(32, 12)] = dot(inverse, cross, 1)[:, :12]
    tri_ref[pl.ds(32, 12), pl.ds(0, 32)] = jnp.zeros((12, 32), jnp.float32)
    tri_ref[pl.ds(32, 12), pl.ds(32, 12)] = work[pl.ds(0, 12), pl.ds(0, 12)]
    basis_ref[pl.ds(0, 32), :] = head[...]
    basis_ref[pl.ds(32, 12), :] = dot(work[:, pl.ds(64, 16)], rest, 0)[:12]


def f32(*shape):
    return jax.ShapeDtypeStruct(shape, jnp.float32)


def vmem(*shape):
    return pltpu.VMEM(shape, jnp.float32)


def held(value):
    return pltpu.with_memory_space_constraint(value, pltpu.VMEM)


def call(kernel, outs, scratch=(), count=None, aliases=None, limit=16, space=pltpu.VMEM):
    specs = [pl.BlockSpec(memory_space=space) for _ in range(count)]
    many = isinstance(outs, (tuple, list))
    out_specs = [pl.BlockSpec(memory_space=pltpu.VMEM)] * len(outs) if many else pl.BlockSpec(memory_space=pltpu.VMEM)
    return pl.pallas_call(
        kernel, out_shape=outs, in_specs=specs, out_specs=out_specs, scratch_shapes=list(scratch),
        input_output_aliases=aliases or {},
        compiler_params=pltpu.CompilerParams(vmem_limit_bytes=limit * 2**20),
    )


def shift(value, axis, step):
    count = lax.axis_size(axis)
    return lax.ppermute(value, axis, [(i, (i + step) % count) for i in range(count)])


def shift_both(value, step_y, step_z):
    ny, nz = lax.axis_size("gy"), lax.axis_size("gz")
    pairs = [
        (y * nz + z, (y + step_y) % ny * nz + (z + step_z) % nz) for y in range(ny) for z in range(nz)
    ]
    return lax.ppermute(value, ("gy", "gz"), pairs)


def across(value, step_z):
    if lax.axis_size("gy") == 2:
        return shift_both(value, 1, step_z)
    half = value.shape[0] // 2
    return jnp.concatenate([shift_both(value[:half], 1, step_z), shift_both(value[half:], -1, step_z)], 0)


def on_device(pop_ratio, solid_flags, class_ids, drag_table, row_map, old_basis, old_sigma):
    slab = ("gy", "gz")
    everyone = ("gx", "gy", "gz")
    owners = lax.axis_size(slab)
    devices = lax.axis_size(everyone)
    rows_local = old_basis.shape[1]
    highs = owners * rows_local // LOW
    cells = 4096
    tile = (8, 128)

    pops, g, zr, zl, y, cr, cl = call(
        init_kernel,
        (vmem(19, 2, 16, 128), vmem(2, 16, 128), vmem(3, *tile), vmem(3, *tile))
        + (vmem(2 * FIELDS, *tile), vmem(2, *tile), vmem(2, *tile)),
        (
            pltpu.SMEM(drag_table.shape, jnp.float32),
            pltpu.VMEM((19, 2, 16, 128), jnp.float32),
            pltpu.VMEM((2, 16, 128), jnp.int32),
            pltpu.VMEM((2, 16, 128), jnp.int32),
            pltpu.SemaphoreType.DMA((4,)),
        ),
        count=4,
        space=pltpu.HBM,
    )(*(pltpu.with_memory_space_constraint(v, pltpu.HBM) for v in (drag_table, pop_ratio, solid_flags, class_ids)))
    y = across(y, 0)
    left, right = shift(zr, "gz", 1), shift(zl, "gz", -1)
    cr, cl = across(cr, 1), across(cl, -1)

    wide = pltpu.VMEM((19, 2, 24, 256), jnp.float32)
    side = pltpu.VMEM((2, 5, 24, 256), jnp.float32)
    big, wall, vel, face = vmem(19, 2, 24, 256), vmem(2, 24, 256), vmem(3, 2, 16, 128), vmem(16, *tile)
    deep_face, loaded, sides = vmem(DEEP_TILES, *tile), vmem(11, *tile), vmem(2, 5, 24, 256)
    relaxed, g_wide, v0 = call(inner_kernel, (big, wall, vel), (wide,), count=4)(
        *map(held, (pops, g, left, right))
    )
    relaxed, g_wide, xr, xl = call(
        outer_kernel, (big, wall, face, face), (wide,), count=5, aliases={0: 0, 1: 1}
    )(*map(held, (relaxed, g_wide, y, cr, cl)))
    old, own = call(
        functools.partial(old_kernel, float(rows_local * devices)),
        (vmem(32, rows_local), vmem(*tile)),
        (pltpu.VMEM((32, 128), jnp.float32),),
        count=2,
    )(old_basis, old_sigma[:, None])
    small = tuple(lax.axis_size(a) for a in everyone) == (4, 2, 4)
    if not small:
        own = lax.psum(own, everyone)
    onehot = call(onehot_kernel, pltpu.VMEM((LOW, cells), jnp.bfloat16), count=1)(row_map)
    xr, xl = shift(xr, "gx", 1), shift(xl, "gx", -1)
    ahead = call(local_kernel, big, count=1)(held(relaxed))
    if small:
        own = own + shift(own, "gy", 1)
    ahead, going, v1, xr, xl = call(
        step_kernel, (big, sides, vel, deep_face, deep_face), (side, wide), count=4
    )(*map(held, (ahead, g_wide, xr, xl)))
    xr, xl = shift(xr, "gx", 1), shift(xl, "gx", -1)
    if small:
        own = (own + shift(own, "gz", 2)) + (shift(own, "gz", 1) + shift(own, "gz", -1))
    lefts = pltpu.VMEM((12 * highs, cells), jnp.bfloat16)
    early = call(early_kernel, vmem(12 * highs, LOW), (lefts,), count=4, limit=12 + highs // 2)(
        held(v0), held(v1), row_map, held(onehot)
    )
    small_vel = pltpu.VMEM((3, 2, 16, 128), jnp.float32)
    ahead, faces, term = call(
        pair_late_kernel,
        (big, sides, f32(12 * highs, LOW)),
        (pltpu.VMEM((2, DEEP, 24, 256), jnp.float32), wide, small_vel, small_vel, lefts),
        count=8,
        limit=16 + highs // 2,
    )(*map(held, (ahead, going, g_wide, xr, xl)), row_map, held(onehot), held(early))
    state = tuple(map(held, (ahead, g_wide, faces)))
    relaxed, xr, xl = call(end_step_kernel, (big, loaded, loaded), count=4)(*state, held(own))
    xr, xl = shift(xr, "gx", 1), shift(xl, "gx", -1)
    if small:
        own = (own + shift(own, "gx", 2)) + (xr[10] + xl[10])

    parts = lax.all_to_all(term, slab, 0, 0, tiled=True)
    snap, gram = call(
        functools.partial(gram_kernel, float(rows_local * devices)),
        (vmem(16, rows_local), f32(4 * devices, 128)),
        (pltpu.VMEM((128, rows_local), jnp.float32),),
        count=2,
    )(held(parts), held(old))
    grams = lax.all_to_all(gram, everyone, 0, 0, tiled=True)
    factor, head = call(old_factor_kernel, (vmem(32, 128), vmem(32, rows_local)), count=2)(
        held(own), held(old)
    )
    new_basis, upper = call(
        factor_kernel, (f32(44, rows_local), f32(44, 44)), (pltpu.VMEM((16, 128), jnp.float32),), count=4
    )(*map(held, (grams, factor, head, snap)))
    populations = call(last_kernel, f32(19, 2, 16, 128), count=3)(*map(held, (relaxed, xr, xl)))
    return (populations, new_basis, upper)


def solution(mesh):
    in_specs = (
        P(None, "gx", "gy", "gz"),
        P("gx", "gy", "gz"),
        P("gx", "gy", "gz"),
        P(),
        P("gx", "gy", "gz"),
        P(None, ("gx", "gy", "gz")),
        P(),
    )
    out_specs = (P(None, "gx", "gy", "gz"), P(None, ("gx", "gy", "gz")), P())

    return jax.shard_map(on_device, mesh=mesh, in_specs=in_specs, out_specs=out_specs, check_vma=False)
```
